256 devices in a mesh: gx: 32 (over z, y), gy: 8 (over x, core).
Axes of the slice: x: 4, y: 4, z: 8, core: 2. Of those that a mesh axis runs over, the one named last changes fastest.
Arguments:
- e_adj: float32 [3, 8, 2048, 2048], P(None, None, 'gx', 'gy'), may hold values from -6 to 6
- h_adj: float32 [3, 8, 2048, 2048], P(None, None, 'gx', 'gy'), may hold values from -6 to 6
- density: float32 [2048, 2048], P('gx', 'gy'), may hold values from 0.05 to 0.95
- material: int32 [8, 2048, 2048], P(None, 'gx', 'gy'), may hold values from 0 to 3
- eps_table: float32 [4], replicated, may hold values from 1 to 12
- dft_adj: float32 [4, 2, 3, 2, 2048, 2048], P(None, None, None, None, 'gx', 'gy'), may hold values from -6 to 6
- dft_fwd: bfloat16 [4, 2, 3, 2, 2048, 2048], P(None, None, None, None, 'gx', 'gy'), may hold values from -6 to 6
- tile_map: int32 [32, 32], P('gx', 'gy'), may hold values from 0 to 255, as said below
Outputs:
- e_out: float32 [3, 8, 2048, 2048], P(None, None, 'gx', 'gy')
- h_out: float32 [3, 8, 2048, 2048], P(None, None, 'gx', 'gy')
- param_grad: float32 [256, 4096], P(('gx', 'gy'))
The draws below stay inside these ranges and needn't reach their ends.
Inputs may be any that keep to these rules, and one draw needn't show every extreme that they name: `tile_map`: each of the 256 design parameters is named by exactly 4 tiles. Parameter p belongs to the device at position p // (256 / number of devices) in the gx-major order of devices.
All inputs are finite; a program needn't handle non-finite values.
Results may differ from the reference program's by a relative error of at most 0.0003.
Values sent between devices are 32-bit elements; how exact they have to be, the bound alone decides.
A program may use at most 64 MiB of HBM per device.

```python
import math
import jax
import jax.numpy as jnp
from jax import lax

CX = 64
CY = 256
NZ = 8
PLANES = 2
ZLO = 3
STEPS = 2
FREQ = 4
PML = 12
MATS = 4
TILE = 64
REPEAT = 4
NX = 2048
NY = 2048
PARAMS = 256


def draw_tile_map(key, part):
    count_gx = NX // CX
    count_gy = NY // CY
    tiles_x = CX // TILE
    tiles_y = CY // TILE
    per_device = tiles_x * tiles_y
    rows_each = per_device // REPEAT
    devices_all = count_gx * count_gy
    key_mag = jax.random.fold_in(key, 11)
    key_sign = jax.random.fold_in(key, 12)
    key_perm = jax.random.fold_in(key, 13)
    magnitude = jax.random.randint(key_mag, (), 2, devices_all // 2)
    signs = 2 * jax.random.randint(key_sign, (), 0, 2) - 1
    extra = (magnitude * signs).astype(jnp.int32)
    offsets = jnp.stack([jnp.zeros((), jnp.int32), jnp.ones((), jnp.int32), jnp.full((), devices_all // 2, jnp.int32), extra]).astype(jnp.int32)
    device_ids = jnp.arange(devices_all, dtype=jnp.int32)[:, None]
    slots = jnp.arange(per_device, dtype=jnp.int32)[None, :]
    chosen = jnp.take(offsets, slots % REPEAT)
    owner = (device_ids - chosen + 2 * devices_all) % devices_all
    params = (owner * rows_each + slots // REPEAT).astype(jnp.int32)
    perm_keys = jax.random.split(key_perm, devices_all)
    orders = jax.vmap(lambda one_key: jax.random.permutation(one_key, per_device))(perm_keys)
    mixed = jnp.take_along_axis(params, orders.astype(jnp.int32), axis=1)
    layout = mixed.reshape(count_gx, count_gy, tiles_x, tiles_y).transpose(0, 2, 1, 3)
    return layout.reshape(count_gx * tiles_x, count_gy * tiles_y).astype(jnp.int32)


def with_ends(array, own_key, low, high):
    longest = array.shape.index(max(array.shape))
    spots = []
    for shift in (0, 1):
        where = [jax.random.randint(jax.random.fold_in(own_key, axis), (), 0, length) for axis, length in enumerate(array.shape)]
        where[longest] = (where[longest] + shift) % array.shape[longest]
        spots.append(tuple(where))
    return array.at[spots[0]].set(low).at[spots[1]].set(high)


def shard_levels(stream_key, dims, pieces, least, largest):
    factor_of = 1.0
    for position, parts in pieces:
        draws = jax.random.uniform(jax.random.fold_in(jax.random.fold_in(stream_key, 6), position), (parts,), jnp.float32, least / len(pieces), largest / len(pieces))
        factor_of = factor_of * jnp.repeat(jnp.exp(draws), dims[position] // parts).reshape((-1,) + (1,) * (len(dims) - 1 - position))
    return factor_of


def noise(stream_key, extent, deviation, bound, pieces=(), kind=jnp.bfloat16):
    gain = shard_levels(stream_key, extent, pieces, -0.22, 0.18) if pieces else 1.0
    values = jax.random.normal(stream_key, extent, jnp.float32) * deviation * gain
    return jnp.minimum(jnp.maximum(values, -bound), bound).astype(kind)


def setup_inputs(seed: int = 0) -> dict:
    arg_keys = jax.random.split(jax.random.key(seed), 9)
    e_adj = noise(arg_keys[0], (3, NZ, NX, NY), 1.0, 6.0, ((2, 32), (3, 8)), jnp.float32)
    h_adj = noise(arg_keys[1], (3, NZ, NX, NY), 1.0, 6.0, ((2, 32), (3, 8)), jnp.float32)
    density = jnp.clip(0.05 + 0.9 * jax.random.uniform(arg_keys[2], (NX, NY), jnp.float32) ** shard_levels(arg_keys[2], (NX, NY), ((0, 32), (1, 8)), -0.2, 0.2), 0.05, 0.95)
    material = with_ends(jax.random.randint(arg_keys[3], (NZ, NX, NY), 0, MATS), jax.random.fold_in(arg_keys[3], 1), 0, MATS - 1).astype(jnp.int32)
    eps_table = jnp.clip(jnp.exp(jax.random.uniform(arg_keys[4], (MATS,), jnp.float32, math.log(1.0), math.log(12.0))), 1.0, 12.0)
    dft_adj = noise(arg_keys[5], (FREQ, 2, 3, PLANES, NX, NY), 1.0, 6.0, ((4, 32), (5, 8)), jnp.float32)
    dft_fwd = noise(arg_keys[6], (FREQ, 2, 3, PLANES, NX, NY), 1.0, 6.0, ((4, 32), (5, 8)))
    tile_map = draw_tile_map(jax.random.fold_in(arg_keys[8], 71), 0)
    return dict(e_adj=e_adj, h_adj=h_adj, density=density, material=material, eps_table=eps_table, dft_adj=dft_adj, dft_fwd=dft_fwd, tile_map=tile_map)


courant = 0.5
sigma_peak = 0.8
dft_weight = 0.5
sharpness = 4.0
threshold = 0.5
eps_low = 2.1
eps_high = 12.1
grad_scale = 0.01


def profile(places, total):
    depth = jnp.maximum(jnp.maximum(PML - places, places - (total - 1 - PML)), 0.0) / PML
    return depth * depth * depth


def smooth(grid_field):
    padded = jnp.pad(grid_field, 1)
    summed = padded[:-2] + 2.0 * padded[1:-1] + padded[2:]
    return (summed[:, :-2] + 2.0 * summed[:, 1:-1] + summed[:, 2:]) / 16.0


def step_next(values, border, dim_index):
    inner = lax.slice_in_dim(values, 1, values.shape[dim_index], axis=dim_index)
    return jnp.concatenate([inner, border], axis=dim_index) - values


def step_prev(values, border, dim_index):
    inner = lax.slice_in_dim(values, 0, values.shape[dim_index] - 1, axis=dim_index)
    return values - jnp.concatenate([border, inner], axis=dim_index)


def zero_rim(values, dim_index):
    return jnp.zeros_like(lax.slice_in_dim(values, 0, 1, axis=dim_index))


def curl_forward(elec_x, elec_y, elec_z, ahead_x, ahead_y):
    curl_x = step_next(elec_z, ahead_y[1], 2) - step_next(elec_y, zero_rim(elec_y, 0), 0)
    curl_y = step_next(elec_x, zero_rim(elec_x, 0), 0) - step_next(elec_z, ahead_x[1], 1)
    curl_z = step_next(elec_y, ahead_x[0], 1) - step_next(elec_x, ahead_y[0], 2)
    return curl_x, curl_y, curl_z


def curl_backward(mag_x, mag_y, mag_z, behind_x, behind_y):
    curl_x = step_prev(mag_z, behind_y[1], 2) - step_prev(mag_y, zero_rim(mag_y, 0), 0)
    curl_y = step_prev(mag_x, zero_rim(mag_x, 0), 0) - step_prev(mag_z, behind_x[1], 1)
    curl_z = step_prev(mag_y, behind_x[0], 1) - step_prev(mag_x, behind_y[0], 2)
    return curl_x, curl_y, curl_z


def accumulate(accum, elec_x, elec_y, elec_z, step_index):
    design = jnp.stack([elec_x, elec_y, elec_z])[:, ZLO:ZLO + PLANES]
    angular = 0.21 + 0.06 * jnp.arange(FREQ, dtype=jnp.float32)
    turned = angular * (step_index + 1)
    weights = jnp.stack([dft_weight * jnp.cos(turned), -dft_weight * jnp.sin(turned)], axis=1)
    return accum + weights[:, :, None, None, None, None] * design[None, None]


def reference(e_adj, h_adj, density, material, eps_table, dft_adj, dft_fwd, tile_map):
    sigma = sigma_peak * (profile(jnp.arange(NX, dtype=jnp.float32), NX)[:, None]
                          + profile(jnp.arange(NY, dtype=jnp.float32), NY)[None, :])
    half_sum = 1.0 + 0.5 * sigma
    damping = (1.0 - 0.5 * sigma) / half_sum
    coef_h = courant / half_sum
    filtered = smooth(density)
    bend_value = jnp.tanh(sharpness * (filtered - threshold))
    scale_sum = jnp.tanh(sharpness * threshold) + jnp.tanh(sharpness * (1.0 - threshold))
    projected = (jnp.tanh(sharpness * threshold) + bend_value) / scale_sum
    slope = sharpness * (1.0 - bend_value * bend_value) / scale_sum
    design_eps = eps_low + (eps_high - eps_low) * projected
    eps_grid = jnp.zeros(material.shape, jnp.float32)
    for material_id in range(MATS):
        eps_grid = jnp.where(material == material_id, eps_table[material_id], eps_grid)
    layer_ids = jnp.arange(NZ, dtype=jnp.int32)[:, None, None]
    inside = (layer_ids >= ZLO) & (layer_ids < ZLO + PLANES)
    eps_grid = jnp.where(inside, design_eps[None], eps_grid)
    coef_e = courant / (eps_grid * half_sum[None])
    elec_x, elec_y, elec_z = e_adj[0], e_adj[1], e_adj[2]
    mag_x, mag_y, mag_z = h_adj[0], h_adj[1], h_adj[2]
    border_x = jnp.zeros((2, NZ, 1, NY), jnp.float32)
    border_y = jnp.zeros((2, NZ, NX, 1), jnp.float32)
    accum = dft_adj
    for step_index in range(STEPS):
        curl_x, curl_y, curl_z = curl_forward(elec_x, elec_y, elec_z, border_x, border_y)
        mag_x = damping * mag_x - coef_h * curl_x
        mag_y = damping * mag_y - coef_h * curl_y
        mag_z = damping * mag_z - coef_h * curl_z
        curl_x, curl_y, curl_z = curl_backward(mag_x, mag_y, mag_z, border_x, border_y)
        elec_x = damping * elec_x + coef_e * curl_x
        elec_y = damping * elec_y + coef_e * curl_y
        elec_z = damping * elec_z + coef_e * curl_z
        accum = accumulate(accum, elec_x, elec_y, elec_z, step_index)
    forward = dft_fwd.astype(jnp.float32)
    intersection = jnp.sum(forward[:, 0] * accum[:, 0] - forward[:, 1] * accum[:, 1], axis=(0, 1, 2))
    local_grad = grad_scale * (eps_high - eps_low) * slope * intersection
    grad_cells = smooth(local_grad)
    tile_rows = grad_cells.reshape(NX // TILE, TILE, NY // TILE, TILE).transpose(0, 2, 1, 3).reshape(-1, TILE * TILE)
    param_grad = jax.ops.segment_sum(tile_rows, tile_map.reshape(-1), num_segments=PARAMS)
    return (jnp.stack([elec_x, elec_y, elec_z]), jnp.stack([mag_x, mag_y, mag_z]), param_grad)
```

```python
import functools
import math

import jax
import jax.numpy as jnp
from jax import lax
from jax.experimental import pallas as pl
from jax.experimental.pallas import tpu as pltpu
from jax.sharding import PartitionSpec as P

MESH = pl.DeviceIdType.MESH

PLANES = 2
ZLO = 3
STEPS = 2
FREQ = 4
PML = 12
MATS = 4
TILE = 64

courant = 0.5
sigma_peak = 0.8
dft_weight = 0.5
sharpness = 4.0
threshold = 0.5
eps_low = 2.1
eps_high = 12.1
grad_scale = 0.01

F32 = jnp.float32
BF16 = jnp.bfloat16
VMEM = pl.BlockSpec(memory_space=pltpu.VMEM)
ANY = pl.BlockSpec(memory_space=pl.ANY)

CX, CY, NZ = 64, 256, 8
EX = CX + 8
KINDS = 8
EDGE = 2
ZL = KINDS * EDGE


def iota(shape, dim):
    return lax.broadcasted_iota(jnp.int32, shape, dim)


def wrapped(index, shift, count):
    return lax.rem(index + (shift + count), count)


def around(gx, gy, nx, ny):
    places = {}
    for dx in (-1, 0, 1):
        for dy in (-1, 0, 1):
            if dx or dy:
                places[dx, dy] = (wrapped(gx, dx, nx), wrapped(gy, dy, ny))
    return places


def remote(src, dst, send, recv, device):
    return pltpu.make_async_remote_copy(
        src_ref=src, dst_ref=dst, send_sem=send, recv_sem=recv, device_id=device, device_id_type=MESH
    )


def exchange_kernel(
    nx, ny,
    e_hbm, h_hbm, mat_hbm, den_hbm, fwd_hbm, adj_hbm,
    own, got, rim_prev, rim_next, xprev, xnext, total, gain,
    e, h, mat, den, fwd, adj, xdown, xup, load_sem, send_sem, recv_sem,
):
    gx, gy = lax.axis_index("gx"), lax.axis_index("gy")
    near = around(gx, gy, nx, ny)
    barrier = pltpu.get_barrier_semaphore()
    for device in near.values():
        pl.semaphore_signal(barrier, inc=1, device_id=device, device_id_type=MESH)

    loads = [
        pltpu.make_async_copy(src, dst, load_sem.at[i])
        for i, (src, dst) in enumerate(
            ((e_hbm, e), (h_hbm, h), (mat_hbm, mat), (den_hbm, den), (fwd_hbm, fwd), (adj_hbm, adj))
        )
    ]
    for load in loads:
        load.start()
    for load in loads[:4]:
        load.wait()

    lane = iota((CX, 128), 1)
    sub = iota((8, CY), 0)

    def plane(kind, z, rows, columns):
        if kind < 3:
            return e[kind, z, rows, columns]
        if kind < 6:
            return h[kind - 3, z, rows, columns]
        if kind == 6:
            return mat[z, rows, columns].astype(F32)
        return den[rows, columns]

    def pack(z, carry):
        first, last = carry
        every, low, high = pl.ds(0, CX), pl.ds(0, 128), pl.ds(128, 128)
        left = jnp.zeros((CX, 128), F32)
        right = jnp.zeros((CX, 128), F32)
        for kind in range(KINDS):
            mine = (lane >= EDGE * kind) & (lane < EDGE * (kind + 1))
            a = plane(kind, z, every, low)
            b = plane(kind, z, every, high)
            left = jnp.where(mine, pltpu.roll(a, EDGE * kind, 1) if kind else a, left)
            right = jnp.where(mine, pltpu.roll(b, EDGE * kind + EDGE, 1), right)
        first = first + pltpu.roll(left, z * ZL, 1)
        last = last + pltpu.roll(right, z * ZL, 1)
        for group in range(2):
            up = jnp.zeros((8, CY), F32)
            down = jnp.zeros((8, CY), F32)
            for q in range(4):
                kind = 4 * group + q
                mine = (sub >= 2 * q) & (sub < 2 * q + 2)
                a = plane(kind, z, pl.ds(0, 8), pl.ds(0, CY))
                b = plane(kind, z, pl.ds(CX - 8, 8), pl.ds(0, CY))
                up = jnp.where(mine, pltpu.roll(a, 2 * q, 0) if q else a, up)
                down = jnp.where(mine, pltpu.roll(b, 2 * q + 2, 0) if q < 3 else b, down)
            xup[2 * z + group] = up
            xdown[2 * z + group] = down
        return first, last

    empty = jnp.zeros((CX, 128), F32)
    first, last = lax.fori_loop(0, NZ, pack, (empty, empty))
    own[0] = first
    own[1] = last

    pl.semaphore_wait(barrier, 8)
    top, bottom = pl.ds(0, 8), pl.ds(CX - 8, 8)
    plan = (
        (own.at[1], got.at[0], (0, 1)),
        (own.at[0], got.at[1], (0, -1)),
        (xdown, xprev, (1, 0)),
        (xup, xnext, (-1, 0)),
        (own.at[:, bottom], rim_prev.at[pl.ds(1, 2)], (1, 0)),
        (own.at[:, top], rim_next.at[pl.ds(1, 2)], (-1, 0)),
        (own.at[1, bottom], rim_prev.at[0], (1, 1)),
        (own.at[0, bottom], rim_prev.at[3], (1, -1)),
        (own.at[1, top], rim_next.at[0], (-1, 1)),
        (own.at[0, top], rim_next.at[3], (-1, -1)),
    )
    copies = [
        remote(src, dst, send_sem.at[i], recv_sem.at[i], near[to]) for i, (src, dst, to) in enumerate(plan)
    ]
    for copy in copies:
        copy.start()

    for load in loads[4:]:
        load.wait()
    cosines = [[dft_weight * math.cos((0.21 + 0.06 * f) * (n + 1)) for f in range(FREQ)] for n in range(STEPS)]
    sines = [[dft_weight * math.sin((0.21 + 0.06 * f) * (n + 1)) for f in range(FREQ)] for n in range(STEPS)]

    def chunk(r, _):
        rows = pl.ds(pl.multiple_of(r * 16, 16), 16)

        def entry(k, acc):
            one = jnp.zeros((16, CY), F32)
            two = jnp.zeros((16, CY), F32)
            for f in range(FREQ):
                re = fwd[f, 0, k, rows].astype(F32)
                im = fwd[f, 1, k, rows].astype(F32)
                acc = acc + (re * adj[f, 0, k, rows] - im * adj[f, 1, k, rows])
                one = one + (cosines[0][f] * re + sines[0][f] * im)
                two = two + (cosines[1][f] * re + sines[1][f] * im)
            gain[k, 0, rows] = one
            gain[k, 1, rows] = two
            return acc

        total[rows] = lax.fori_loop(0, 3 * PLANES, entry, jnp.zeros((16, CY), F32))
        return 0

    lax.fori_loop(0, CX // 16, chunk, 0)
    for copy in copies:
        copy.wait()


def exchange(nx, ny, e, h, mat, den, fwd, adj):
    shape = jax.ShapeDtypeStruct
    return pl.pallas_call(
        functools.partial(exchange_kernel, nx, ny),
        name="exchange",
        out_shape=(
            shape((2, CX, 128), F32),
            shape((2, CX, 128), F32),
            shape((4, 8, 128), F32),
            shape((4, 8, 128), F32),
            shape((2 * NZ, 8, CY), F32),
            shape((2 * NZ, 8, CY), F32),
            shape((CX, CY), F32),
            shape((3 * PLANES, STEPS, CX, CY), F32),
        ),
        in_specs=[ANY] * 6,
        out_specs=(VMEM,) * 8,
        scratch_shapes=[
            pltpu.VMEM(e.shape, F32),
            pltpu.VMEM(h.shape, F32),
            pltpu.VMEM(mat.shape, jnp.int32),
            pltpu.VMEM(den.shape, F32),
            pltpu.VMEM(fwd.shape, BF16),
            pltpu.VMEM(adj.shape, F32),
            pltpu.VMEM((2 * NZ, 8, CY), F32),
            pltpu.VMEM((2 * NZ, 8, CY), F32),
            pltpu.SemaphoreType.DMA((6,)),
            pltpu.SemaphoreType.DMA((10,)),
            pltpu.SemaphoreType.DMA((10,)),
        ],
        compiler_params=pltpu.CompilerParams(collective_id=0, has_side_effects=True),
    )(e, h, mat, den, fwd, adj)


def profile(places, total):
    depth = jnp.maximum(jnp.maximum(PML - places, places - (total - 1 - PML)), 0.0) / PML
    return depth * depth * depth


def bend_of(filtered):
    return jnp.tanh(sharpness * (filtered - threshold))


def fdtd_kernel(
    nx, ny,
    e_ref, h_ref, mat_ref, den_ref, table_ref, own, got, rim_prev, rim_next, xprev, xnext, total, gain,
    e_out, h_out, local,
    E, H, CE, damp, ch, cm, slope, inter, strips,
):
    s = pl.program_id(0)
    gx, gy = lax.axis_index("gx"), lax.axis_index("gy")
    has_prev, has_next = gx > 0, gx < nx - 1
    has_left, has_right = gy > 0, gy < ny - 1
    total_x, total_y = nx * CX, ny * CY
    lane = iota((EX, 128), 1)
    half_sum_scale = math.tanh(sharpness * threshold) + math.tanh(sharpness * (1.0 - threshold))

    def xn(f):
        return pltpu.roll(f, EX - 1, 0)

    def xp(f):
        return pltpu.roll(f, 1, 0)

    def yn(f, strip, z):
        a, b = pltpu.roll(f[:, :128], 127, 1), pltpu.roll(f[:, 128:], 127, 1)
        edge = pltpu.roll(strip, 127 - 6 + 128 - z * ZL, 1)
        last = lane == 127
        return jnp.concatenate([jnp.where(last, b, a), jnp.where(last, edge, b)], axis=1)

    def yp(f, strip, z):
        a, b = pltpu.roll(f[:, :128], 1, 1), pltpu.roll(f[:, 128:], 1, 1)
        edge = pltpu.roll(strip, 127 - z * ZL, 1)
        first = lane == 0
        return jnp.concatenate([jnp.where(first, edge, a), jnp.where(first, a, b)], axis=1)

    def x_halo(kind, z):
        q = kind % 4
        sub = iota((8, CY), 0)
        ahead = xnext[2 * z + kind // 4]
        behind = xprev[2 * z + kind // 4]
        if q:
            ahead = pltpu.roll(ahead, 8 - 2 * q, 0)
        if q < 3:
            behind = pltpu.roll(behind, 6 - 2 * q, 0)
        return jnp.where((sub < 2) & has_next, ahead, jnp.where((sub >= 6) & has_prev, behind, 0.0))

    def places(columns, width):
        rows = iota((EX, width), 0)
        rows = gx * CX + jnp.where(rows < CX + 4, rows, rows - EX)
        inside = (rows >= 0) & (rows < total_x) & (columns >= 0) & (columns < total_y)
        sigma = sigma_peak * (profile(rows.astype(F32), total_x) + profile(columns.astype(F32), total_y))
        half = 1.0 + 0.5 * sigma
        damping = jnp.where(inside, (1.0 - 0.5 * sigma) / half, 0.0)
        return inside, half, damping, jnp.where(inside, courant / half, 0.0)

    def design(filtered):
        bend = bend_of(filtered)
        projected = (math.tanh(sharpness * threshold) + bend) / half_sum_scale
        return bend, eps_low + (eps_high - eps_low) * projected

    @pl.when(s == 0)
    def _():
        zero = jnp.zeros((EX, CY), F32)
        for c in range(3):
            E[c, NZ] = zero
            H[c, 0] = zero
        sub = iota((8, 128), 0)
        pieces = []
        for i, body in enumerate((got[0], own[0], own[1], got[1])):
            rim = jnp.where((sub < 4) & has_next, rim_next[i], jnp.where((sub >= 4) & has_prev, rim_prev[i], 0.0))
            piece = jnp.concatenate([body, rim], axis=0)
            if i == 0:
                piece = jnp.where(has_left, piece, 0.0)
            if i == 3:
                piece = jnp.where(has_right, piece, 0.0)
            pieces.append(piece)
        slot = lax.rem(lane, ZL)

        def strip(kind):
            value = jnp.zeros((EX, 128), F32)
            for i, piece in enumerate(pieces):
                shift = (EDGE * i - EDGE * kind) % 128
                moved = pltpu.roll(piece, shift, 1) if shift else piece
                value = jnp.where((slot >= EDGE * i) & (slot < EDGE * (i + 1)), moved, value)
            return value

        inside, half, damping, coef_h = places(gy * CY + iota((EX, CY), 1), CY)
        damp[...] = damping
        ch[...] = coef_h
        dens = jnp.concatenate([den_ref[...], x_halo(7, 0)], axis=0)
        dens_s = strip(7)
        sums = xp(dens) + 2.0 * dens + xn(dens)
        sums_s = xp(dens_s) + 2.0 * dens_s + xn(dens_s)
        filtered = (yp(sums, sums_s, ZLO) + 2.0 * sums + yn(sums, sums_s, ZLO)) / 16.0
        filtered_s = (pltpu.roll(sums_s, 1, 1) + 2.0 * sums_s + pltpu.roll(sums_s, 127, 1)) / 16.0
        bend, design_eps = design(filtered)
        slope[...] = (sharpness * (1.0 - bend * bend) / half_sum_scale)[:CX]
        for k in range(MATS):
            cm[k] = jnp.where(inside, courant / (table_ref[k] * half), 0.0)
        cm[MATS] = jnp.where(inside, courant / (design_eps * half), 0.0)
        inter[...] = total[...]

        columns = gy * CY + jnp.where(slot < 4, slot - EDGE, slot + (CY - EDGE - 4))
        inside, half, damping, coef_h = places(columns, 128)
        inside = inside & (slot < 8)
        damping = jnp.where(slot < 8, damping, 0.0)
        coef_h = jnp.where(slot < 8, coef_h, 0.0)
        mats = strip(6)
        eps = jnp.zeros((EX, 128), F32)
        for k in range(MATS):
            eps = jnp.where(mats == float(k), table_ref[k], eps)
        layer = (lane >= ZLO * ZL) & (lane < (ZLO + PLANES) * ZL)
        eps = jnp.where(layer, design(filtered_s)[1], eps)
        coef_e = jnp.where(inside, courant / (eps * half), 0.0)

        def yns(f):
            return pltpu.roll(f, 127, 1)

        def yps(f):
            return pltpu.roll(f, 1, 1)

        def zns(f):
            return jnp.where(lane < 128 - ZL, pltpu.roll(f, 128 - ZL, 1), 0.0)

        def zps(f):
            return jnp.where(lane >= ZL, pltpu.roll(f, ZL, 1), 0.0)

        def strip_h(ex, ey, ez, hx, hy, hz):
            cx = (yns(ez) - ez) - (zns(ey) - ey)
            cy = (zns(ex) - ex) - (xn(ez) - ez)
            cz = (xn(ey) - ey) - (yns(ex) - ex)
            return damping * hx - coef_h * cx, damping * hy - coef_h * cy, damping * hz - coef_h * cz

        def strip_e(ex, ey, ez, hx, hy, hz):
            cx = (hz - yps(hz)) - (hy - zps(hy))
            cy = (hx - zps(hx)) - (hz - xp(hz))
            cz = (hy - xp(hy)) - (hx - yps(hx))
            return damping * ex + coef_e * cx, damping * ey + coef_e * cy, damping * ez + coef_e * cz

        es = tuple(strip(c) for c in range(3))
        hs = tuple(strip(c) for c in range(3, 6))
        strips[0], strips[1] = es[0], es[2]
        hs = strip_h(*es, *hs)
        strips[2], strips[3] = hs[0], hs[2]
        es = strip_e(*es, *hs)
        strips[4], strips[5] = es[0], es[2]
        hs = strip_h(*es, *hs)
        strips[6], strips[7] = hs[0], hs[2]

    @pl.when(s < NZ)
    def _():
        for c in range(3):
            E[c, s] = jnp.concatenate([e_ref[c, 0], x_halo(c, s)], axis=0)
            H[c, s + 1] = jnp.concatenate([h_ref[c, 0], x_halo(3 + c, s)], axis=0)
        mats = jnp.concatenate([mat_ref[0].astype(F32), x_halo(6, s)], axis=0)
        mats = jnp.where((s >= ZLO) & (s < ZLO + PLANES), float(MATS), mats)
        coef = cm[MATS]
        for k in range(MATS):
            coef = jnp.where(mats == float(k), cm[k], coef)
        CE[s] = coef

    def half_h(z, first):
        ex, ey, ez = E[0, z], E[1, z], E[2, z]
        d, c = damp[...], ch[...]
        H[0, z + 1] = d * H[0, z + 1] - c * ((yn(ez, strips[first + 1], z) - ez) - (E[1, z + 1] - ey))
        H[1, z + 1] = d * H[1, z + 1] - c * ((E[0, z + 1] - ex) - (xn(ez) - ez))
        H[2, z + 1] = d * H[2, z + 1] - c * ((xn(ey) - ey) - (yn(ex, strips[first], z) - ex))

    def half_e(z, first):
        hx, hy, hz = H[0, z + 1], H[1, z + 1], H[2, z + 1]
        d, c = damp[...], CE[z]
        E[0, z] = d * E[0, z] + c * ((hz - yp(hz, strips[first + 1], z)) - (hy - H[1, z]))
        E[1, z] = d * E[1, z] + c * ((hx - H[0, z]) - (hz - xp(hz)))
        E[2, z] = d * E[2, z] + c * ((hy - xp(hy)) - (hx - yp(hx, strips[first], z)))

    def collect(z, n):
        @pl.when((z >= ZLO) & (z < ZLO + PLANES))
        def _():
            acc = inter[...]
            for c in range(3):
                acc = acc + gain[PLANES * c + (z - ZLO), n] * E[c, z, :CX]
            inter[...] = acc

    @pl.when((s >= 1) & (s <= NZ))
    def _():
        z = s - 1
        half_h(z, 0)
        half_e(z, 2)
        collect(z, 0)

    @pl.when(s >= 2)
    def _():
        z = s - 2
        half_h(z, 4)
        half_e(z, 6)
        collect(z, 1)
        for c in range(3):
            e_out[c, 0] = E[c, z, :CX]
            h_out[c, 0] = H[c, z + 1, :CX]

    @pl.when(s == NZ + 1)
    def _():
        local[...] = grad_scale * (eps_high - eps_low) * slope[...] * inter[...]


def fdtd(nx, ny, e, h, mat, den, table, halo):
    whole = lambda array: pl.BlockSpec(array.shape, lambda s: (0,) * array.ndim)
    incoming = pl.BlockSpec((3, 1, CX, CY), lambda s: (0, jnp.minimum(s, NZ - 1), 0, 0))
    outgoing = pl.BlockSpec((3, 1, CX, CY), lambda s: (0, jnp.maximum(s - 2, 0), 0, 0))
    shape = jax.ShapeDtypeStruct
    return pl.pallas_call(
        functools.partial(fdtd_kernel, nx, ny),
        name="fdtd",
        grid=(NZ + 2,),
        out_shape=(shape(e.shape, F32), shape(h.shape, F32), shape((CX, CY), F32)),
        in_specs=[
            incoming,
            incoming,
            pl.BlockSpec((1, CX, CY), lambda s: (jnp.minimum(s, NZ - 1), 0, 0)),
            whole(den),
            pl.BlockSpec(memory_space=pltpu.SMEM),
        ]
        + [whole(array) for array in halo],
        out_specs=(outgoing, outgoing, pl.BlockSpec((CX, CY), lambda s: (0, 0))),
        scratch_shapes=[
            pltpu.VMEM((3, NZ + 1, EX, CY), F32),
            pltpu.VMEM((3, NZ + 1, EX, CY), F32),
            pltpu.VMEM((NZ, EX, CY), F32),
            pltpu.VMEM((EX, CY), F32),
            pltpu.VMEM((EX, CY), F32),
            pltpu.VMEM((MATS + 1, EX, CY), F32),
            pltpu.VMEM((CX, CY), F32),
            pltpu.VMEM((CX, CY), F32),
            pltpu.VMEM((8, EX, 128), F32),
        ],
    )(e, h, mat, den, table, *halo)


def tiles_kernel(
    G, Zn,
    local, tile_map, out,
    rim_left, rim_right, rim_prev, rim_next, corner, cells, message, gathered, sums, arrived, ready, landed,
    rim_send, rim_recv, a_send, a_recv, b_send, b_recv, c_send, c_recv,
):
    gx, gy = lax.axis_index("gx"), lax.axis_index("gy")
    nx, ny = Zn * G, 2 * G
    x, core = gy // 2, lax.rem(gy, 2)
    z, y = gx // G, lax.rem(gx, G)

    def dev(x, y, z, core):
        return (z * G + y, x * 2 + core)

    near = around(gx, gy, nx, ny)
    partners = list(near.values())
    for k in range(1, G):
        for c in range(2):
            partners.append(dev(wrapped(x, k, G), y, z, c))
            partners.append(dev(x, wrapped(y, k, G), z, c))
    partners.append(dev(x, y, z, 1 - core))
    for k in range(1, Zn):
        for c in range(2):
            partners.append(dev(x, y, wrapped(z, k, Zn), c))
    barrier = pltpu.get_barrier_semaphore()
    for device in partners:
        pl.semaphore_signal(barrier, inc=1, device_id=device, device_id_type=MESH)
    pl.semaphore_wait(barrier, len(partners))

    low, high, top, bottom = pl.ds(0, 128), pl.ds(128, 128), pl.ds(0, 8), pl.ds(CX - 8, 8)
    plan = (
        (local.at[:, high], rim_left, (0, 1)),
        (local.at[:, low], rim_right, (0, -1)),
        (local.at[bottom], rim_prev, (1, 0)),
        (local.at[top], rim_next, (-1, 0)),
        (local.at[bottom, high], corner.at[0], (1, 1)),
        (local.at[bottom, low], corner.at[1], (1, -1)),
        (local.at[top, high], corner.at[2], (-1, 1)),
        (local.at[top, low], corner.at[3], (-1, -1)),
    )
    rims = [remote(src, dst, rim_send.at[i], rim_recv.at[i], near[to]) for i, (src, dst, to) in enumerate(plan)]
    for copy in rims:
        copy.start()

    lane8 = iota((8, 128), 1)
    names = jnp.zeros((8, 128), F32)
    for j in range(4):
        names = jnp.where(((lane8 == j) | (lane8 == 4 + j)), tile_map[0, j].astype(F32), names)
    message[0, pl.ds(CX, 8)] = names
    message[1, pl.ds(CX, 8)] = names

    for copy in rims:
        copy.wait_recv()

    lane = iota((EX, 128), 1)
    sub = iota((8, 128), 0)
    wide = iota((8, CY), 0)
    has_prev, has_next = gx > 0, gx < nx - 1
    has_left, has_right = gy > 0, gy < ny - 1
    rows = jnp.where((wide < 4) & has_next, rim_next[...], jnp.where((wide >= 4) & has_prev, rim_prev[...], 0.0))
    main = jnp.concatenate([local[...], rows], axis=0)
    left = jnp.concatenate(
        [
            rim_left[...],
            jnp.where((sub < 4) & has_next, corner[2], jnp.where((sub >= 4) & has_prev, corner[0], 0.0)),
        ],
        axis=0,
    )
    left = jnp.where(has_left, left, 0.0)
    right = jnp.concatenate(
        [
            rim_right[...],
            jnp.where((sub < 4) & has_next, corner[3], jnp.where((sub >= 4) & has_prev, corner[1], 0.0)),
        ],
        axis=0,
    )
    right = jnp.where(has_right, right, 0.0)

    def along_x(f):
        return pltpu.roll(f, 1, 0) + 2.0 * f + pltpu.roll(f, EX - 1, 0)

    a, b = along_x(main[:, :128]), along_x(main[:, 128:])
    left, right = along_x(left), along_x(right)
    first, last = lane == 0, lane == 127
    ra, rb = pltpu.roll(a, 1, 1), pltpu.roll(b, 1, 1)
    la, lb = pltpu.roll(a, 127, 1), pltpu.roll(b, 127, 1)
    left, right = pltpu.roll(left, 1, 1), pltpu.roll(right, 127, 1)
    a = (jnp.where(first, left, ra) + 2.0 * a + jnp.where(last, lb, la)) / 16.0
    b = (jnp.where(first, ra, rb) + 2.0 * b + jnp.where(last, right, lb)) / 16.0
    cells[0] = a[:CX]
    cells[1] = b[:CX]

    narrow = iota((CX // 2, 128), 1) < TILE
    for j in range(4):
        even = cells[j // 2, pl.ds(0, CX // 2, stride=2), :]
        odd = cells[j // 2, pl.ds(1, CX // 2, stride=2), :]
        if j % 2:
            tile = jnp.where(narrow, pltpu.roll(even, TILE, 1), odd)
        else:
            tile = jnp.where(narrow, even, pltpu.roll(odd, TILE, 1))
        for h in range(2):
            message[h, pl.ds(j, 16, stride=4), :] = tile[16 * h : 16 * h + 16]

    sends = []
    for k in range(1, G):
        sends.append((message.at[0], 2 * k + core, dev(wrapped(x, k, G), y, z, 0)))
        sends.append((message.at[1], 2 * k + core, dev(x, wrapped(y, k, G), z, 1)))
    sends.append((message.at[1 - core], core, dev(x, y, z, 1 - core)))
    first_stop = [
        remote(src, gathered.at[slot], a_send.at[i], a_recv.at[slot], to) for i, (src, slot, to) in enumerate(sends)
    ]
    for copy in first_stop:
        copy.start()
    gathered[core] = message[core]

    def arrival(slot):
        return remote(message.at[0], gathered.at[slot], a_send.at[0], a_recv.at[slot], dev(x, y, z, 1 - core))

    arrival(1 - core).wait_recv()
    for k in range(1, G):
        for c in range(2):
            arrival(2 * k + c).wait_recv()

    slots = 2 * G
    K = slots * 8
    P_rows = G * Zn * 2
    per = Zn * 2
    found = jnp.zeros((8, 128), F32)
    for slot in range(slots):
        part = gathered[slot, pl.ds(CX, 8)]
        part = pltpu.roll(part, 8 * slot, 1) if slot else part
        found = jnp.where((lane8 >= 8 * slot) & (lane8 < 8 * slot + 8), part, found)
    shift = K
    while shift < 128:
        found = jnp.where(lane8 < shift, found, pltpu.roll(found, shift, 1))
        shift *= 2
    found = jnp.broadcast_to(found[0:1], (2 * P_rows, 128))
    found = jnp.concatenate([found] * max(1, 4 * K // 128), axis=1)
    row = iota((2 * P_rows, 4 * K), 0)
    column = iota((2 * P_rows, 4 * K), 1)
    q = lax.rem(row // per, G)
    place = lax.rem(row, per)
    fixed = (1 - core) * (x * 2) + core * (y * (2 * G))
    param = (place // 2) * (2 * G * G) + lax.rem(place, 2) + q * ((1 - core) * (2 * G) + core * 2) + fixed
    same = (row // P_rows == lax.rem(column, 8) // 4) & (column < 3 * K)
    chosen = jnp.where(same & (found == param.astype(F32)), 1.0, 0.0).astype(BF16)

    for m in range(8):
        data = jnp.concatenate([gathered[slot, pl.ds(8 * m, 8)] for slot in range(slots)], axis=0)
        hi = data.astype(BF16)
        rest = data - hi.astype(F32)
        mid = rest.astype(BF16)
        lo = (rest - mid.astype(F32)).astype(BF16)
        picked = jnp.dot(chosen, jnp.concatenate([hi, mid, lo, hi], axis=0), preferred_element_type=F32)
        for parity in range(2):
            for place_q in range(G):
                start = parity * P_rows + place_q * per
                sums[place_q, 2 * m + parity] = picked[start : start + per]

    mine = (1 - core) * y + core * x
    second_stop = []
    for k in range(1, G):
        there = wrapped(mine, k, G)
        to = dev((1 - core) * x + core * there, (1 - core) * there + core * y, z, core)
        second_stop.append(remote(sums.at[there], arrived.at[k - 1], b_send.at[k - 1], b_recv.at[k - 1], to))
    for copy in second_stop:
        copy.start()
    for copy in second_stop:
        copy.wait_recv()
    for b in range(16):
        value = sums[mine, b]
        for k in range(G - 1):
            value = value + arrived[k, b]
        ready[pl.ds(b, per, stride=16), :] = value

    third_stop = []
    for k in range(Zn - 1, -1, -1):
        there = wrapped(z, k, Zn)
        for c in range(2):
            if k == 0 and c == 0:
                continue
            target = c if k else 1 - core
            start = pl.multiple_of((there * 2 + target) * 16, 16)
            i = 2 * k + c
            third_stop.append(
                remote(
                    ready.at[pl.ds(start, 16)], landed.at[2 * k + core], c_send.at[i], c_recv.at[2 * k + core],
                    dev(x, y, there, target),
                )
            )
    for copy in third_stop:
        copy.start()
    landed[core] = ready[pl.ds(pl.multiple_of((z * 2 + core) * 16, 16), 16)]

    def landing(slot):
        return remote(
            ready.at[pl.ds(0, 16)], landed.at[slot], c_send.at[0], c_recv.at[slot], dev(x, y, z, 1 - core)
        )

    landing(1 - core).wait_recv()
    for k in range(1, Zn):
        for c in range(2):
            landing(2 * k + c).wait_recv()
    for h in range(2):
        value = landed[h]
        for k in range(1, Zn):
            value = value + landed[2 * k + h]
        out[pl.ds(16 * h, 16)] = value
    for copy in rims + first_stop + second_stop + third_stop:
        copy.wait_send()


def route_tiles(G, Zn, local, tile_map):
    per = Zn * 2
    dma = pltpu.SemaphoreType.DMA
    return pl.pallas_call(
        functools.partial(tiles_kernel, G, Zn),
        name="tiles",
        out_shape=jax.ShapeDtypeStruct((32, 128), F32),
        in_specs=[VMEM, pl.BlockSpec(memory_space=pltpu.SMEM)],
        out_specs=VMEM,
        scratch_shapes=[
            pltpu.VMEM((CX, 128), F32),
            pltpu.VMEM((CX, 128), F32),
            pltpu.VMEM((8, CY), F32),
            pltpu.VMEM((8, CY), F32),
            pltpu.VMEM((4, 8, 128), F32),
            pltpu.VMEM((2, CX, 128), F32),
            pltpu.VMEM((2, CX + 8, 128), F32),
            pltpu.VMEM((2 * G, CX + 8, 128), F32),
            pltpu.VMEM((G, 16, per, 128), F32),
            pltpu.VMEM((G - 1, 16, per, 128), F32),
            pltpu.VMEM((per * 16, 128), F32),
            pltpu.VMEM((2 * Zn, 16, 128), F32),
            dma((8,)),
            dma((8,)),
            dma((2 * G,)),
            dma((2 * G,)),
            dma((G - 1,)),
            dma((G - 1,)),
            dma((2 * Zn,)),
            dma((2 * Zn,)),
        ],
        compiler_params=pltpu.CompilerParams(collective_id=1, has_side_effects=True),
    )(local, tile_map)


def on_device(nx, ny, e_adj, h_adj, density, material, eps_table, dft_adj, dft_fwd, tile_map):
    G = ny // 2
    flat = lambda array: array.reshape(FREQ, 2, 3 * PLANES, CX, CY)
    halo = exchange(nx, ny, e_adj, h_adj, material, density, flat(dft_fwd), flat(dft_adj))
    e_out, h_out, local = fdtd(nx, ny, e_adj, h_adj, material, density, eps_table, halo)
    params = route_tiles(G, nx // G, local, tile_map)
    return e_out, h_out, params.reshape(1, TILE * TILE)


def solution(mesh):
    in_specs = (
        P(None, None, "gx", "gy"),
        P(None, None, "gx", "gy"),
        P("gx", "gy"),
        P(None, "gx", "gy"),
        P(),
        P(None, None, None, None, "gx", "gy"),
        P(None, None, None, None, "gx", "gy"),
        P("gx", "gy"),
    )
    out_specs = (P(None, None, "gx", "gy"), P(None, None, "gx", "gy"), P(("gx", "gy"), None))
    return jax.shard_map(
        functools.partial(on_device, mesh.shape["gx"], mesh.shape["gy"]),
        mesh=mesh,
        in_specs=in_specs,
        out_specs=out_specs,
        check_vma=False,
    )
```

```python
import functools
import math

import jax
import jax.numpy as jnp
from jax import lax
from jax.experimental import pallas as pl
from jax.experimental.pallas import tpu as pltpu
from jax.sharding import PartitionSpec as P

MESH = pl.DeviceIdType.MESH

PLANES = 2
ZLO = 3
STEPS = 2
FREQ = 4
PML = 12
MATS = 4
TILE = 64

courant = 0.5
sigma_peak = 0.8
dft_weight = 0.5
sharpness = 4.0
threshold = 0.5
eps_low = 2.1
eps_high = 12.1
grad_scale = 0.01

F32 = jnp.float32
BF16 = jnp.bfloat16
VMEM = pl.BlockSpec(memory_space=pltpu.VMEM)
ANY = pl.BlockSpec(memory_space=pl.ANY)

CX, CY, NZ = 64, 256, 8
EX = CX + 8
KINDS = 8
EDGE = 2
ZL = KINDS * EDGE


def iota(shape, dim):
    return lax.broadcasted_iota(jnp.int32, shape, dim)


def wrapped(index, shift, count):
    return lax.rem(index + (shift + count), count)


def around(gx, gy, nx, ny):
    places = {}
    for dx in (-1, 0, 1):
        for dy in (-1, 0, 1):
            if dx or dy:
                places[dx, dy] = (wrapped(gx, dx, nx), wrapped(gy, dy, ny))
    return places


def remote(src, dst, send, recv, device):
    return pltpu.make_async_remote_copy(
        src_ref=src, dst_ref=dst, send_sem=send, recv_sem=recv, device_id=device, device_id_type=MESH
    )


def exchange_kernel(
    nx, ny,
    e_hbm, h_hbm, mat_hbm, den_hbm, fwd_hbm, adj_hbm,
    own, got, rim_prev, rim_next, xprev, xnext, total, gain,
    e, h, mat, den, fwd, adj, xdown, xup, load_sem, send_sem, recv_sem,
):
    gx, gy = lax.axis_index("gx"), lax.axis_index("gy")
    near = around(gx, gy, nx, ny)
    barrier = pltpu.get_barrier_semaphore()
    for device in near.values():
        pl.semaphore_signal(barrier, inc=1, device_id=device, device_id_type=MESH)

    loads = [
        pltpu.make_async_copy(src, dst, load_sem.at[i])
        for i, (src, dst) in enumerate(
            ((e_hbm, e), (h_hbm, h), (mat_hbm, mat), (den_hbm, den), (fwd_hbm, fwd), (adj_hbm, adj))
        )
    ]
    for load in loads:
        load.start()
    for load in loads[:4]:
        load.wait()

    lane = iota((CX, 128), 1)
    sub = iota((8, CY), 0)

    def plane(kind, z, rows, columns):
        if kind < 3:
            return e[kind, z, rows, columns]
        if kind < 6:
            return h[kind - 3, z, rows, columns]
        if kind == 6:
            return mat[z, rows, columns].astype(F32)
        return den[rows, columns]

    def pack(z, carry):
        first, last = carry
        every, low, high = pl.ds(0, CX), pl.ds(0, 128), pl.ds(128, 128)
        left = jnp.zeros((CX, 128), F32)
        right = jnp.zeros((CX, 128), F32)
        for kind in range(KINDS):
            mine = (lane >= EDGE * kind) & (lane < EDGE * (kind + 1))
            a = plane(kind, z, every, low)
            b = plane(kind, z, every, high)
            left = jnp.where(mine, pltpu.roll(a, EDGE * kind, 1) if kind else a, left)
            right = jnp.where(mine, pltpu.roll(b, EDGE * kind + EDGE, 1), right)
        first = first + pltpu.roll(left, z * ZL, 1)
        last = last + pltpu.roll(right, z * ZL, 1)
        for group in range(2):
            up = jnp.zeros((8, CY), F32)
            down = jnp.zeros((8, CY), F32)
            for q in range(4):
                kind = 4 * group + q
                mine = (sub >= 2 * q) & (sub < 2 * q + 2)
                a = plane(kind, z, pl.ds(0, 8), pl.ds(0, CY))
                b = plane(kind, z, pl.ds(CX - 8, 8), pl.ds(0, CY))
                up = jnp.where(mine, pltpu.roll(a, 2 * q, 0) if q else a, up)
                down = jnp.where(mine, pltpu.roll(b, 2 * q + 2, 0) if q < 3 else b, down)
            xup[2 * z + group] = up
            xdown[2 * z + group] = down
        return first, last

    empty = jnp.zeros((CX, 128), F32)
    first, last = lax.fori_loop(0, NZ, pack, (empty, empty))
    own[0] = first
    own[1] = last

    pl.semaphore_wait(barrier, 8)
    top, bottom = pl.ds(0, 8), pl.ds(CX - 8, 8)
    plan = (
        (own.at[1], got.at[0], (0, 1)),
        (own.at[0], got.at[1], (0, -1)),
        (xdown, xprev, (1, 0)),
        (xup, xnext, (-1, 0)),
        (own.at[:, bottom], rim_prev.at[pl.ds(1, 2)], (1, 0)),
        (own.at[:, top], rim_next.at[pl.ds(1, 2)], (-1, 0)),
        (own.at[1, bottom], rim_prev.at[0], (1, 1)),
        (own.at[0, bottom], rim_prev.at[3], (1, -1)),
        (own.at[1, top], rim_next.at[0], (-1, 1)),
        (own.at[0, top], rim_next.at[3], (-1, -1)),
    )
    copies = [
        remote(src, dst, send_sem.at[i], recv_sem.at[i], near[to]) for i, (src, dst, to) in enumerate(plan)
    ]
    for copy in copies:
        copy.start()

    for load in loads[4:]:
        load.wait()
    cosines = [[dft_weight * math.cos((0.21 + 0.06 * f) * (n + 1)) for f in range(FREQ)] for n in range(STEPS)]
    sines = [[dft_weight * math.sin((0.21 + 0.06 * f) * (n + 1)) for f in range(FREQ)] for n in range(STEPS)]

    def chunk(r, _):
        rows = pl.ds(pl.multiple_of(r * 16, 16), 16)

        def entry(k, acc):
            one = jnp.zeros((16, CY), F32)
            two = jnp.zeros((16, CY), F32)
            for f in range(FREQ):
                re = fwd[f, 0, k, rows].astype(F32)
                im = fwd[f, 1, k, rows].astype(F32)
                acc = acc + (re * adj[f, 0, k, rows] - im * adj[f, 1, k, rows])
                one = one + (cosines[0][f] * re + sines[0][f] * im)
                two = two + (cosines[1][f] * re + sines[1][f] * im)
            gain[k, 0, rows] = one
            gain[k, 1, rows] = two
            return acc

        total[rows] = lax.fori_loop(0, 3 * PLANES, entry, jnp.zeros((16, CY), F32))
        return 0

    lax.fori_loop(0, CX // 16, chunk, 0)
    for copy in copies:
        copy.wait()


def exchange(nx, ny, e, h, mat, den, fwd, adj):
    shape = jax.ShapeDtypeStruct
    return pl.pallas_call(
        functools.partial(exchange_kernel, nx, ny),
        name="exchange",
        out_shape=(
            shape((2, CX, 128), F32),
            shape((2, CX, 128), F32),
            shape((4, 8, 128), F32),
            shape((4, 8, 128), F32),
            shape((2 * NZ, 8, CY), F32),
            shape((2 * NZ, 8, CY), F32),
            shape((CX, CY), F32),
            shape((3 * PLANES, STEPS, CX, CY), F32),
        ),
        in_specs=[ANY] * 6,
        out_specs=(VMEM,) * 8,
        scratch_shapes=[
            pltpu.VMEM(e.shape, F32),
            pltpu.VMEM(h.shape, F32),
            pltpu.VMEM(mat.shape, jnp.int32),
            pltpu.VMEM(den.shape, F32),
            pltpu.VMEM(fwd.shape, BF16),
            pltpu.VMEM(adj.shape, F32),
            pltpu.VMEM((2 * NZ, 8, CY), F32),
            pltpu.VMEM((2 * NZ, 8, CY), F32),
            pltpu.SemaphoreType.DMA((6,)),
            pltpu.SemaphoreType.DMA((10,)),
            pltpu.SemaphoreType.DMA((10,)),
        ],
        compiler_params=pltpu.CompilerParams(collective_id=0, has_side_effects=True),
    )(e, h, mat, den, fwd, adj)


def profile(places, total):
    depth = jnp.maximum(jnp.maximum(PML - places, places - (total - 1 - PML)), 0.0) / PML
    return depth * depth * depth


def bend_of(filtered):
    return jnp.tanh(sharpness * (filtered - threshold))


def fdtd_kernel(
    nx, ny,
    e_ref, h_ref, mat_ref, den_ref, table_ref, own, got, rim_prev, rim_next, xprev, xnext, total, gain,
    e_out, h_out, local,
    E, H, CE, damp, ch, cm, slope, inter, strips,
):
    s = pl.program_id(0)
    gx, gy = lax.axis_index("gx"), lax.axis_index("gy")
    has_prev, has_next = gx > 0, gx < nx - 1
    has_left, has_right = gy > 0, gy < ny - 1
    total_x, total_y = nx * CX, ny * CY
    lane = iota((EX, 128), 1)
    half_sum_scale = math.tanh(sharpness * threshold) + math.tanh(sharpness * (1.0 - threshold))

    def xn(f):
        return pltpu.roll(f, EX - 1, 0)

    def xp(f):
        return pltpu.roll(f, 1, 0)

    def yn(f, strip, z):
        a, b = pltpu.roll(f[:, :128], 127, 1), pltpu.roll(f[:, 128:], 127, 1)
        edge = pltpu.roll(strip, 127 - 6 + 128 - z * ZL, 1)
        last = lane == 127
        return jnp.concatenate([jnp.where(last, b, a), jnp.where(last, edge, b)], axis=1)

    def yp(f, strip, z):
        a, b = pltpu.roll(f[:, :128], 1, 1), pltpu.roll(f[:, 128:], 1, 1)
        edge = pltpu.roll(strip, 127 - z * ZL, 1)
        first = lane == 0
        return jnp.concatenate([jnp.where(first, edge, a), jnp.where(first, a, b)], axis=1)

    def x_halo(kind, z):
        q = kind % 4
        sub = iota((8, CY), 0)
        ahead = xnext[2 * z + kind // 4]
        behind = xprev[2 * z + kind // 4]
        if q:
            ahead = pltpu.roll(ahead, 8 - 2 * q, 0)
        if q < 3:
            behind = pltpu.roll(behind, 6 - 2 * q, 0)
        return jnp.where((sub < 2) & has_next, ahead, jnp.where((sub >= 6) & has_prev, behind, 0.0))

    def places(columns, width):
        rows = iota((EX, width), 0)
        rows = gx * CX + jnp.where(rows < CX + 4, rows, rows - EX)
        inside = (rows >= 0) & (rows < total_x) & (columns >= 0) & (columns < total_y)
        sigma = sigma_peak * (profile(rows.astype(F32), total_x) + profile(columns.astype(F32), total_y))
        half = 1.0 + 0.5 * sigma
        damping = jnp.where(inside, (1.0 - 0.5 * sigma) / half, 0.0)
        return inside, half, damping, jnp.where(inside, courant / half, 0.0)

    def design(filtered):
        bend = bend_of(filtered)
        projected = (math.tanh(sharpness * threshold) + bend) / half_sum_scale
        return bend, eps_low + (eps_high - eps_low) * projected

    @pl.when(s == 0)
    def _():
        zero = jnp.zeros((EX, CY), F32)
        for c in range(3):
            E[c, NZ] = zero
            H[c, 0] = zero
        sub = iota((8, 128), 0)
        pieces = []
        for i, body in enumerate((got[0], own[0], own[1], got[1])):
            rim = jnp.where((sub < 4) & has_next, rim_next[i], jnp.where((sub >= 4) & has_prev, rim_prev[i], 0.0))
            piece = jnp.concatenate([body, rim], axis=0)
            if i == 0:
                piece = jnp.where(has_left, piece, 0.0)
            if i == 3:
                piece = jnp.where(has_right, piece, 0.0)
            pieces.append(piece)
        slot = lax.rem(lane, ZL)

        def strip(kind):
            value = jnp.zeros((EX, 128), F32)
            for i, piece in enumerate(pieces):
                shift = (EDGE * i - EDGE * kind) % 128
                moved = pltpu.roll(piece, shift, 1) if shift else piece
                value = jnp.where((slot >= EDGE * i) & (slot < EDGE * (i + 1)), moved, value)
            return value

        inside, half, damping, coef_h = places(gy * CY + iota((EX, CY), 1), CY)
        damp[...] = damping
        ch[...] = coef_h
        dens = jnp.concatenate([den_ref[...], x_halo(7, 0)], axis=0)
        dens_s = strip(7)
        sums = xp(dens) + 2.0 * dens + xn(dens)
        sums_s = xp(dens_s) + 2.0 * dens_s + xn(dens_s)
        filtered = (yp(sums, sums_s, ZLO) + 2.0 * sums + yn(sums, sums_s, ZLO)) / 16.0
        filtered_s = (pltpu.roll(sums_s, 1, 1) + 2.0 * sums_s + pltpu.roll(sums_s, 127, 1)) / 16.0
        bend, design_eps = design(filtered)
        slope[...] = (sharpness * (1.0 - bend * bend) / half_sum_scale)[:CX]
        for k in range(MATS):
            cm[k] = jnp.where(inside, courant / (table_ref[k] * half), 0.0)
        cm[MATS] = jnp.where(inside, courant / (design_eps * half), 0.0)
        inter[...] = total[...]

        columns = gy * CY + jnp.where(slot < 4, slot - EDGE, slot + (CY - EDGE - 4))
        inside, half, damping, coef_h = places(columns, 128)
        inside = inside & (slot < 8)
        damping = jnp.where(slot < 8, damping, 0.0)
        coef_h = jnp.where(slot < 8, coef_h, 0.0)
        mats = strip(6)
        eps = jnp.zeros((EX, 128), F32)
        for k in range(MATS):
            eps = jnp.where(mats == float(k), table_ref[k], eps)
        layer = (lane >= ZLO * ZL) & (lane < (ZLO + PLANES) * ZL)
        eps = jnp.where(layer, design(filtered_s)[1], eps)
        coef_e = jnp.where(inside, courant / (eps * half), 0.0)

        def yns(f):
            return pltpu.roll(f, 127, 1)

        def yps(f):
            return pltpu.roll(f, 1, 1)

        def zns(f):
            return jnp.where(lane < 128 - ZL, pltpu.roll(f, 128 - ZL, 1), 0.0)

        def zps(f):
            return jnp.where(lane >= ZL, pltpu.roll(f, ZL, 1), 0.0)

        def strip_h(ex, ey, ez, hx, hy, hz):
            cx = (yns(ez) - ez) - (zns(ey) - ey)
            cy = (zns(ex) - ex) - (xn(ez) - ez)
            cz = (xn(ey) - ey) - (yns(ex) - ex)
            return damping * hx - coef_h * cx, damping * hy - coef_h * cy, damping * hz - coef_h * cz

        def strip_e(ex, ey, ez, hx, hy, hz):
            cx = (hz - yps(hz)) - (hy - zps(hy))
            cy = (hx - zps(hx)) - (hz - xp(hz))
            cz = (hy - xp(hy)) - (hx - yps(hx))
            return damping * ex + coef_e * cx, damping * ey + coef_e * cy, damping * ez + coef_e * cz

        es = tuple(strip(c) for c in range(3))
        hs = tuple(strip(c) for c in range(3, 6))
        strips[0], strips[1] = es[0], es[2]
        hs = strip_h(*es, *hs)
        strips[2], strips[3] = hs[0], hs[2]
        es = strip_e(*es, *hs)
        strips[4], strips[5] = es[0], es[2]
        hs = strip_h(*es, *hs)
        strips[6], strips[7] = hs[0], hs[2]

    @pl.when(s < NZ)
    def _():
        for c in range(3):
            E[c, s] = jnp.concatenate([e_ref[c, 0], x_halo(c, s)], axis=0)
            H[c, s + 1] = jnp.concatenate([h_ref[c, 0], x_halo(3 + c, s)], axis=0)
        mats = jnp.concatenate([mat_ref[0].astype(F32), x_halo(6, s)], axis=0)
        mats = jnp.where((s >= ZLO) & (s < ZLO + PLANES), float(MATS), mats)
        coef = cm[MATS]
        for k in range(MATS):
            coef = jnp.where(mats == float(k), cm[k], coef)
        CE[s] = coef

    def half_h(z, first):
        ex, ey, ez = E[0, z], E[1, z], E[2, z]
        d, c = damp[...], ch[...]
        H[0, z + 1] = d * H[0, z + 1] - c * ((yn(ez, strips[first + 1], z) - ez) - (E[1, z + 1] - ey))
        H[1, z + 1] = d * H[1, z + 1] - c * ((E[0, z + 1] - ex) - (xn(ez) - ez))
        H[2, z + 1] = d * H[2, z + 1] - c * ((xn(ey) - ey) - (yn(ex, strips[first], z) - ex))

    def half_e(z, first):
        hx, hy, hz = H[0, z + 1], H[1, z + 1], H[2, z + 1]
        d, c = damp[...], CE[z]
        E[0, z] = d * E[0, z] + c * ((hz - yp(hz, strips[first + 1], z)) - (hy - H[1, z]))
        E[1, z] = d * E[1, z] + c * ((hx - H[0, z]) - (hz - xp(hz)))
        E[2, z] = d * E[2, z] + c * ((hy - xp(hy)) - (hx - yp(hx, strips[first], z)))

    def collect(z, n):
        @pl.when((z >= ZLO) & (z < ZLO + PLANES))
        def _():
            acc = inter[...]
            for c in range(3):
                acc = acc + gain[PLANES * c + (z - ZLO), n] * E[c, z, :CX]
            inter[...] = acc

    @pl.when((s >= 1) & (s <= NZ))
    def _():
        z = s - 1
        half_h(z, 0)
        half_e(z, 2)
        collect(z, 0)

    @pl.when(s >= 2)
    def _():
        z = s - 2
        half_h(z, 4)
        half_e(z, 6)
        collect(z, 1)
        for c in range(3):
            e_out[c, 0] = E[c, z, :CX]
            h_out[c, 0] = H[c, z + 1, :CX]

    @pl.when(s == NZ + 1)
    def _():
        local[...] = grad_scale * (eps_high - eps_low) * slope[...] * inter[...]


def fdtd(nx, ny, e, h, mat, den, table, halo):
    whole = lambda array: pl.BlockSpec(array.shape, lambda s: (0,) * array.ndim)
    incoming = pl.BlockSpec((3, 1, CX, CY), lambda s: (0, jnp.minimum(s, NZ - 1), 0, 0))
    outgoing = pl.BlockSpec((3, 1, CX, CY), lambda s: (0, jnp.maximum(s - 2, 0), 0, 0))
    shape = jax.ShapeDtypeStruct
    return pl.pallas_call(
        functools.partial(fdtd_kernel, nx, ny),
        name="fdtd",
        grid=(NZ + 2,),
        out_shape=(shape(e.shape, F32), shape(h.shape, F32), shape((CX, CY), F32)),
        in_specs=[
            incoming,
            incoming,
            pl.BlockSpec((1, CX, CY), lambda s: (jnp.minimum(s, NZ - 1), 0, 0)),
            whole(den),
            pl.BlockSpec(memory_space=pltpu.SMEM),
        ]
        + [whole(array) for array in halo],
        out_specs=(outgoing, outgoing, pl.BlockSpec((CX, CY), lambda s: (0, 0))),
        scratch_shapes=[
            pltpu.VMEM((3, NZ + 1, EX, CY), F32),
            pltpu.VMEM((3, NZ + 1, EX, CY), F32),
            pltpu.VMEM((NZ, EX, CY), F32),
            pltpu.VMEM((EX, CY), F32),
            pltpu.VMEM((EX, CY), F32),
            pltpu.VMEM((MATS + 1, EX, CY), F32),
            pltpu.VMEM((CX, CY), F32),
            pltpu.VMEM((CX, CY), F32),
            pltpu.VMEM((8, EX, 128), F32),
        ],
    )(e, h, mat, den, table, *halo)


def tiles_kernel(
    G, Zn,
    local, tile_map, out,
    rim_left, rim_right, rim_prev, rim_next, corner, cells, message, name_out, name_in, gathered, sums, passing, direct,
    combined, ready, landed,
    rim_send, rim_recv, name_send, name_recv, a_send, a_recv, b_send, b_recv, c_send, c_recv, heard,
):
    gx, gy = lax.axis_index("gx"), lax.axis_index("gy")
    nx, ny = Zn * G, 2 * G
    x, core = gy // 2, lax.rem(gy, 2)
    z, y = gx // G, lax.rem(gx, G)

    def dev(x, y, z, core):
        return (z * G + y, x * 2 + core)

    def signal(semaphore, device):
        pl.semaphore_signal(semaphore, inc=1, device_id=device, device_id_type=MESH)

    near = around(gx, gy, nx, ny)
    partners = list(near.values())
    for k in range(1, G):
        for c in range(2):
            partners.append(dev(wrapped(x, k, G), y, z, c))
            partners.append(dev(x, wrapped(y, k, G), z, c))
    partners.append(dev(x, y, z, 1 - core))
    above, below = wrapped(z, 1, Zn), wrapped(z, -1, Zn)
    for c in range(2):
        partners.append(dev(x, y, above, c))
        partners.append(dev(x, y, below, c))
    barrier = pltpu.get_barrier_semaphore()
    for device in partners:
        signal(barrier, device)
    names = jnp.zeros((8, 128), F32)
    lane8 = iota((8, 128), 1)
    for j in range(4):
        names = jnp.where(((lane8 == j) | (lane8 == 4 + j)), tile_map[0, j].astype(F32), names)
    name_out[...] = names
    pl.semaphore_wait(barrier, len(partners))

    rounds = Zn // 2 - 1

    def pass_word(i):
        if i < rounds:
            signal(heard.at[i], dev(x, y, above, core))
            signal(heard.at[i], dev(x, y, below, core))

    def hear_word(i):
        if i < rounds:
            pl.semaphore_wait(heard.at[i], 2)

    low, high, top, bottom = pl.ds(0, 128), pl.ds(128, 128), pl.ds(0, 8), pl.ds(CX - 8, 8)
    plan = (
        (local.at[bottom, high], corner.at[0], (1, 1)),
        (local.at[bottom, low], corner.at[1], (1, -1)),
        (local.at[top, high], corner.at[2], (-1, 1)),
        (local.at[top, low], corner.at[3], (-1, -1)),
        (local.at[bottom], rim_prev, (1, 0)),
        (local.at[top], rim_next, (-1, 0)),
        (local.at[:, high], rim_left, (0, 1)),
        (local.at[:, low], rim_right, (0, -1)),
    )
    rims = [remote(src, dst, rim_send.at[i], rim_recv.at[i], near[to]) for i, (src, dst, to) in enumerate(plan)]
    for copy in rims:
        copy.start()
    pass_word(0)

    targets = []
    for k in (2, 1, 3) if G == 4 else range(1, G):
        targets.append((0, 2 * k + core, dev(wrapped(x, k, G), y, z, 0)))
        targets.append((1, 2 * k + core, dev(x, wrapped(y, k, G), z, 1)))
    targets.append((1 - core, core, dev(x, y, z, 1 - core)))
    other = dev(x, y, z, 1 - core)
    slots = 2 * G
    name_copies = [
        remote(name_out, name_in.at[slot], name_send.at[i], name_recv.at[slot], to)
        for i, (_, slot, to) in enumerate(targets)
    ]
    for copy in name_copies:
        copy.start()
    name_in[core] = name_out[...]

    def each_slot(wait):
        wait(1 - core)
        for k in range(1, G):
            for c in range(2):
                wait(2 * k + c)

    each_slot(lambda slot: remote(name_out, name_in.at[slot], name_send.at[0], name_recv.at[slot], other).wait_recv())

    K = slots * 8
    P_rows = G * Zn * 2
    per = Zn * 2
    found = jnp.zeros((8, 128), F32)
    for slot in range(slots):
        part = name_in[slot]
        part = pltpu.roll(part, 8 * slot, 1) if slot else part
        found = jnp.where((lane8 >= 8 * slot) & (lane8 < 8 * slot + 8), part, found)
    shift = K
    while shift < 128:
        found = jnp.where(lane8 < shift, found, pltpu.roll(found, shift, 1))
        shift *= 2
    found = jnp.broadcast_to(found[0:1], (P_rows, 128))
    row = iota((P_rows, 128), 0)
    column = iota((P_rows, 128), 1)
    q = row // per
    place = lax.rem(row, per)
    fixed = (1 - core) * (x * 2) + core * (y * (2 * G))
    param = (place // 2) * (2 * G * G) + lax.rem(place, 2) + q * ((1 - core) * (2 * G) + core * 2) + fixed
    match = found == param.astype(F32)
    even_cells = lax.rem(column, 8) < 4
    both = jnp.concatenate(
        [jnp.where(match & even_cells, 1.0, 0.0), jnp.where(match & (~even_cells), 1.0, 0.0)], axis=0
    )
    half_k = jnp.where(iota((2 * P_rows, 128), 1) < max(0, 3 * K - 128), both, 0.0)
    chosen = jnp.concatenate([both, half_k], axis=1).astype(BF16) if K == 64 else jnp.where(
        iota((2 * P_rows, 128), 1) < 3 * K, both, 0.0
    ).astype(BF16)

    for copy in rims:
        copy.wait_recv()
    hear_word(0)
    pass_word(1)

    lane = iota((EX, 128), 1)
    sub = iota((8, 128), 0)
    wide = iota((8, CY), 0)
    has_prev, has_next = gx > 0, gx < nx - 1
    has_left, has_right = gy > 0, gy < ny - 1
    rows = jnp.where((wide < 4) & has_next, rim_next[...], jnp.where((wide >= 4) & has_prev, rim_prev[...], 0.0))
    main = jnp.concatenate([local[...], rows], axis=0)
    left = jnp.concatenate(
        [
            rim_left[...],
            jnp.where((sub < 4) & has_next, corner[2], jnp.where((sub >= 4) & has_prev, corner[0], 0.0)),
        ],
        axis=0,
    )
    left = jnp.where(has_left, left, 0.0)
    right = jnp.concatenate(
        [
            rim_right[...],
            jnp.where((sub < 4) & has_next, corner[3], jnp.where((sub >= 4) & has_prev, corner[1], 0.0)),
        ],
        axis=0,
    )
    right = jnp.where(has_right, right, 0.0)

    def along_x(f):
        return pltpu.roll(f, 1, 0) + 2.0 * f + pltpu.roll(f, EX - 1, 0)

    a, b = along_x(main[:, :128]), along_x(main[:, 128:])
    left, right = along_x(left), along_x(right)
    first, last = lane == 0, lane == 127
    ra, rb = pltpu.roll(a, 1, 1), pltpu.roll(b, 1, 1)
    la, lb = pltpu.roll(a, 127, 1), pltpu.roll(b, 127, 1)
    left, right = pltpu.roll(left, 1, 1), pltpu.roll(right, 127, 1)
    a = (jnp.where(first, left, ra) + 2.0 * a + jnp.where(last, lb, la)) / 16.0
    b = (jnp.where(first, ra, rb) + 2.0 * b + jnp.where(last, right, lb)) / 16.0
    cells[0] = a[:CX]
    cells[1] = b[:CX]

    narrow = iota((CX // 2, 128), 1) < TILE
    for j in range(4):
        even = cells[j // 2, pl.ds(0, CX // 2, stride=2), :]
        odd = cells[j // 2, pl.ds(1, CX // 2, stride=2), :]
        if j % 2:
            tile = jnp.where(narrow, pltpu.roll(even, TILE, 1), odd)
        else:
            tile = jnp.where(narrow, even, pltpu.roll(odd, TILE, 1))
        for h in range(2):
            message[h, pl.ds(j, 16, stride=4), :] = tile[16 * h : 16 * h + 16]

    chunk_rows = [pl.ds(32 * ch, 32) for ch in range(2)]
    first_stop = []
    for ch in range(2):
        for i, (h, slot, to) in enumerate(targets):
            copy = remote(
                message.at[h, chunk_rows[ch]], gathered.at[slot, chunk_rows[ch]], a_send.at[ch, i], a_recv.at[ch, slot], to
            )
            copy.start()
            first_stop.append(copy)
    gathered[core] = message[core]

    mine = (1 - core) * y + core * x

    def ring(k):
        there = wrapped(mine, k, G)
        return there, dev((1 - core) * x + core * there, (1 - core) * there + core * y, z, core)

    ahead, to_ahead = ring(1)
    behind, to_behind = ring(-1)
    across, _ = ring(2)
    second_stop = []
    for ch in range(2):
        each_slot(
            lambda slot: remote(
                message.at[0, chunk_rows[ch]], gathered.at[slot, chunk_rows[ch]], a_send.at[ch, 0], a_recv.at[ch, slot], other
            ).wait_recv()
        )
        for m in range(4 * ch, 4 * ch + 4):
            data = jnp.concatenate([gathered[slot, pl.ds(8 * m, 8)] for slot in range(slots)], axis=0)
            hi = data.astype(BF16)
            rest = data - hi.astype(F32)
            mid = rest.astype(BF16)
            lo = (rest - mid.astype(F32)).astype(BF16)
            picked = jnp.dot(chosen, jnp.concatenate([hi, mid, lo, hi], axis=0), preferred_element_type=F32)
            for parity in range(2):
                for place_q in range(G):
                    start = parity * P_rows + place_q * per
                    sums[ch, place_q, 2 * (m - 4 * ch) + parity] = picked[start : start + per]
        far, near_by = (to_ahead, to_behind) if ch == 0 else (to_behind, to_ahead)
        straight = behind if ch == 0 else ahead
        second_stop.append(remote(sums.at[ch, across], passing.at[ch], b_send.at[ch, 0], b_recv.at[ch, 0], far))
        second_stop.append(remote(sums.at[ch, straight], direct.at[ch], b_send.at[ch, 1], b_recv.at[ch, 1], near_by))
        second_stop[-2].start()
        second_stop[-1].start()
    hear_word(1)
    pass_word(2)
    for ch in range(2):
        far = to_ahead if ch == 0 else to_behind
        onward = ahead if ch == 0 else behind
        second_stop[2 * ch].wait_recv()
        passing[ch] = passing[ch] + sums[ch, onward]
        copy = remote(passing.at[ch], combined.at[ch], b_send.at[ch, 2], b_recv.at[ch, 2], far)
        copy.start()
        second_stop.append(copy)
    hear_word(2)

    third_stop = []
    for ch in range(2):
        second_stop[2 * ch + 1].wait_recv()
        second_stop[4 + ch].wait_recv()
        for b in range(8):
            value = sums[ch, mine, b] + direct[ch, b] + combined[ch, b]
            ready[ch, pl.ds(b, per, stride=8), :] = value
        eight = pl.ds(8 * ch, 8)
        order = sorted(range(Zn), key=lambda k: -min(k, Zn - k))
        for k in order:
            there = wrapped(z, k, Zn)
            for c in range(2):
                if k == 0 and c == 0:
                    continue
                target = c if k else 1 - core
                start = pl.multiple_of((there * 2 + target) * 8, 8)
                copy = remote(
                    ready.at[ch, pl.ds(start, 8)],
                    landed.at[2 * k + core, eight],
                    c_send.at[ch, 2 * k + c],
                    c_recv.at[ch, 2 * k + core],
                    dev(x, y, there, target),
                )
                copy.start()
                third_stop.append(copy)
        landed[core, eight] = ready[ch, pl.ds(pl.multiple_of((z * 2 + core) * 8, 8), 8)]

    for ch in range(2):
        eight = pl.ds(8 * ch, 8)

        def landing(slot):
            remote(
                ready.at[ch, pl.ds(0, 8)], landed.at[slot, eight], c_send.at[ch, 0], c_recv.at[ch, slot], other
            ).wait_recv()

        landing(1 - core)
        for k in range(1, Zn):
            for c in range(2):
                landing(2 * k + c)
        for h in range(2):
            value = landed[h, eight]
            for k in range(1, Zn):
                value = value + landed[2 * k + h, eight]
            out[pl.ds(16 * h + 8 * ch, 8)] = value
    for copy in rims + name_copies + first_stop + second_stop + third_stop:
        copy.wait_send()


def route_tiles(G, Zn, local, tile_map):
    per = Zn * 2
    dma = pltpu.SemaphoreType.DMA
    return pl.pallas_call(
        functools.partial(tiles_kernel, G, Zn),
        name="tiles",
        out_shape=jax.ShapeDtypeStruct((32, 128), F32),
        in_specs=[VMEM, pl.BlockSpec(memory_space=pltpu.SMEM)],
        out_specs=VMEM,
        scratch_shapes=[
            pltpu.VMEM((CX, 128), F32),
            pltpu.VMEM((CX, 128), F32),
            pltpu.VMEM((8, CY), F32),
            pltpu.VMEM((8, CY), F32),
            pltpu.VMEM((4, 8, 128), F32),
            pltpu.VMEM((2, CX, 128), F32),
            pltpu.VMEM((2, CX, 128), F32),
            pltpu.VMEM((8, 128), F32),
            pltpu.VMEM((2 * G, 8, 128), F32),
            pltpu.VMEM((2 * G, CX, 128), F32),
            pltpu.VMEM((2, G, 8, per, 128), F32),
            pltpu.VMEM((2, 8, per, 128), F32),
            pltpu.VMEM((2, 8, per, 128), F32),
            pltpu.VMEM((2, 8, per, 128), F32),
            pltpu.VMEM((2, per * 8, 128), F32),
            pltpu.VMEM((2 * Zn, 16, 128), F32),
            dma((8,)),
            dma((8,)),
            dma((2 * G,)),
            dma((2 * G,)),
            dma((2, 2 * G)),
            dma((2, 2 * G)),
            dma((2, 3)),
            dma((2, 3)),
            dma((2, 2 * Zn)),
            dma((2, 2 * Zn)),
            pltpu.SemaphoreType.REGULAR((3,)),
        ],
        compiler_params=pltpu.CompilerParams(collective_id=1, has_side_effects=True),
    )(local, tile_map)


def on_device(nx, ny, e_adj, h_adj, density, material, eps_table, dft_adj, dft_fwd, tile_map):
    G = ny // 2
    flat = lambda array: array.reshape(FREQ, 2, 3 * PLANES, CX, CY)
    halo = exchange(nx, ny, e_adj, h_adj, material, density, flat(dft_fwd), flat(dft_adj))
    e_out, h_out, local = fdtd(nx, ny, e_adj, h_adj, material, density, eps_table, halo)
    params = route_tiles(G, nx // G, local, tile_map)
    return e_out, h_out, params.reshape(1, TILE * TILE)


def solution(mesh):
    in_specs = (
        P(None, None, "gx", "gy"),
        P(None, None, "gx", "gy"),
        P("gx", "gy"),
        P(None, "gx", "gy"),
        P(),
        P(None, None, None, None, "gx", "gy"),
        P(None, None, None, None, "gx", "gy"),
        P("gx", "gy"),
    )
    out_specs = (P(None, None, "gx", "gy"), P(None, None, "gx", "gy"), P(("gx", "gy"), None))
    return jax.shard_map(
        functools.partial(on_device, mesh.shape["gx"], mesh.shape["gy"]),
        mesh=mesh,
        in_specs=in_specs,
        out_specs=out_specs,
        check_vma=False,
    )
```

```python
import functools
import math

import jax
import jax.numpy as jnp
from jax import lax
from jax.experimental import pallas as pl
from jax.experimental.pallas import tpu as pltpu
from jax.sharding import PartitionSpec as P

MESH = pl.DeviceIdType.MESH

PLANES = 2
ZLO = 3
STEPS = 2
FREQ = 4
PML = 12
MATS = 4
TILE = 64

courant = 0.5
sigma_peak = 0.8
dft_weight = 0.5
sharpness = 4.0
threshold = 0.5
eps_low = 2.1
eps_high = 12.1
grad_scale = 0.01

F32 = jnp.float32
BF16 = jnp.bfloat16
VMEM = pl.BlockSpec(memory_space=pltpu.VMEM)
ANY = pl.BlockSpec(memory_space=pl.ANY)

CX, CY, NZ = 64, 256, 8
EX = CX + 8
KINDS = 8
EDGE = 2
ZL = KINDS * EDGE


def iota(shape, dim):
    return lax.broadcasted_iota(jnp.int32, shape, dim)


def wrapped(index, shift, count):
    return lax.rem(index + (shift + count), count)


def around(gx, gy, nx, ny):
    places = {}
    for dx in (-1, 0, 1):
        for dy in (-1, 0, 1):
            if dx or dy:
                places[dx, dy] = (wrapped(gx, dx, nx), wrapped(gy, dy, ny))
    return places


def remote(src, dst, send, recv, device):
    return pltpu.make_async_remote_copy(
        src_ref=src, dst_ref=dst, send_sem=send, recv_sem=recv, device_id=device, device_id_type=MESH
    )


def profile(places, total):
    depth = jnp.maximum(jnp.maximum(PML - places, places - (total - 1 - PML)), 0.0) / PML
    return depth * depth * depth


DOWN_GROUPS = NZ + (NZ * 6 + 7) // 8
UP_GROUPS = NZ + (NZ * 3 + 7) // 8


def row_slot(down, kind, z):
    if kind < 3:
        return z, 2 * kind, 2
    if kind == 6:
        return z, 6, 1
    each = 2 if down else 1
    row = (3 * z + kind - 3) * each
    return NZ + row // 8, row % 8, each


def solve_kernel(
    G, Zn,
    e_hbm, h_hbm, mat_hbm, den_hbm, fwd_hbm, adj_hbm, table_ref, tile_map,
    e_out, h_out, out,
    E, H, CE, mat, den, fwd, adj, gain, inter, slope, damp, coef, own, got, halo_prev, halo_next, xdown, xup, xprev, xnext, strips,
    local, rim_left, rim_right, rim_prev, rim_next, corner, cells, message, name_out, name_in, gathered, sums, passing, direct,
    combined, ready, landed,
    load_sem, halo_send, halo_recv,
    rim_send, rim_recv, name_send, name_recv, a_send, a_recv, b_send, b_recv, c_send, c_recv, heard,
):
    gx, gy = lax.axis_index("gx"), lax.axis_index("gy")
    nx, ny = Zn * G, 2 * G
    x, core = gy // 2, lax.rem(gy, 2)
    z, y = gx // G, lax.rem(gx, G)
    has_prev, has_next = gx > 0, gx < nx - 1
    has_left, has_right = gy > 0, gy < ny - 1
    total_x, total_y = nx * CX, ny * CY

    def dev(x, y, z, core):
        return (z * G + y, x * 2 + core)

    def signal(semaphore, device):
        pl.semaphore_signal(semaphore, inc=1, device_id=device, device_id_type=MESH)

    near = around(gx, gy, nx, ny)
    partners = list(near.values())
    for k in range(1, G):
        for c in range(2):
            partners.append(dev(wrapped(x, k, G), y, z, c))
            partners.append(dev(x, wrapped(y, k, G), z, c))
    partners.append(dev(x, y, z, 1 - core))
    above, below = wrapped(z, 1, Zn), wrapped(z, -1, Zn)
    for c in range(2):
        partners.append(dev(x, y, above, c))
        partners.append(dev(x, y, below, c))
    barrier = pltpu.get_barrier_semaphore()
    for device in partners:
        signal(barrier, device)

    block = pl.ds(0, CX)
    loads = []

    def load(src, dst):
        copy = pltpu.make_async_copy(src, dst, load_sem.at[len(loads)])
        copy.start()
        loads.append(copy)
        return copy

    load_den = load(den_hbm, den)
    load_mat = load(mat_hbm, mat)
    load_planes = [
        (load(e_hbm.at[:, p], E.at[:, p, block]), load(h_hbm.at[:, p], H.at[:, p + 1, block])) for p in range(NZ)
    ]
    load_dft = [load(fwd_hbm, fwd), load(adj_hbm, adj)]

    names = jnp.zeros((8, 128), F32)
    lane8 = iota((8, 128), 1)
    for j in range(4):
        names = jnp.where(((lane8 == j) | (lane8 == 4 + j)), tile_map[0, j].astype(F32), names)
    name_out[...] = names

    lane64 = iota((CX, 128), 1)
    low, high, top, bottom = pl.ds(0, 128), pl.ds(128, 128), pl.ds(0, 8), pl.ds(CX - 8, 8)

    def plane(kind, p, rows, columns):
        if kind < 3:
            return E[kind, p, rows, columns]
        if kind < 6:
            return H[kind - 3, p + 1, rows, columns]
        if kind == 6:
            return mat[p, rows, columns].astype(F32)
        return den[rows, columns]

    load_den.wait()
    load_mat.wait()
    first = jnp.zeros((CX, 128), F32)
    last = jnp.zeros((CX, 128), F32)
    empty = jnp.zeros((8, CY), F32)
    for g in range(DOWN_GROUPS - 1, DOWN_GROUPS):
        xdown[g] = empty
    for g in range(UP_GROUPS):
        xup[g] = empty
    for p in range(NZ):
        for copy in load_planes[p]:
            copy.wait()
        kinds = list(range(7)) + ([7] if ZLO <= p < ZLO + PLANES else [])
        for kind in kinds:
            at = p * ZL + EDGE * kind
            mine = (lane64 >= at) & (lane64 < at + EDGE)
            a = plane(kind, p, block, low)
            b = plane(kind, p, block, high)
            first = jnp.where(mine, pltpu.roll(a, at, 1) if at else a, first)
            last = jnp.where(mine, pltpu.roll(b, at + EDGE, 1) if at + EDGE < 128 else b, last)
        for kind in range(7):
            g, row, n = row_slot(True, kind, p)
            xdown[g, pl.ds(row, n)] = plane(kind, p, pl.ds(CX - n, n), pl.ds(0, CY))
            g, row, n = row_slot(False, kind, p)
            xup[g, pl.ds(row, n)] = plane(kind, p, pl.ds(0, n), pl.ds(0, CY))
        xdown[p, pl.ds(7, 1)] = den[pl.ds(CX - 2 + p % 2, 1), :]
        xup[p, pl.ds(7, 1)] = den[pl.ds(p % 2, 1), :]
    own[0] = first
    own[1] = last

    pl.semaphore_wait(barrier, len(partners))

    rounds = Zn // 2 - 1

    def pass_word(i):
        if i < rounds:
            signal(heard.at[i], dev(x, y, above, core))
            signal(heard.at[i], dev(x, y, below, core))

    def hear_word(i):
        if i < rounds:
            pl.semaphore_wait(heard.at[i], 2)

    plan = (
        (xdown, xprev, (1, 0)),
        (xup, xnext, (-1, 0)),
        (own.at[1], got.at[0], (0, 1)),
        (own.at[0], got.at[1], (0, -1)),
        (own.at[:, bottom], halo_prev.at[pl.ds(1, 2)], (1, 0)),
        (own.at[:, top], halo_next.at[pl.ds(1, 2)], (-1, 0)),
        (own.at[1, bottom], halo_prev.at[0], (1, 1)),
        (own.at[0, bottom], halo_prev.at[3], (1, -1)),
        (own.at[1, top], halo_next.at[0], (-1, 1)),
        (own.at[0, top], halo_next.at[3], (-1, -1)),
    )
    halos = [remote(src, dst, halo_send.at[i], halo_recv.at[i], near[to]) for i, (src, dst, to) in enumerate(plan)]
    for copy in halos:
        copy.start()
    pass_word(0)

    targets = []
    for k in (2, 1, 3) if G == 4 else range(1, G):
        targets.append((0, 2 * k + core, dev(wrapped(x, k, G), y, z, 0)))
        targets.append((1, 2 * k + core, dev(x, wrapped(y, k, G), z, 1)))
    targets.append((1 - core, core, dev(x, y, z, 1 - core)))
    other = dev(x, y, z, 1 - core)
    slots = 2 * G
    name_copies = [
        remote(name_out, name_in.at[slot], name_send.at[i], name_recv.at[slot], to)
        for i, (_, slot, to) in enumerate(targets)
    ]
    for copy in name_copies:
        copy.start()
    name_in[core] = name_out[...]

    def each_slot(wait):
        wait(1 - core)
        for k in range(1, G):
            for c in range(2):
                wait(2 * k + c)

    for copy in load_dft:
        copy.wait()
    cosines = [[dft_weight * math.cos((0.21 + 0.06 * f) * (n + 1)) for f in range(FREQ)] for n in range(STEPS)]
    sines = [[dft_weight * math.sin((0.21 + 0.06 * f) * (n + 1)) for f in range(FREQ)] for n in range(STEPS)]

    def chunk(r, _):
        rows = pl.ds(pl.multiple_of(r * 16, 16), 16)

        def entry(k, acc):
            one = jnp.zeros((16, CY), F32)
            two = jnp.zeros((16, CY), F32)
            for f in range(FREQ):
                re = fwd[f, 0, k, rows].astype(F32)
                im = fwd[f, 1, k, rows].astype(F32)
                acc = acc + (re * adj[f, 0, k, rows] - im * adj[f, 1, k, rows])
                one = one + (cosines[0][f] * re + sines[0][f] * im)
                two = two + (cosines[1][f] * re + sines[1][f] * im)
            gain[k, 0, rows] = one
            gain[k, 1, rows] = two
            return acc

        inter[rows] = lax.fori_loop(0, 3 * PLANES, entry, jnp.zeros((16, CY), F32))
        return 0

    lax.fori_loop(0, CX // 16, chunk, 0)

    lane = iota((EX, 128), 1)
    slot_of = lax.rem(lane, ZL)
    half_sum_scale = math.tanh(sharpness * threshold) + math.tanh(sharpness * (1.0 - threshold))

    def places(columns, width):
        rows = iota((EX, width), 0)
        rows = gx * CX + jnp.where(rows < CX + 4, rows, rows - EX)
        inside = (rows >= 0) & (rows < total_x) & (columns >= 0) & (columns < total_y)
        sigma = sigma_peak * (profile(rows.astype(F32), total_x) + profile(columns.astype(F32), total_y))
        part = jnp.where(inside, 1.0 / (1.0 + 0.5 * sigma), 0.0)
        return (1.0 - 0.5 * sigma) * part, courant * part

    damping, coef_h = places(gy * CY + iota((EX, CY), 1), CY)
    damp[...] = damping
    coef[...] = coef_h
    columns = gy * CY + jnp.where(slot_of < 4, slot_of - EDGE, slot_of + (CY - EDGE - 4))
    damp_s, ch_s = places(columns, 128)
    damp_s = jnp.where(slot_of < 8, damp_s, 0.0)
    ch_s = jnp.where(slot_of < 8, ch_s, 0.0)
    inverse = [1.0 / jnp.full((1, 128), table_ref[k], F32) for k in range(MATS)]

    each_slot(lambda slot: remote(name_out, name_in.at[slot], name_send.at[0], name_recv.at[slot], other).wait_recv())
    K = slots * 8
    P_rows = G * Zn * 2
    per = Zn * 2
    found = jnp.zeros((8, 128), F32)
    for slot in range(slots):
        part = name_in[slot]
        part = pltpu.roll(part, 8 * slot, 1) if slot else part
        found = jnp.where((lane8 >= 8 * slot) & (lane8 < 8 * slot + 8), part, found)
    shift = K
    while shift < 128:
        found = jnp.where(lane8 < shift, found, pltpu.roll(found, shift, 1))
        shift *= 2
    found = jnp.broadcast_to(found[0:1], (P_rows, 128))
    row = iota((P_rows, 128), 0)
    column = iota((P_rows, 128), 1)
    q = row // per
    place = lax.rem(row, per)
    fixed = (1 - core) * (x * 2) + core * (y * (2 * G))
    param = (place // 2) * (2 * G * G) + lax.rem(place, 2) + q * ((1 - core) * (2 * G) + core * 2) + fixed
    match = found == param.astype(F32)
    even_cells = lax.rem(column, 8) < 4
    both = jnp.concatenate(
        [jnp.where(match & even_cells, 1.0, 0.0), jnp.where(match & (~even_cells), 1.0, 0.0)], axis=0
    )
    if K == 64:
        third = jnp.where(iota((2 * P_rows, 128), 1) < 3 * K - 128, both, 0.0)
        chosen = jnp.concatenate([both, third], axis=1).astype(BF16)
    else:
        chosen = jnp.where(iota((2 * P_rows, 128), 1) < 3 * K, both, 0.0).astype(BF16)
    hear_word(0)
    pass_word(1)

    for copy in halos:
        copy.wait_recv()

    def xn(f):
        return pltpu.roll(f, EX - 1, 0)

    def xp(f):
        return pltpu.roll(f, 1, 0)

    def yn(f, strip, p):
        a, b = pltpu.roll(f[:, :128], 127, 1), pltpu.roll(f[:, 128:], 127, 1)
        edge = pltpu.roll(strip, (127 - 6 - p * ZL) % 128, 1)
        end = lane == 127
        return jnp.concatenate([jnp.where(end, b, a), jnp.where(end, edge, b)], axis=1)

    def yp(f, strip, p):
        a, b = pltpu.roll(f[:, :128], 1, 1), pltpu.roll(f[:, 128:], 1, 1)
        edge = pltpu.roll(strip, (127 - p * ZL) % 128, 1)
        start = lane == 0
        return jnp.concatenate([jnp.where(start, edge, a), jnp.where(start, a, b)], axis=1)

    wide = iota((8, CY), 0)
    narrow8 = iota((8, 128), 0)
    from_next, from_prev = (wide < 2) & has_next, (wide >= 6) & has_prev

    def x_halo(kind, p):
        if kind == 7:
            first_row, second_row = xnext[0], xnext[1]
            ahead = jnp.where(wide == 0, pltpu.roll(first_row, 1, 0), pltpu.roll(second_row, 2, 0))
            behind = jnp.where(wide == 6, pltpu.roll(xprev[0], 7, 0), xprev[1])
        else:
            g, at, _ = row_slot(False, kind, p)
            ahead = pltpu.roll(xnext[g], (8 - at) % 8, 0) if at else xnext[g]
            g, at, n = row_slot(True, kind, p)
            shift = (8 - n - at) % 8
            behind = pltpu.roll(xprev[g], shift, 0) if shift else xprev[g]
        return jnp.where(from_next, ahead, jnp.where(from_prev, behind, 0.0))

    halo_rows = pl.ds(CX, 8)
    for c in range(3):
        E[c, NZ] = jnp.zeros((EX, CY), F32)
        H[c, 0] = jnp.zeros((EX, CY), F32)
        for p in range(NZ):
            E[c, p, halo_rows] = x_halo(c, p)
            H[c, p + 1, halo_rows] = x_halo(3 + c, p)

    pieces = []
    for i, body in enumerate((got[0], own[0], own[1], got[1])):
        rim = jnp.where((narrow8 < 4) & has_next, halo_next[i], jnp.where((narrow8 >= 4) & has_prev, halo_prev[i], 0.0))
        piece = jnp.concatenate([body, rim], axis=0)
        if i == 0:
            piece = jnp.where(has_left, piece, 0.0)
        if i == 3:
            piece = jnp.where(has_right, piece, 0.0)
        pieces.append(piece)

    def strip(kind):
        value = jnp.zeros((EX, 128), F32)
        for i, piece in enumerate(pieces):
            shift = (EDGE * i - EDGE * kind) % 128
            moved = pltpu.roll(piece, shift, 1) if shift else piece
            value = jnp.where((slot_of >= EDGE * i) & (slot_of < EDGE * (i + 1)), moved, value)
        return value

    def design(filtered):
        bend = jnp.tanh(sharpness * (filtered - threshold))
        projected = (math.tanh(sharpness * threshold) + bend) / half_sum_scale
        return bend, eps_low + (eps_high - eps_low) * projected

    dens = jnp.concatenate([den[...], x_halo(7, 0)], axis=0)
    dens_s = strip(7)
    dens = xp(dens) + 2.0 * dens + xn(dens)
    dens_s = xp(dens_s) + 2.0 * dens_s + xn(dens_s)
    bend, eps = design((yp(dens, dens_s, ZLO) + 2.0 * dens + yn(dens, dens_s, ZLO)) / 16.0)
    slope[...] = (sharpness * (1.0 - bend * bend) / half_sum_scale)[:CX]
    design_coef = coef[...] / eps
    for p in range(NZ):
        if ZLO <= p < ZLO + PLANES:
            CE[p] = design_coef
        else:
            mats = jnp.concatenate([mat[p].astype(F32), x_halo(6, p)], axis=0)
            part = jnp.broadcast_to(inverse[MATS - 1][:, :1], (EX, CY))
            for k in range(MATS - 1):
                part = jnp.where(mats == float(k), inverse[k][:, :1], part)
            CE[p] = coef[...] * part
    eps_s = design((pltpu.roll(dens_s, 1, 1) + 2.0 * dens_s + pltpu.roll(dens_s, 127, 1)) / 16.0)[1]
    mats = strip(6)
    part = jnp.broadcast_to(inverse[MATS - 1], (EX, 128))
    for k in range(MATS - 1):
        part = jnp.where(mats == float(k), inverse[k], part)
    layer = (lane >= ZLO * ZL) & (lane < (ZLO + PLANES) * ZL)
    ce_s = ch_s * jnp.where(layer, 1.0 / eps_s, part)

    def yns(f):
        return pltpu.roll(f, 127, 1)

    def yps(f):
        return pltpu.roll(f, 1, 1)

    def zns(f):
        return jnp.where(lane < 128 - ZL, pltpu.roll(f, 128 - ZL, 1), 0.0)

    def zps(f):
        return jnp.where(lane >= ZL, pltpu.roll(f, ZL, 1), 0.0)

    def strip_h(ex, ey, ez, hx, hy, hz):
        cx = (yns(ez) - ez) - (zns(ey) - ey)
        cy = (zns(ex) - ex) - (xn(ez) - ez)
        cz = (xn(ey) - ey) - (yns(ex) - ex)
        return damp_s * hx - ch_s * cx, damp_s * hy - ch_s * cy, damp_s * hz - ch_s * cz

    def strip_e(ex, ey, ez, hx, hy, hz):
        cx = (hz - yps(hz)) - (hy - zps(hy))
        cy = (hx - zps(hx)) - (hz - xp(hz))
        cz = (hy - xp(hy)) - (hx - yps(hx))
        return damp_s * ex + ce_s * cx, damp_s * ey + ce_s * cy, damp_s * ez + ce_s * cz

    es = tuple(strip(c) for c in range(3))
    hs = tuple(strip(c) for c in range(3, 6))
    strips[0], strips[1] = es[0], es[2]
    hs = strip_h(*es, *hs)
    strips[2], strips[3] = hs[0], hs[2]
    es = strip_e(*es, *hs)
    strips[4], strips[5] = es[0], es[2]
    hs = strip_h(*es, *hs)
    strips[6], strips[7] = hs[0], hs[2]

    def half_h(p, n):
        ex, ey, ez = E[0, p], E[1, p], E[2, p]
        d, c = damp[...], coef[...]
        hx = d * H[0, p + 1] - c * ((yn(ez, strips[4 * n + 1], p) - ez) - (E[1, p + 1] - ey))
        hy = d * H[1, p + 1] - c * ((E[0, p + 1] - ex) - (xn(ez) - ez))
        hz = d * H[2, p + 1] - c * ((xn(ey) - ey) - (yn(ex, strips[4 * n], p) - ex))
        for i, value in enumerate((hx, hy, hz)):
            H[i, p + 1] = value
            if n:
                h_out[i, p] = value[:CX]

    def half_e(p, n):
        hx, hy, hz = H[0, p + 1], H[1, p + 1], H[2, p + 1]
        d, c = damp[...], CE[p]
        ex = d * E[0, p] + c * ((hz - yp(hz, strips[4 * n + 3], p)) - (hy - H[1, p]))
        ey = d * E[1, p] + c * ((hx - H[0, p]) - (hz - xp(hz)))
        ez = d * E[2, p] + c * ((hy - xp(hy)) - (hx - yp(hx, strips[4 * n + 2], p)))
        acc = inter[...]
        for i, value in enumerate((ex, ey, ez)):
            if n:
                e_out[i, p] = value[:CX]
            else:
                E[i, p] = value
            if ZLO <= p < ZLO + PLANES:
                acc = acc + gain[PLANES * i + (p - ZLO), n] * value[:CX]
        if ZLO <= p < ZLO + PLANES:
            inter[...] = acc

    before, behind_layer = ZLO - 2, ZLO + PLANES
    for p in range(before, behind_layer + 1):
        half_h(p, 0)
        if p > before:
            half_e(p, 0)
        if p > before + 1:
            half_h(p - 1, 1)
        if p > before + 2:
            half_e(p - 1, 1)
    local[...] = grad_scale * (eps_high - eps_low) * slope[...] * inter[...]

    plan = (
        (local.at[bottom, high], corner.at[0], (1, 1)),
        (local.at[bottom, low], corner.at[1], (1, -1)),
        (local.at[top, high], corner.at[2], (-1, 1)),
        (local.at[top, low], corner.at[3], (-1, -1)),
        (local.at[bottom], rim_prev, (1, 0)),
        (local.at[top], rim_next, (-1, 0)),
        (local.at[:, high], rim_left, (0, 1)),
        (local.at[:, low], rim_right, (0, -1)),
    )
    rims = [remote(src, dst, rim_send.at[i], rim_recv.at[i], near[to]) for i, (src, dst, to) in enumerate(plan)]
    for copy in rims:
        copy.start()

    for p in range(behind_layer + 1, NZ + 1):
        if p < NZ:
            half_h(p, 0)
            half_e(p, 0)
        half_h(p - 1, 1)
        half_e(p - 1, 1)

    for copy in rims:
        copy.wait_recv()
    hear_word(1)
    pass_word(2)

    rows = jnp.where((wide < 4) & has_next, rim_next[...], jnp.where((wide >= 4) & has_prev, rim_prev[...], 0.0))
    main = jnp.concatenate([local[...], rows], axis=0)
    left = jnp.concatenate(
        [
            rim_left[...],
            jnp.where((narrow8 < 4) & has_next, corner[2], jnp.where((narrow8 >= 4) & has_prev, corner[0], 0.0)),
        ],
        axis=0,
    )
    left = jnp.where(has_left, left, 0.0)
    right = jnp.concatenate(
        [
            rim_right[...],
            jnp.where((narrow8 < 4) & has_next, corner[3], jnp.where((narrow8 >= 4) & has_prev, corner[1], 0.0)),
        ],
        axis=0,
    )
    right = jnp.where(has_right, right, 0.0)

    def along_x(f):
        return pltpu.roll(f, 1, 0) + 2.0 * f + pltpu.roll(f, EX - 1, 0)

    a, b = along_x(main[:, :128]), along_x(main[:, 128:])
    left, right = along_x(left), along_x(right)
    first, last = lane == 0, lane == 127
    ra, rb = pltpu.roll(a, 1, 1), pltpu.roll(b, 1, 1)
    la, lb = pltpu.roll(a, 127, 1), pltpu.roll(b, 127, 1)
    left, right = pltpu.roll(left, 1, 1), pltpu.roll(right, 127, 1)
    a = (jnp.where(first, left, ra) + 2.0 * a + jnp.where(last, lb, la)) / 16.0
    b = (jnp.where(first, ra, rb) + 2.0 * b + jnp.where(last, right, lb)) / 16.0
    cells[0] = a[:CX]
    cells[1] = b[:CX]

    narrow = iota((CX // 2, 128), 1) < TILE
    for j in range(4):
        even = cells[j // 2, pl.ds(0, CX // 2, stride=2), :]
        odd = cells[j // 2, pl.ds(1, CX // 2, stride=2), :]
        if j % 2:
            tile = jnp.where(narrow, pltpu.roll(even, TILE, 1), odd)
        else:
            tile = jnp.where(narrow, even, pltpu.roll(odd, TILE, 1))
        for h in range(2):
            message[h, pl.ds(j, 16, stride=4), :] = tile[16 * h : 16 * h + 16]

    chunk_rows = [pl.ds(32 * ch, 32) for ch in range(2)]
    first_stop = []
    for ch in range(2):
        for i, (h, slot, to) in enumerate(targets):
            copy = remote(
                message.at[h, chunk_rows[ch]], gathered.at[slot, chunk_rows[ch]], a_send.at[ch, i], a_recv.at[ch, slot], to
            )
            copy.start()
            first_stop.append(copy)
    gathered[core] = message[core]

    for p in range(before):
        half_h(p, 0)
    for p in range(before + 1):
        half_e(p, 0)
    for p in range(before + 1):
        half_h(p, 1)
    for p in range(before + 2):
        half_e(p, 1)

    mine = (1 - core) * y + core * x

    def ring(k):
        there = wrapped(mine, k, G)
        return there, dev((1 - core) * x + core * there, (1 - core) * there + core * y, z, core)

    ahead, to_ahead = ring(1)
    behind, to_behind = ring(-1)
    across, _ = ring(2)
    second_stop = []
    for ch in range(2):
        each_slot(
            lambda slot: remote(
                message.at[0, chunk_rows[ch]], gathered.at[slot, chunk_rows[ch]], a_send.at[ch, 0], a_recv.at[ch, slot], other
            ).wait_recv()
        )
        for m in range(4 * ch, 4 * ch + 4):
            data = jnp.concatenate([gathered[slot, pl.ds(8 * m, 8)] for slot in range(slots)], axis=0)
            hi = data.astype(BF16)
            rest = data - hi.astype(F32)
            mid = rest.astype(BF16)
            lo = (rest - mid.astype(F32)).astype(BF16)
            picked = jnp.dot(chosen, jnp.concatenate([hi, mid, lo, hi], axis=0), preferred_element_type=F32)
            for parity in range(2):
                for place_q in range(G):
                    start = parity * P_rows + place_q * per
                    sums[ch, place_q, 2 * (m - 4 * ch) + parity] = picked[start : start + per]
        far, near_by = (to_ahead, to_behind) if ch == 0 else (to_behind, to_ahead)
        straight = behind if ch == 0 else ahead
        second_stop.append(remote(sums.at[ch, across], passing.at[ch], b_send.at[ch, 0], b_recv.at[ch, 0], far))
        second_stop.append(remote(sums.at[ch, straight], direct.at[ch], b_send.at[ch, 1], b_recv.at[ch, 1], near_by))
        second_stop[-2].start()
        second_stop[-1].start()
    for ch in range(2):
        far = to_ahead if ch == 0 else to_behind
        onward = ahead if ch == 0 else behind
        second_stop[2 * ch].wait_recv()
        passing[ch] = passing[ch] + sums[ch, onward]
        copy = remote(passing.at[ch], combined.at[ch], b_send.at[ch, 2], b_recv.at[ch, 2], far)
        copy.start()
        second_stop.append(copy)
    hear_word(2)

    third_stop = []
    for ch in range(2):
        second_stop[2 * ch + 1].wait_recv()
        second_stop[4 + ch].wait_recv()
        for b in range(8):
            value = sums[ch, mine, b] + direct[ch, b] + combined[ch, b]
            ready[ch, pl.ds(b, per, stride=8), :] = value
        eight = pl.ds(8 * ch, 8)
        order = sorted(range(Zn), key=lambda k: -min(k, Zn - k))
        for k in order:
            there = wrapped(z, k, Zn)
            for c in range(2):
                if k == 0 and c == 0:
                    continue
                target = c if k else 1 - core
                start = pl.multiple_of((there * 2 + target) * 8, 8)
                copy = remote(
                    ready.at[ch, pl.ds(start, 8)],
                    landed.at[2 * k + core, eight],
                    c_send.at[ch, 2 * k + c],
                    c_recv.at[ch, 2 * k + core],
                    dev(x, y, there, target),
                )
                copy.start()
                third_stop.append(copy)
        landed[core, eight] = ready[ch, pl.ds(pl.multiple_of((z * 2 + core) * 8, 8), 8)]

    for ch in range(2):
        eight = pl.ds(8 * ch, 8)

        def landing(slot):
            remote(
                ready.at[ch, pl.ds(0, 8)], landed.at[slot, eight], c_send.at[ch, 0], c_recv.at[ch, slot], other
            ).wait_recv()

        landing(1 - core)
        for k in range(1, Zn):
            for c in range(2):
                landing(2 * k + c)
        for h in range(2):
            value = landed[h, eight]
            for k in range(1, Zn):
                value = value + landed[2 * k + h, eight]
            out[pl.ds(16 * h + 8 * ch, 8)] = value
    for copy in halos + rims + name_copies + first_stop + second_stop + third_stop:
        copy.wait_send()


def solve(G, Zn, e, h, mat, den, fwd, adj, table, tile_map):
    per = Zn * 2
    dma = pltpu.SemaphoreType.DMA
    vmem = lambda *shape: pltpu.VMEM(shape, F32)
    smem = pl.BlockSpec(memory_space=pltpu.SMEM)
    return pl.pallas_call(
        functools.partial(solve_kernel, G, Zn),
        name="solve",
        out_shape=(pltpu.VMEM(e.shape, F32), pltpu.VMEM(h.shape, F32), pltpu.VMEM((32, 128), F32)),
        in_specs=[ANY] * 6 + [smem, smem],
        out_specs=(VMEM, VMEM, VMEM),
        scratch_shapes=[
            vmem(3, NZ + 1, EX, CY),
            vmem(3, NZ + 1, EX, CY),
            vmem(NZ, EX, CY),
            pltpu.VMEM(mat.shape, jnp.int32),
            vmem(CX, CY),
            pltpu.VMEM(fwd.shape, BF16),
            pltpu.VMEM(adj.shape, F32),
            vmem(3 * PLANES, STEPS, CX, CY),
            vmem(CX, CY),
            vmem(CX, CY),
            vmem(EX, CY),
            vmem(EX, CY),
            vmem(2, CX, 128),
            vmem(2, CX, 128),
            vmem(4, 8, 128),
            vmem(4, 8, 128),
            vmem(DOWN_GROUPS, 8, CY),
            vmem(UP_GROUPS, 8, CY),
            vmem(DOWN_GROUPS, 8, CY),
            vmem(UP_GROUPS, 8, CY),
            vmem(8, EX, 128),
            vmem(CX, CY),
            vmem(CX, 128),
            vmem(CX, 128),
            vmem(8, CY),
            vmem(8, CY),
            vmem(4, 8, 128),
            vmem(2, CX, 128),
            vmem(2, CX, 128),
            vmem(8, 128),
            vmem(2 * G, 8, 128),
            vmem(2 * G, CX, 128),
            vmem(2, G, 8, per, 128),
            vmem(2, 8, per, 128),
            vmem(2, 8, per, 128),
            vmem(2, 8, per, 128),
            vmem(2, per * 8, 128),
            vmem(2 * Zn, 16, 128),
            dma((2 * NZ + 4,)),
            dma((10,)),
            dma((10,)),
            dma((8,)),
            dma((8,)),
            dma((2 * G,)),
            dma((2 * G,)),
            dma((2, 2 * G)),
            dma((2, 2 * G)),
            dma((2, 3)),
            dma((2, 3)),
            dma((2, 2 * Zn)),
            dma((2, 2 * Zn)),
            pltpu.SemaphoreType.REGULAR((3,)),
        ],
        compiler_params=pltpu.CompilerParams(collective_id=0, has_side_effects=True),
    )(e, h, mat, den, fwd, adj, table, tile_map)


def on_device(nx, ny, e_adj, h_adj, density, material, eps_table, dft_adj, dft_fwd, tile_map):
    G = ny // 2
    flat = lambda array: array.reshape(FREQ, 2, 3 * PLANES, CX, CY)
    e_out, h_out, params = solve(
        G, nx // G, e_adj, h_adj, material, density, flat(dft_fwd), flat(dft_adj), eps_table, tile_map
    )
    return e_out, h_out, params.reshape(1, TILE * TILE)


def solution(mesh):
    in_specs = (
        P(None, None, "gx", "gy"),
        P(None, None, "gx", "gy"),
        P("gx", "gy"),
        P(None, "gx", "gy"),
        P(),
        P(None, None, None, None, "gx", "gy"),
        P(None, None, None, None, "gx", "gy"),
        P("gx", "gy"),
    )
    out_specs = (P(None, None, "gx", "gy"), P(None, None, "gx", "gy"), P(("gx", "gy"), None))
    return jax.shard_map(
        functools.partial(on_device, mesh.shape["gx"], mesh.shape["gy"]),
        mesh=mesh,
        in_specs=in_specs,
        out_specs=out_specs,
        check_vma=False,
    )
```

```python
import functools
import math

import jax
import jax.numpy as jnp
from jax import lax
from jax.experimental import pallas as pl
from jax.experimental.pallas import tpu as pltpu
from jax.sharding import PartitionSpec as P

MESH = pl.DeviceIdType.MESH

PLANES = 2
ZLO = 3
STEPS = 2
FREQ = 4
PML = 12
MATS = 4
TILE = 64

courant = 0.5
sigma_peak = 0.8
dft_weight = 0.5
sharpness = 4.0
threshold = 0.5
eps_low = 2.1
eps_high = 12.1
grad_scale = 0.01

F32 = jnp.float32
BF16 = jnp.bfloat16
VMEM = pl.BlockSpec(memory_space=pltpu.VMEM)
ANY = pl.BlockSpec(memory_space=pl.ANY)

CX, CY, NZ = 64, 256, 8
EX = CX + 8
KINDS = 8
EDGE = 2
ZL = KINDS * EDGE


def iota(shape, dim):
    return lax.broadcasted_iota(jnp.int32, shape, dim)


def wrapped(index, shift, count):
    return lax.rem(index + (shift + count), count)


def around(gx, gy, nx, ny):
    places = {}
    for dx in (-1, 0, 1):
        for dy in (-1, 0, 1):
            if dx or dy:
                places[dx, dy] = (wrapped(gx, dx, nx), wrapped(gy, dy, ny))
    return places


def remote(src, dst, send, recv, device):
    return pltpu.make_async_remote_copy(
        src_ref=src, dst_ref=dst, send_sem=send, recv_sem=recv, device_id=device, device_id_type=MESH
    )


def profile(places, total):
    depth = jnp.maximum(jnp.maximum(PML - places, places - (total - 1 - PML)), 0.0) / PML
    return depth * depth * depth


ORDER = (1, 2, 3, 4, 5, 6, 0, 7)
EARLY = 6
DOWN_EARLY, DOWN_GROUPS = 11, 15
UP_EARLY, UP_GROUPS = 9, 12


def row_slot(down, kind, z):
    at = ORDER.index(z)
    early = DOWN_EARLY if down else UP_EARLY
    start, at, count = (0, at, EARLY) if at < EARLY else (early, at - EARLY, NZ - EARLY)
    if kind < 3:
        return start + at, 2 * kind, 2
    if kind == 6:
        return start + at, 6, 1
    each = 2 if down else 1
    row = (3 * at + kind - 3) * each
    return start + count + row // 8, row % 8, each


def solve_kernel(
    G, Zn,
    e_hbm, h_hbm, mat_hbm, den_hbm, fwd_hbm, adj_hbm, table_hbm, map_hbm,
    e_out, h_out, out,
    table_ref, tile_map, E, H, CE, mat, den, fwd, adj, gain, inter, slope, damp, coef, own, got, halo_prev, halo_next, xdown, xup, xprev, xnext, strips,
    local, rim_left, rim_right, rim_prev, rim_next, corner, cells, message, name_out, name_in, gathered, sums, passing, direct,
    combined, ready, landed,
    load_sem, halo_send, halo_recv,
    rim_send, rim_recv, name_send, name_recv, a_send, a_recv, b_send, b_recv, c_send, c_recv, heard,
):
    gx, gy = lax.axis_index("gx"), lax.axis_index("gy")
    nx, ny = Zn * G, 2 * G
    x, core = gy // 2, lax.rem(gy, 2)
    z, y = gx // G, lax.rem(gx, G)
    has_prev, has_next = gx > 0, gx < nx - 1
    has_left, has_right = gy > 0, gy < ny - 1
    total_x, total_y = nx * CX, ny * CY

    def dev(x, y, z, core):
        return (z * G + y, x * 2 + core)

    def signal(semaphore, device):
        pl.semaphore_signal(semaphore, inc=1, device_id=device, device_id_type=MESH)

    near = around(gx, gy, nx, ny)
    partners = list(near.values())
    for k in range(1, G):
        for c in range(2):
            partners.append(dev(wrapped(x, k, G), y, z, c))
            partners.append(dev(x, wrapped(y, k, G), z, c))
    partners.append(dev(x, y, z, 1 - core))
    above, below = wrapped(z, 1, Zn), wrapped(z, -1, Zn)
    for c in range(2):
        partners.append(dev(x, y, above, c))
        partners.append(dev(x, y, below, c))
    block = pl.ds(0, CX)
    loads = []

    def load(src, dst):
        copy = pltpu.make_async_copy(src, dst, load_sem.at[len(loads)])
        copy.start()
        loads.append(copy)
        return copy

    load_den = load(den_hbm, den)
    load_small = [load(map_hbm, tile_map), load(table_hbm, table_ref)]
    load_planes = {
        p: (
            load(e_hbm.at[:, p], E.at[:, p, block]),
            load(h_hbm.at[:, p], H.at[:, p + 1, block]),
            load(mat_hbm.at[p], mat.at[p]),
        )
        for p in ORDER
    }

    barrier = pltpu.get_barrier_semaphore()
    for device in partners:
        signal(barrier, device)

    lane64 = iota((CX, 128), 1)
    lane8 = iota((8, 128), 1)
    low, high, top, bottom = pl.ds(0, 128), pl.ds(128, 128), pl.ds(0, 8), pl.ds(CX - 8, 8)

    def plane(kind, p, rows, columns):
        if kind < 3:
            return E[kind, p, rows, columns]
        if kind < 6:
            return H[kind - 3, p + 1, rows, columns]
        if kind == 6:
            return mat[p, rows, columns].astype(F32)
        return den[rows, columns]

    load_den.wait()
    first = jnp.zeros((CX, 128), F32)
    last = jnp.zeros((CX, 128), F32)
    empty = jnp.zeros((8, CY), F32)
    for g in range(DOWN_GROUPS):
        xdown[g] = empty
    for g in range(UP_GROUPS):
        xup[g] = empty
    for p in ORDER:
        for copy in load_planes[p]:
            copy.wait()
        kinds = list(range(7)) + ([7] if ZLO <= p < ZLO + PLANES else [])
        for kind in kinds:
            at = p * ZL + EDGE * kind
            mine = (lane64 >= at) & (lane64 < at + EDGE)
            a = plane(kind, p, block, low)
            b = plane(kind, p, block, high)
            first = jnp.where(mine, pltpu.roll(a, at, 1) if at else a, first)
            last = jnp.where(mine, pltpu.roll(b, at + EDGE, 1) if at + EDGE < 128 else b, last)
        for kind in range(7):
            g, row, n = row_slot(True, kind, p)
            xdown[g, pl.ds(row, n)] = plane(kind, p, pl.ds(CX - n, n), pl.ds(0, CY))
            g, row, n = row_slot(False, kind, p)
            xup[g, pl.ds(row, n)] = plane(kind, p, pl.ds(0, n), pl.ds(0, CY))
        if p in ORDER[:2]:
            g = ORDER.index(p)
            xdown[g, pl.ds(7, 1)] = den[pl.ds(CX - 2 + g, 1), :]
            xup[g, pl.ds(7, 1)] = den[pl.ds(g, 1), :]
    own[0] = first
    own[1] = last
    load_dft = [load(fwd_hbm, fwd), load(adj_hbm, adj)]

    for copy in load_small:
        copy.wait()
    names = jnp.zeros((8, 128), F32)
    for j in range(4):
        names = jnp.where(((lane8 == j) | (lane8 == 4 + j)), tile_map[0, j].astype(F32), names)
    name_out[...] = names
    pl.semaphore_wait(barrier, len(partners))

    rounds = Zn // 2 - 1

    def pass_word(i):
        if i < rounds:
            signal(heard.at[i], dev(x, y, above, core))
            signal(heard.at[i], dev(x, y, below, core))

    def hear_word(i):
        if i < rounds:
            pl.semaphore_wait(heard.at[i], 2)

    plan = (
        (own.at[1, bottom], halo_prev.at[0], (1, 1)),
        (own.at[0, bottom], halo_prev.at[3], (1, -1)),
        (own.at[1, top], halo_next.at[0], (-1, 1)),
        (own.at[0, top], halo_next.at[3], (-1, -1)),
        (own.at[:, bottom], halo_prev.at[pl.ds(1, 2)], (1, 0)),
        (own.at[:, top], halo_next.at[pl.ds(1, 2)], (-1, 0)),
        (xdown.at[pl.ds(0, DOWN_EARLY)], xprev.at[pl.ds(0, DOWN_EARLY)], (1, 0)),
        (xup.at[pl.ds(0, UP_EARLY)], xnext.at[pl.ds(0, UP_EARLY)], (-1, 0)),
        (own.at[1], got.at[0], (0, 1)),
        (own.at[0], got.at[1], (0, -1)),
        (xdown.at[pl.ds(DOWN_EARLY, DOWN_GROUPS - DOWN_EARLY)], xprev.at[pl.ds(DOWN_EARLY, DOWN_GROUPS - DOWN_EARLY)], (1, 0)),
        (xup.at[pl.ds(UP_EARLY, UP_GROUPS - UP_EARLY)], xnext.at[pl.ds(UP_EARLY, UP_GROUPS - UP_EARLY)], (-1, 0)),
    )
    halos = [remote(src, dst, halo_send.at[i], halo_recv.at[i], near[to]) for i, (src, dst, to) in enumerate(plan)]
    for copy in halos:
        copy.start()
    pass_word(0)

    targets = []
    for k in (2, 1, 3) if G == 4 else range(1, G):
        targets.append((0, 2 * k + core, dev(wrapped(x, k, G), y, z, 0)))
        targets.append((1, 2 * k + core, dev(x, wrapped(y, k, G), z, 1)))
    targets.append((1 - core, core, dev(x, y, z, 1 - core)))
    other = dev(x, y, z, 1 - core)
    slots = 2 * G
    name_copies = [
        remote(name_out, name_in.at[slot], name_send.at[i], name_recv.at[slot], to)
        for i, (_, slot, to) in enumerate(targets)
    ]
    for copy in name_copies:
        copy.start()
    name_in[core] = name_out[...]

    def each_slot(wait):
        wait(1 - core)
        for k in range(1, G):
            for c in range(2):
                wait(2 * k + c)

    for copy in load_dft:
        copy.wait()
    cosines = [[dft_weight * math.cos((0.21 + 0.06 * f) * (n + 1)) for f in range(FREQ)] for n in range(STEPS)]
    sines = [[dft_weight * math.sin((0.21 + 0.06 * f) * (n + 1)) for f in range(FREQ)] for n in range(STEPS)]

    def chunk(r, _):
        rows = pl.ds(pl.multiple_of(r * 16, 16), 16)

        def entry(k, acc):
            one = jnp.zeros((16, CY), F32)
            two = jnp.zeros((16, CY), F32)
            for f in range(FREQ):
                re = fwd[f, 0, k, rows].astype(F32)
                im = fwd[f, 1, k, rows].astype(F32)
                acc = acc + (re * adj[f, 0, k, rows] - im * adj[f, 1, k, rows])
                one = one + (cosines[0][f] * re + sines[0][f] * im)
                two = two + (cosines[1][f] * re + sines[1][f] * im)
            gain[k, 0, rows] = one
            gain[k, 1, rows] = two
            return acc

        inter[rows] = lax.fori_loop(0, 3 * PLANES, entry, jnp.zeros((16, CY), F32))
        return 0

    lax.fori_loop(0, CX // 16, chunk, 0)

    lane = iota((EX, 128), 1)
    slot_of = lax.rem(lane, ZL)
    half_sum_scale = math.tanh(sharpness * threshold) + math.tanh(sharpness * (1.0 - threshold))

    def places(columns, width):
        rows = iota((EX, width), 0)
        rows = gx * CX + jnp.where(rows < CX + 4, rows, rows - EX)
        inside = (rows >= 0) & (rows < total_x) & (columns >= 0) & (columns < total_y)
        sigma = sigma_peak * (profile(rows.astype(F32), total_x) + profile(columns.astype(F32), total_y))
        part = jnp.where(inside, 1.0 / (1.0 + 0.5 * sigma), 0.0)
        return (1.0 - 0.5 * sigma) * part, courant * part

    damping, coef_h = places(gy * CY + iota((EX, CY), 1), CY)
    damp[...] = damping
    coef[...] = coef_h
    columns = gy * CY + jnp.where(slot_of < 4, slot_of - EDGE, slot_of + (CY - EDGE - 4))
    damp_s, ch_s = places(columns, 128)
    damp_s = jnp.where(slot_of < 8, damp_s, 0.0)
    ch_s = jnp.where(slot_of < 8, ch_s, 0.0)
    inverse = [1.0 / jnp.full((1, 128), table_ref[k], F32) for k in range(MATS)]

    each_slot(lambda slot: remote(name_out, name_in.at[slot], name_send.at[0], name_recv.at[slot], other).wait_recv())
    K = slots * 8
    P_rows = G * Zn * 2
    per = Zn * 2
    found = jnp.zeros((8, 128), F32)
    for slot in range(slots):
        part = name_in[slot]
        part = pltpu.roll(part, 8 * slot, 1) if slot else part
        found = jnp.where((lane8 >= 8 * slot) & (lane8 < 8 * slot + 8), part, found)
    shift = K
    while shift < 128:
        found = jnp.where(lane8 < shift, found, pltpu.roll(found, shift, 1))
        shift *= 2
    found = jnp.broadcast_to(found[0:1], (P_rows, 128))
    row = iota((P_rows, 128), 0)
    column = iota((P_rows, 128), 1)
    q = row // per
    place = lax.rem(row, per)
    fixed = (1 - core) * (x * 2) + core * (y * (2 * G))
    param = (place // 2) * (2 * G * G) + lax.rem(place, 2) + q * ((1 - core) * (2 * G) + core * 2) + fixed
    match = found == param.astype(F32)
    even_cells = lax.rem(column, 8) < 4
    both = jnp.concatenate(
        [jnp.where(match & even_cells, 1.0, 0.0), jnp.where(match & (~even_cells), 1.0, 0.0)], axis=0
    )
    if K == 64:
        third = jnp.where(iota((2 * P_rows, 128), 1) < 3 * K - 128, both, 0.0)
        chosen = jnp.concatenate([both, third], axis=1).astype(BF16)
    else:
        chosen = jnp.where(iota((2 * P_rows, 128), 1) < 3 * K, both, 0.0).astype(BF16)
    hear_word(0)
    pass_word(1)

    for copy in halos[:10]:
        copy.wait_recv()

    def xn(f):
        return pltpu.roll(f, EX - 1, 0)

    def xp(f):
        return pltpu.roll(f, 1, 0)

    def yn(f, strip, p):
        a, b = pltpu.roll(f[:, :128], 127, 1), pltpu.roll(f[:, 128:], 127, 1)
        edge = pltpu.roll(strip, (127 - 6 - p * ZL) % 128, 1)
        end = lane == 127
        return jnp.concatenate([jnp.where(end, b, a), jnp.where(end, edge, b)], axis=1)

    def yp(f, strip, p):
        a, b = pltpu.roll(f[:, :128], 1, 1), pltpu.roll(f[:, 128:], 1, 1)
        edge = pltpu.roll(strip, (127 - p * ZL) % 128, 1)
        start = lane == 0
        return jnp.concatenate([jnp.where(start, edge, a), jnp.where(start, a, b)], axis=1)

    wide = iota((8, CY), 0)
    narrow8 = iota((8, 128), 0)
    from_next, from_prev = (wide < 2) & has_next, (wide >= 6) & has_prev

    def x_halo(kind, p):
        if kind == 7:
            ahead = jnp.where(wide == 0, pltpu.roll(xnext[0], 1, 0), pltpu.roll(xnext[1], 2, 0))
            behind = jnp.where(wide == 6, pltpu.roll(xprev[0], 7, 0), xprev[1])
        else:
            g, at, _ = row_slot(False, kind, p)
            ahead = pltpu.roll(xnext[g], (8 - at) % 8, 0) if at else xnext[g]
            g, at, n = row_slot(True, kind, p)
            shift = (8 - n - at) % 8
            behind = pltpu.roll(xprev[g], shift, 0) if shift else xprev[g]
        return jnp.where(from_next, ahead, jnp.where(from_prev, behind, 0.0))

    halo_rows = pl.ds(CX, 8)
    for c in range(3):
        E[c, NZ] = jnp.zeros((EX, CY), F32)
        H[c, 0] = jnp.zeros((EX, CY), F32)

    def take_halo(planes):
        for p in planes:
            for c in range(3):
                E[c, p, halo_rows] = x_halo(c, p)
                H[c, p + 1, halo_rows] = x_halo(3 + c, p)

    take_halo(ORDER[:EARLY])

    pieces = []
    for i, body in enumerate((got[0], own[0], own[1], got[1])):
        rim = jnp.where((narrow8 < 4) & has_next, halo_next[i], jnp.where((narrow8 >= 4) & has_prev, halo_prev[i], 0.0))
        piece = jnp.concatenate([body, rim], axis=0)
        if i == 0:
            piece = jnp.where(has_left, piece, 0.0)
        if i == 3:
            piece = jnp.where(has_right, piece, 0.0)
        pieces.append(piece)

    def strip(kind):
        value = jnp.zeros((EX, 128), F32)
        for i, piece in enumerate(pieces):
            shift = (EDGE * i - EDGE * kind) % 128
            moved = pltpu.roll(piece, shift, 1) if shift else piece
            value = jnp.where((slot_of >= EDGE * i) & (slot_of < EDGE * (i + 1)), moved, value)
        return value

    def design(filtered):
        bend = jnp.tanh(sharpness * (filtered - threshold))
        projected = (math.tanh(sharpness * threshold) + bend) / half_sum_scale
        return bend, eps_low + (eps_high - eps_low) * projected

    dens = jnp.concatenate([den[...], x_halo(7, 0)], axis=0)
    dens_s = strip(7)
    dens = xp(dens) + 2.0 * dens + xn(dens)
    dens_s = xp(dens_s) + 2.0 * dens_s + xn(dens_s)
    bend, eps = design((yp(dens, dens_s, ZLO) + 2.0 * dens + yn(dens, dens_s, ZLO)) / 16.0)
    slope[...] = (sharpness * (1.0 - bend * bend) / half_sum_scale)[:CX]
    design_coef = coef[...] / eps

    def set_coef(planes):
        for p in planes:
            if ZLO <= p < ZLO + PLANES:
                CE[p] = design_coef
            else:
                mats = jnp.concatenate([mat[p].astype(F32), x_halo(6, p)], axis=0)
                part = jnp.broadcast_to(inverse[MATS - 1][:, :1], (EX, CY))
                for k in range(MATS - 1):
                    part = jnp.where(mats == float(k), inverse[k][:, :1], part)
                CE[p] = coef[...] * part

    set_coef(range(ZLO - 1, ZLO + PLANES + 1))
    eps_s = design((pltpu.roll(dens_s, 1, 1) + 2.0 * dens_s + pltpu.roll(dens_s, 127, 1)) / 16.0)[1]
    mats = strip(6)
    part = jnp.broadcast_to(inverse[MATS - 1], (EX, 128))
    for k in range(MATS - 1):
        part = jnp.where(mats == float(k), inverse[k], part)
    layer = (lane >= ZLO * ZL) & (lane < (ZLO + PLANES) * ZL)
    ce_s = ch_s * jnp.where(layer, 1.0 / eps_s, part)

    def yns(f):
        return pltpu.roll(f, 127, 1)

    def yps(f):
        return pltpu.roll(f, 1, 1)

    def zns(f):
        return jnp.where(lane < 128 - ZL, pltpu.roll(f, 128 - ZL, 1), 0.0)

    def zps(f):
        return jnp.where(lane >= ZL, pltpu.roll(f, ZL, 1), 0.0)

    def strip_h(ex, ey, ez, hx, hy, hz):
        cx = (yns(ez) - ez) - (zns(ey) - ey)
        cy = (zns(ex) - ex) - (xn(ez) - ez)
        cz = (xn(ey) - ey) - (yns(ex) - ex)
        return damp_s * hx - ch_s * cx, damp_s * hy - ch_s * cy, damp_s * hz - ch_s * cz

    def strip_e(ex, ey, ez, hx, hy, hz):
        cx = (hz - yps(hz)) - (hy - zps(hy))
        cy = (hx - zps(hx)) - (hz - xp(hz))
        cz = (hy - xp(hy)) - (hx - yps(hx))
        return damp_s * ex + ce_s * cx, damp_s * ey + ce_s * cy, damp_s * ez + ce_s * cz

    es = tuple(strip(c) for c in range(3))
    hs = tuple(strip(c) for c in range(3, 6))
    strips[0], strips[1] = es[0], es[2]
    hs = strip_h(*es, *hs)
    strips[2], strips[3] = hs[0], hs[2]
    es = strip_e(*es, *hs)
    strips[4], strips[5] = es[0], es[2]
    hs = strip_h(*es, *hs)
    strips[6], strips[7] = hs[0], hs[2]

    def half_h(p, n):
        ex, ey, ez = E[0, p], E[1, p], E[2, p]
        d, c = damp[...], coef[...]
        hx = d * H[0, p + 1] - c * ((yn(ez, strips[4 * n + 1], p) - ez) - (E[1, p + 1] - ey))
        hy = d * H[1, p + 1] - c * ((E[0, p + 1] - ex) - (xn(ez) - ez))
        hz = d * H[2, p + 1] - c * ((xn(ey) - ey) - (yn(ex, strips[4 * n], p) - ex))
        for i, value in enumerate((hx, hy, hz)):
            H[i, p + 1] = value
            if n:
                h_out[i, p] = value[:CX]

    def half_e(p, n):
        hx, hy, hz = H[0, p + 1], H[1, p + 1], H[2, p + 1]
        d, c = damp[...], CE[p]
        ex = d * E[0, p] + c * ((hz - yp(hz, strips[4 * n + 3], p)) - (hy - H[1, p]))
        ey = d * E[1, p] + c * ((hx - H[0, p]) - (hz - xp(hz)))
        ez = d * E[2, p] + c * ((hy - xp(hy)) - (hx - yp(hx, strips[4 * n + 2], p)))
        acc = inter[...]
        for i, value in enumerate((ex, ey, ez)):
            if n:
                e_out[i, p] = value[:CX]
            else:
                E[i, p] = value
            if ZLO <= p < ZLO + PLANES:
                acc = acc + gain[PLANES * i + (p - ZLO), n] * value[:CX]
        if ZLO <= p < ZLO + PLANES:
            inter[...] = acc

    before, behind_layer = ZLO - 2, ZLO + PLANES
    for p in range(before, behind_layer + 1):
        half_h(p, 0)
        if p > before:
            half_e(p, 0)
        if p > before + 1:
            half_h(p - 1, 1)
        if p > before + 2:
            half_e(p - 1, 1)
    local[...] = grad_scale * (eps_high - eps_low) * slope[...] * inter[...]

    plan = (
        (local.at[bottom, high], corner.at[0], (1, 1)),
        (local.at[bottom, low], corner.at[1], (1, -1)),
        (local.at[top, high], corner.at[2], (-1, 1)),
        (local.at[top, low], corner.at[3], (-1, -1)),
        (local.at[bottom], rim_prev, (1, 0)),
        (local.at[top], rim_next, (-1, 0)),
        (local.at[:, high], rim_left, (0, 1)),
        (local.at[:, low], rim_right, (0, -1)),
    )
    rims = [remote(src, dst, rim_send.at[i], rim_recv.at[i], near[to]) for i, (src, dst, to) in enumerate(plan)]
    for copy in rims:
        copy.start()

    for copy in halos[10:]:
        copy.wait_recv()
    take_halo(ORDER[EARLY:])
    set_coef([p for p in range(NZ) if not ZLO - 1 <= p <= ZLO + PLANES])
    for p in range(behind_layer + 1, NZ + 1):
        if p < NZ:
            half_h(p, 0)
            half_e(p, 0)
        half_h(p - 1, 1)
        half_e(p - 1, 1)

    hear_word(1)
    pass_word(2)

    def smooth_rows(main, left, right):
        count = main.shape[0]
        lanes = iota((count, 128), 1)

        def along_x(f):
            return pltpu.roll(f, 1, 0) + 2.0 * f + pltpu.roll(f, count - 1, 0)

        a, b = along_x(main[:, :128]), along_x(main[:, 128:])
        left = pltpu.roll(along_x(jnp.where(has_left, left, 0.0)), 1, 1)
        right = pltpu.roll(along_x(jnp.where(has_right, right, 0.0)), 127, 1)
        start, end = lanes == 0, lanes == 127
        ra, rb = pltpu.roll(a, 1, 1), pltpu.roll(b, 1, 1)
        la, lb = pltpu.roll(a, 127, 1), pltpu.roll(b, 127, 1)
        a = (jnp.where(start, left, ra) + 2.0 * a + jnp.where(end, lb, la)) / 16.0
        b = (jnp.where(start, ra, rb) + 2.0 * b + jnp.where(end, right, lb)) / 16.0
        return a, b

    def put(at, h, row):
        slim = iota((8, 128), 1) < TILE
        for j in range(4):
            even = cells[j // 2, pl.ds(at, 8, stride=2), :]
            odd = cells[j // 2, pl.ds(at + 1, 8, stride=2), :]
            if j % 2:
                tile = jnp.where(slim, pltpu.roll(even, TILE, 1), odd)
            else:
                tile = jnp.where(slim, even, pltpu.roll(odd, TILE, 1))
            message[h, pl.ds(4 * row + j, 8, stride=4), :] = tile

    first_stop = []

    def rows_of(turn, h):
        if isinstance(h, int):
            return pl.ds(32 * ((turn + 1 - h) % 2), 32)
        return pl.ds(pl.multiple_of(32 * lax.rem(turn + 1 - h, 2), 32), 32)

    def send_turn(turn):
        for i, (h, slot, to) in enumerate(targets):
            where = rows_of(turn, h if isinstance(h, int) else 1 - core)
            copy = remote(
                message.at[h, where], gathered.at[slot, where], a_send.at[turn, i], a_recv.at[turn, slot], to
            )
            copy.start()
            first_stop.append(copy)

    for copy in rims[6:]:
        copy.wait_recv()
    inner = pl.ds(8, 48)
    a, b = smooth_rows(local[inner], rim_left[inner], rim_right[inner])
    cells[0, inner] = a
    cells[1, inner] = b
    put(16, 0, 8)
    put(32, 1, 0)
    send_turn(0)
    for p in range(before):
        half_h(p, 0)
    for copy in rims[:6]:
        copy.wait_recv()
    tail, head = pl.ds(40, 24), pl.ds(0, 24)
    rows = jnp.where((wide < 4) & has_next, rim_next[...], jnp.where((wide >= 4) & has_prev, rim_prev[...], 0.0))
    side = lambda ahead, back: jnp.where(
        (narrow8 < 4) & has_next, corner[ahead], jnp.where((narrow8 >= 4) & has_prev, corner[back], 0.0)
    )
    a, b = smooth_rows(
        jnp.concatenate([local[tail], rows, local[head]], axis=0),
        jnp.concatenate([rim_left[tail], side(2, 0), rim_left[head]], axis=0),
        jnp.concatenate([rim_right[tail], side(3, 1), rim_right[head]], axis=0),
    )
    for i, value in enumerate((a, b)):
        cells[i, pl.ds(48, 16)] = value[8:24]
        cells[i, pl.ds(0, 16)] = value[32:48]
    put(0, 0, 0)
    put(48, 1, 8)
    send_turn(1)
    gathered[core] = message[core]

    for p in range(before + 1):
        half_e(p, 0)
    for p in range(before + 1):
        half_h(p, 1)
    for p in range(before + 2):
        half_e(p, 1)

    mine = (1 - core) * y + core * x

    def ring(k):
        there = wrapped(mine, k, G)
        return there, dev((1 - core) * x + core * there, (1 - core) * there + core * y, z, core)

    ahead, to_ahead = ring(1)
    behind, to_behind = ring(-1)
    across, _ = ring(2)
    second_stop = {}
    for turn in range(2):
        where = rows_of(turn, core)
        each_slot(
            lambda slot: remote(
                message.at[0, where], gathered.at[slot, where], a_send.at[turn, 0], a_recv.at[turn, slot], other
            ).wait_recv()
        )
        offset = 32 * lax.rem(turn + 1 - core, 2)
        for way in range(2):
            for m in range(2 * way, 2 * way + 2):
                eight = pl.ds(pl.multiple_of(offset + 8 * m, 8), 8)
                data = jnp.concatenate([gathered[slot, eight] for slot in range(slots)], axis=0)
                hi = data.astype(BF16)
                rest = data - hi.astype(F32)
                mid = rest.astype(BF16)
                lo = (rest - mid.astype(F32)).astype(BF16)
                picked = jnp.dot(chosen, jnp.concatenate([hi, mid, lo, hi], axis=0), preferred_element_type=F32)
                for parity in range(2):
                    for place_q in range(G):
                        start = parity * P_rows + place_q * per
                        sums[turn, way, place_q, 2 * (m - 2 * way) + parity] = picked[start : start + per]
            far, near_by = (to_ahead, to_behind) if way == 0 else (to_behind, to_ahead)
            straight = behind if way == 0 else ahead
            for kind, src, dst, to in ((0, across, passing, far), (1, straight, direct, near_by)):
                copy = remote(
                    sums.at[turn, way, src], dst.at[turn, way], b_send.at[turn, way, kind], b_recv.at[turn, way, kind], to
                )
                copy.start()
                second_stop[turn, way, kind] = copy
    for turn in range(2):
        for way in range(2):
            far = to_ahead if way == 0 else to_behind
            onward = ahead if way == 0 else behind
            second_stop[turn, way, 0].wait_recv()
            passing[turn, way] = passing[turn, way] + sums[turn, way, onward]
            copy = remote(
                passing.at[turn, way], combined.at[turn, way], b_send.at[turn, way, 2], b_recv.at[turn, way, 2], far
            )
            copy.start()
            second_stop[turn, way, 2] = copy
    hear_word(2)

    third_stop = []
    order = sorted(range(Zn), key=lambda k: -min(k, Zn - k))
    for turn in range(2):
        for way in range(2):
            second_stop[turn, way, 1].wait_recv()
            second_stop[turn, way, 2].wait_recv()
            for b in range(4):
                value = sums[turn, way, mine, b] + direct[turn, way, b] + combined[turn, way, b]
                ready[turn, pl.ds(4 * way + b, per, stride=8), :] = value
        eight = pl.ds(8 * turn, 8)
        for k in order:
            there = wrapped(z, k, Zn)
            for c in range(2):
                if k == 0 and c == 0:
                    continue
                target = c if k else 1 - core
                start = pl.multiple_of((there * 2 + target) * 8, 8)
                copy = remote(
                    ready.at[turn, pl.ds(start, 8)],
                    landed.at[2 * k + core, eight],
                    c_send.at[turn, 2 * k + c],
                    c_recv.at[turn, 2 * k + core],
                    dev(x, y, there, target),
                )
                copy.start()
                third_stop.append(copy)
        landed[core, eight] = ready[turn, pl.ds(pl.multiple_of((z * 2 + core) * 8, 8), 8)]

    for turn in range(2):
        eight = pl.ds(8 * turn, 8)

        def landing(slot):
            remote(
                ready.at[turn, pl.ds(0, 8)], landed.at[slot, eight], c_send.at[turn, 0], c_recv.at[turn, slot], other
            ).wait_recv()

        landing(1 - core)
        for k in range(1, Zn):
            for c in range(2):
                landing(2 * k + c)
        for h in range(2):
            value = landed[h, eight]
            for k in range(1, Zn):
                value = value + landed[2 * k + h, eight]
            out[pl.ds(16 * h + 8 * ((turn + 1 - h) % 2), 8)] = value
    for copy in halos + rims + name_copies + first_stop + list(second_stop.values()) + third_stop:
        copy.wait_send()


def solve(G, Zn, e, h, mat, den, fwd, adj, table, tile_map):
    per = Zn * 2
    dma = pltpu.SemaphoreType.DMA
    vmem = lambda *shape: pltpu.VMEM(shape, F32)
    return pl.pallas_call(
        functools.partial(solve_kernel, G, Zn),
        name="solve",
        out_shape=(pltpu.VMEM(e.shape, F32), pltpu.VMEM(h.shape, F32), pltpu.VMEM((32, 128), F32)),
        in_specs=[ANY] * 8,
        out_specs=(VMEM, VMEM, VMEM),
        scratch_shapes=[
            pltpu.SMEM(table.shape, F32),
            pltpu.SMEM(tile_map.shape, jnp.int32),
            vmem(3, NZ + 1, EX, CY),
            vmem(3, NZ + 1, EX, CY),
            vmem(NZ, EX, CY),
            pltpu.VMEM(mat.shape, jnp.int32),
            vmem(CX, CY),
            pltpu.VMEM(fwd.shape, BF16),
            pltpu.VMEM(adj.shape, F32),
            vmem(3 * PLANES, STEPS, CX, CY),
            vmem(CX, CY),
            vmem(CX, CY),
            vmem(EX, CY),
            vmem(EX, CY),
            vmem(2, CX, 128),
            vmem(2, CX, 128),
            vmem(4, 8, 128),
            vmem(4, 8, 128),
            vmem(DOWN_GROUPS, 8, CY),
            vmem(UP_GROUPS, 8, CY),
            vmem(DOWN_GROUPS, 8, CY),
            vmem(UP_GROUPS, 8, CY),
            vmem(8, EX, 128),
            vmem(CX, CY),
            vmem(CX, 128),
            vmem(CX, 128),
            vmem(8, CY),
            vmem(8, CY),
            vmem(4, 8, 128),
            vmem(2, CX, 128),
            vmem(2, CX, 128),
            vmem(8, 128),
            vmem(2 * G, 8, 128),
            vmem(2 * G, CX, 128),
            vmem(2, 2, G, 4, per, 128),
            vmem(2, 2, 4, per, 128),
            vmem(2, 2, 4, per, 128),
            vmem(2, 2, 4, per, 128),
            vmem(2, per * 8, 128),
            vmem(2 * Zn, 16, 128),
            dma((3 * NZ + 5,)),
            dma((12,)),
            dma((12,)),
            dma((8,)),
            dma((8,)),
            dma((2 * G,)),
            dma((2 * G,)),
            dma((2, 2 * G)),
            dma((2, 2 * G)),
            dma((2, 2, 3)),
            dma((2, 2, 3)),
            dma((2, 2 * Zn)),
            dma((2, 2 * Zn)),
            pltpu.SemaphoreType.REGULAR((3,)),
        ],
        compiler_params=pltpu.CompilerParams(collective_id=0, has_side_effects=True),
    )(e, h, mat, den, fwd, adj, table, tile_map)


def write_kernel(e, h, params, e_out, h_out, params_out, sems):
    copies = []
    for src, dst in ((e, e_out), (h, h_out)):
        for c in range(3):
            for half in range(2):
                part = pl.ds(half * (NZ // 2), NZ // 2)
                copies.append(pltpu.make_async_copy(src.at[c, part], dst.at[c, part], sems.at[len(copies)]))
    copies.append(pltpu.make_async_copy(params, params_out, sems.at[len(copies)]))
    for copy in copies:
        copy.start()
    for copy in copies:
        copy.wait()


def write(e, h, params):
    shape = jax.ShapeDtypeStruct
    return pl.pallas_call(
        write_kernel,
        name="write",
        out_shape=tuple(shape(array.shape, F32) for array in (e, h, params)),
        in_specs=[VMEM] * 3,
        out_specs=(ANY,) * 3,
        scratch_shapes=[pltpu.SemaphoreType.DMA((13,))],
    )(*(pltpu.with_memory_space_constraint(array, pltpu.VMEM) for array in (e, h, params)))


def on_device(nx, ny, e_adj, h_adj, density, material, eps_table, dft_adj, dft_fwd, tile_map):
    G = ny // 2
    flat = lambda array: array.reshape(FREQ, 2, 3 * PLANES, CX, CY)
    e_out, h_out, params = solve(
        G, nx // G, e_adj, h_adj, material, density, flat(dft_fwd), flat(dft_adj), eps_table, tile_map
    )
    e_out, h_out, params = write(e_out, h_out, params)
    return e_out, h_out, params.reshape(1, TILE * TILE)


def solution(mesh):
    in_specs = (
        P(None, None, "gx", "gy"),
        P(None, None, "gx", "gy"),
        P("gx", "gy"),
        P(None, "gx", "gy"),
        P(),
        P(None, None, None, None, "gx", "gy"),
        P(None, None, None, None, "gx", "gy"),
        P("gx", "gy"),
    )
    out_specs = (P(None, None, "gx", "gy"), P(None, None, "gx", "gy"), P(("gx", "gy"), None))
    return jax.shard_map(
        functools.partial(on_device, mesh.shape["gx"], mesh.shape["gy"]),
        mesh=mesh,
        in_specs=in_specs,
        out_specs=out_specs,
        check_vma=False,
    )
```

```python
import functools
import math

import jax
import jax.numpy as jnp
from jax import lax
from jax.experimental import pallas as pl
from jax.experimental.pallas import tpu as pltpu
from jax.sharding import PartitionSpec as P

MESH = pl.DeviceIdType.MESH

PLANES = 2
ZLO = 3
STEPS = 2
FREQ = 4
PML = 12
MATS = 4
TILE = 64

courant = 0.5
sigma_peak = 0.8
dft_weight = 0.5
sharpness = 4.0
threshold = 0.5
eps_low = 2.1
eps_high = 12.1
grad_scale = 0.01

F32 = jnp.float32
BF16 = jnp.bfloat16
VMEM = pl.BlockSpec(memory_space=pltpu.VMEM)
ANY = pl.BlockSpec(memory_space=pl.ANY)

CX, CY, NZ = 64, 256, 8
EX = CX + 8
KINDS = 8
EDGE = 2
ZL = KINDS * EDGE


def iota(shape, dim):
    return lax.broadcasted_iota(jnp.int32, shape, dim)


def wrapped(index, shift, count):
    return lax.rem(index + (shift + count), count)


def around(gx, gy, nx, ny):
    places = {}
    for dx in (-1, 0, 1):
        for dy in (-1, 0, 1):
            if dx or dy:
                places[dx, dy] = (wrapped(gx, dx, nx), wrapped(gy, dy, ny))
    return places


def remote(src, dst, send, recv, device):
    return pltpu.make_async_remote_copy(
        src_ref=src, dst_ref=dst, send_sem=send, recv_sem=recv, device_id=device, device_id_type=MESH
    )


def profile(places, total):
    depth = jnp.maximum(jnp.maximum(PML - places, places - (total - 1 - PML)), 0.0) / PML
    return depth * depth * depth


ORDER = (1, 2, 3, 4, 5, 6, 0, 7)
EARLY = 6
DOWN_EARLY, DOWN_GROUPS = 11, 15
UP_EARLY, UP_GROUPS = 9, 12


def row_slot(down, kind, z):
    at = ORDER.index(z)
    early = DOWN_EARLY if down else UP_EARLY
    start, at, count = (0, at, EARLY) if at < EARLY else (early, at - EARLY, NZ - EARLY)
    if kind < 3:
        return start + at, 2 * kind, 2
    if kind == 6:
        return start + at, 6, 1
    each = 2 if down else 1
    row = (3 * at + kind - 3) * each
    return start + count + row // 8, row % 8, each


def solve_kernel(
    G, Zn,
    e_hbm, h_hbm, mat_hbm, den_hbm, fwd_hbm, adj_hbm, table_hbm, map_hbm,
    e_out, h_out, out,
    table_ref, tile_map, E, H, CE, mat, den, fwd, adj, gain, inter, slope, damp, coef, own, got, halo_prev, halo_next, xdown, xup, xprev, xnext, strips,
    local, rim_left, rim_right, rim_prev, rim_next, corner, cells, message, name_out, name_in, gathered, sums, passing, direct,
    combined, ready, landed,
    load_sem, halo_send, halo_recv,
    rim_send, rim_recv, name_send, name_recv, a_send, a_recv, b_send, b_recv, c_send, c_recv, heard,
):
    gx, gy = lax.axis_index("gx"), lax.axis_index("gy")
    nx, ny = Zn * G, 2 * G
    x, core = gy // 2, lax.rem(gy, 2)
    z, y = gx // G, lax.rem(gx, G)
    has_prev, has_next = gx > 0, gx < nx - 1
    has_left, has_right = gy > 0, gy < ny - 1
    total_x, total_y = nx * CX, ny * CY

    def dev(x, y, z, core):
        return (z * G + y, x * 2 + core)

    def signal(semaphore, device):
        pl.semaphore_signal(semaphore, inc=1, device_id=device, device_id_type=MESH)

    near = around(gx, gy, nx, ny)
    partners = list(near.values())
    for k in range(1, G):
        for c in range(2):
            partners.append(dev(wrapped(x, k, G), y, z, c))
            partners.append(dev(x, wrapped(y, k, G), z, c))
    partners.append(dev(x, y, z, 1 - core))
    above, below = wrapped(z, 1, Zn), wrapped(z, -1, Zn)
    for c in range(2):
        partners.append(dev(x, y, above, c))
        partners.append(dev(x, y, below, c))
    block = pl.ds(0, CX)
    loads = []

    def load(src, dst):
        copy = pltpu.make_async_copy(src, dst, load_sem.at[len(loads)])
        copy.start()
        loads.append(copy)
        return copy

    load_den = load(den_hbm, den)
    load_small = [load(map_hbm, tile_map), load(table_hbm, table_ref)]
    load_planes = {
        p: (
            load(e_hbm.at[:, p], E.at[:, p, block]),
            load(h_hbm.at[:, p], H.at[:, p + 1, block]),
            load(mat_hbm.at[p], mat.at[p]),
        )
        for p in ORDER
    }

    barrier = pltpu.get_barrier_semaphore()
    for device in partners:
        signal(barrier, device)

    lane64 = iota((CX, 128), 1)
    lane8 = iota((8, 128), 1)
    low, high, top, bottom = pl.ds(0, 128), pl.ds(128, 128), pl.ds(0, 8), pl.ds(CX - 8, 8)

    def plane(kind, p, rows, columns):
        if kind < 3:
            return E[kind, p, rows, columns]
        if kind < 6:
            return H[kind - 3, p + 1, rows, columns]
        if kind == 6:
            return mat[p, rows, columns].astype(F32)
        return den[rows, columns]

    load_den.wait()
    first = jnp.zeros((CX, 128), F32)
    last = jnp.zeros((CX, 128), F32)
    empty = jnp.zeros((8, CY), F32)
    for g in range(DOWN_GROUPS):
        xdown[g] = empty
    for g in range(UP_GROUPS):
        xup[g] = empty
    for p in ORDER:
        for copy in load_planes[p]:
            copy.wait()
        kinds = list(range(7)) + ([7] if ZLO <= p < ZLO + PLANES else [])
        for kind in kinds:
            at = p * ZL + EDGE * kind
            mine = (lane64 >= at) & (lane64 < at + EDGE)
            a = plane(kind, p, block, low)
            b = plane(kind, p, block, high)
            first = jnp.where(mine, pltpu.roll(a, at, 1) if at else a, first)
            last = jnp.where(mine, pltpu.roll(b, at + EDGE, 1) if at + EDGE < 128 else b, last)
        for kind in range(7):
            g, row, n = row_slot(True, kind, p)
            xdown[g, pl.ds(row, n)] = plane(kind, p, pl.ds(CX - n, n), pl.ds(0, CY))
            g, row, n = row_slot(False, kind, p)
            xup[g, pl.ds(row, n)] = plane(kind, p, pl.ds(0, n), pl.ds(0, CY))
        if p in ORDER[:2]:
            g = ORDER.index(p)
            xdown[g, pl.ds(7, 1)] = den[pl.ds(CX - 2 + g, 1), :]
            xup[g, pl.ds(7, 1)] = den[pl.ds(g, 1), :]
    own[0] = first
    own[1] = last
    load_dft = [load(fwd_hbm, fwd), load(adj_hbm, adj)]

    for copy in load_small:
        copy.wait()
    names = jnp.zeros((8, 128), F32)
    for j in range(4):
        names = jnp.where(((lane8 == j) | (lane8 == 4 + j)), tile_map[0, j].astype(F32), names)
    name_out[...] = names
    pl.semaphore_wait(barrier, len(partners))

    rounds = Zn // 2 - 1

    def pass_word(i):
        if i < rounds:
            signal(heard.at[i], dev(x, y, above, core))
            signal(heard.at[i], dev(x, y, below, core))

    def hear_word(i):
        if i < rounds:
            pl.semaphore_wait(heard.at[i], 2)

    plan = (
        (own.at[1, bottom], halo_prev.at[0], (1, 1)),
        (own.at[0, bottom], halo_prev.at[3], (1, -1)),
        (own.at[1, top], halo_next.at[0], (-1, 1)),
        (own.at[0, top], halo_next.at[3], (-1, -1)),
        (own.at[:, bottom], halo_prev.at[pl.ds(1, 2)], (1, 0)),
        (own.at[:, top], halo_next.at[pl.ds(1, 2)], (-1, 0)),
        (xdown.at[pl.ds(0, DOWN_EARLY)], xprev.at[pl.ds(0, DOWN_EARLY)], (1, 0)),
        (xup.at[pl.ds(0, UP_EARLY)], xnext.at[pl.ds(0, UP_EARLY)], (-1, 0)),
        (own.at[1], got.at[0], (0, 1)),
        (own.at[0], got.at[1], (0, -1)),
        (xdown.at[pl.ds(DOWN_EARLY, DOWN_GROUPS - DOWN_EARLY)], xprev.at[pl.ds(DOWN_EARLY, DOWN_GROUPS - DOWN_EARLY)], (1, 0)),
        (xup.at[pl.ds(UP_EARLY, UP_GROUPS - UP_EARLY)], xnext.at[pl.ds(UP_EARLY, UP_GROUPS - UP_EARLY)], (-1, 0)),
    )
    halos = [remote(src, dst, halo_send.at[i], halo_recv.at[i], near[to]) for i, (src, dst, to) in enumerate(plan)]
    for copy in halos:
        copy.start()
    pass_word(0)

    targets = []
    for k in (2, 1, 3) if G == 4 else range(1, G):
        targets.append((0, 2 * k + core, dev(wrapped(x, k, G), y, z, 0)))
        targets.append((1, 2 * k + core, dev(x, wrapped(y, k, G), z, 1)))
    targets.append((1 - core, core, dev(x, y, z, 1 - core)))
    other = dev(x, y, z, 1 - core)
    slots = 2 * G
    name_copies = [
        remote(name_out, name_in.at[slot], name_send.at[i], name_recv.at[slot], to)
        for i, (_, slot, to) in enumerate(targets)
    ]
    for copy in name_copies:
        copy.start()
    name_in[core] = name_out[...]

    def each_slot(wait):
        wait(1 - core)
        for k in range(1, G):
            for c in range(2):
                wait(2 * k + c)

    for copy in load_dft:
        copy.wait()
    cosines = [[dft_weight * math.cos((0.21 + 0.06 * f) * (n + 1)) for f in range(FREQ)] for n in range(STEPS)]
    sines = [[dft_weight * math.sin((0.21 + 0.06 * f) * (n + 1)) for f in range(FREQ)] for n in range(STEPS)]

    def chunk(r, _):
        rows = pl.ds(pl.multiple_of(r * 16, 16), 16)

        def entry(k, acc):
            one = jnp.zeros((16, CY), F32)
            two = jnp.zeros((16, CY), F32)
            for f in range(FREQ):
                re = fwd[f, 0, k, rows].astype(F32)
                im = fwd[f, 1, k, rows].astype(F32)
                acc = acc + (re * adj[f, 0, k, rows] - im * adj[f, 1, k, rows])
                one = one + (cosines[0][f] * re + sines[0][f] * im)
                two = two + (cosines[1][f] * re + sines[1][f] * im)
            gain[k, 0, rows] = one
            gain[k, 1, rows] = two
            return acc

        inter[rows] = lax.fori_loop(0, 3 * PLANES, entry, jnp.zeros((16, CY), F32))
        return 0

    lax.fori_loop(0, CX // 16, chunk, 0)

    lane = iota((EX, 128), 1)
    slot_of = lax.rem(lane, ZL)
    half_sum_scale = math.tanh(sharpness * threshold) + math.tanh(sharpness * (1.0 - threshold))

    def places(columns, width):
        rows = iota((EX, width), 0)
        rows = gx * CX + jnp.where(rows < CX + 4, rows, rows - EX)
        inside = (rows >= 0) & (rows < total_x) & (columns >= 0) & (columns < total_y)
        sigma = sigma_peak * (profile(rows.astype(F32), total_x) + profile(columns.astype(F32), total_y))
        part = jnp.where(inside, 1.0 / (1.0 + 0.5 * sigma), 0.0)
        return (1.0 - 0.5 * sigma) * part, courant * part

    damping, coef_h = places(gy * CY + iota((EX, CY), 1), CY)
    damp[...] = damping
    coef[...] = coef_h
    columns = gy * CY + jnp.where(slot_of < 4, slot_of - EDGE, slot_of + (CY - EDGE - 4))
    damp_s, ch_s = places(columns, 128)
    damp_s = jnp.where(slot_of < 8, damp_s, 0.0)
    ch_s = jnp.where(slot_of < 8, ch_s, 0.0)
    inverse = [1.0 / jnp.full((1, 128), table_ref[k], F32) for k in range(MATS)]

    each_slot(lambda slot: remote(name_out, name_in.at[slot], name_send.at[0], name_recv.at[slot], other).wait_recv())
    K = slots * 8
    P_rows = G * Zn * 2
    per = Zn * 2
    found = jnp.zeros((8, 128), F32)
    for slot in range(slots):
        part = name_in[slot]
        part = pltpu.roll(part, 8 * slot, 1) if slot else part
        found = jnp.where((lane8 >= 8 * slot) & (lane8 < 8 * slot + 8), part, found)
    shift = K
    while shift < 128:
        found = jnp.where(lane8 < shift, found, pltpu.roll(found, shift, 1))
        shift *= 2
    found = jnp.broadcast_to(found[0:1], (P_rows, 128))
    row = iota((P_rows, 128), 0)
    column = iota((P_rows, 128), 1)
    q = row // per
    place = lax.rem(row, per)
    fixed = (1 - core) * (x * 2) + core * (y * (2 * G))
    param = (place // 2) * (2 * G * G) + lax.rem(place, 2) + q * ((1 - core) * (2 * G) + core * 2) + fixed
    match = found == param.astype(F32)
    even_cells = lax.rem(column, 8) < 4
    both = jnp.concatenate(
        [jnp.where(match & even_cells, 1.0, 0.0), jnp.where(match & (~even_cells), 1.0, 0.0)], axis=0
    )
    if K == 64:
        third = jnp.where(iota((2 * P_rows, 128), 1) < 3 * K - 128, both, 0.0)
        chosen = jnp.concatenate([both, third], axis=1).astype(BF16)
    else:
        chosen = jnp.where(iota((2 * P_rows, 128), 1) < 3 * K, both, 0.0).astype(BF16)
    hear_word(0)
    pass_word(1)

    for copy in halos[:10]:
        copy.wait_recv()

    def xn(f):
        return pltpu.roll(f, EX - 1, 0)

    def xp(f):
        return pltpu.roll(f, 1, 0)

    def yn(f, strip, p):
        a, b = pltpu.roll(f[:, :128], 127, 1), pltpu.roll(f[:, 128:], 127, 1)
        edge = pltpu.roll(strip, (127 - 6 - p * ZL) % 128, 1)
        end = lane == 127
        return jnp.concatenate([jnp.where(end, b, a), jnp.where(end, edge, b)], axis=1)

    def yp(f, strip, p):
        a, b = pltpu.roll(f[:, :128], 1, 1), pltpu.roll(f[:, 128:], 1, 1)
        edge = pltpu.roll(strip, (127 - p * ZL) % 128, 1)
        start = lane == 0
        return jnp.concatenate([jnp.where(start, edge, a), jnp.where(start, a, b)], axis=1)

    wide = iota((8, CY), 0)
    narrow8 = iota((8, 128), 0)
    from_next, from_prev = (wide < 2) & has_next, (wide >= 6) & has_prev

    def x_halo(kind, p):
        if kind == 7:
            ahead = jnp.where(wide == 0, pltpu.roll(xnext[0], 1, 0), pltpu.roll(xnext[1], 2, 0))
            behind = jnp.where(wide == 6, pltpu.roll(xprev[0], 7, 0), xprev[1])
        else:
            g, at, _ = row_slot(False, kind, p)
            ahead = pltpu.roll(xnext[g], (8 - at) % 8, 0) if at else xnext[g]
            g, at, n = row_slot(True, kind, p)
            shift = (8 - n - at) % 8
            behind = pltpu.roll(xprev[g], shift, 0) if shift else xprev[g]
        return jnp.where(from_next, ahead, jnp.where(from_prev, behind, 0.0))

    halo_rows = pl.ds(CX, 8)
    for c in range(3):
        E[c, NZ] = jnp.zeros((EX, CY), F32)
        H[c, 0] = jnp.zeros((EX, CY), F32)

    def take_halo(planes):
        for p in planes:
            for c in range(3):
                E[c, p, halo_rows] = x_halo(c, p)
                H[c, p + 1, halo_rows] = x_halo(3 + c, p)

    take_halo(ORDER[:EARLY])

    pieces = []
    for i, body in enumerate((got[0], own[0], own[1], got[1])):
        rim = jnp.where((narrow8 < 4) & has_next, halo_next[i], jnp.where((narrow8 >= 4) & has_prev, halo_prev[i], 0.0))
        piece = jnp.concatenate([body, rim], axis=0)
        if i == 0:
            piece = jnp.where(has_left, piece, 0.0)
        if i == 3:
            piece = jnp.where(has_right, piece, 0.0)
        pieces.append(piece)

    def strip(kind):
        value = jnp.zeros((EX, 128), F32)
        for i, piece in enumerate(pieces):
            shift = (EDGE * i - EDGE * kind) % 128
            moved = pltpu.roll(piece, shift, 1) if shift else piece
            value = jnp.where((slot_of >= EDGE * i) & (slot_of < EDGE * (i + 1)), moved, value)
        return value

    def design(filtered):
        bend = jnp.tanh(sharpness * (filtered - threshold))
        projected = (math.tanh(sharpness * threshold) + bend) / half_sum_scale
        return bend, eps_low + (eps_high - eps_low) * projected

    dens = jnp.concatenate([den[...], x_halo(7, 0)], axis=0)
    dens_s = strip(7)
    dens = xp(dens) + 2.0 * dens + xn(dens)
    dens_s = xp(dens_s) + 2.0 * dens_s + xn(dens_s)
    bend, eps = design((yp(dens, dens_s, ZLO) + 2.0 * dens + yn(dens, dens_s, ZLO)) / 16.0)
    slope[...] = (sharpness * (1.0 - bend * bend) / half_sum_scale)[:CX]
    design_coef = coef[...] / eps

    def set_coef(planes):
        for p in planes:
            if ZLO <= p < ZLO + PLANES:
                CE[p] = design_coef
            else:
                mats = jnp.concatenate([mat[p].astype(F32), x_halo(6, p)], axis=0)
                part = jnp.broadcast_to(inverse[MATS - 1][:, :1], (EX, CY))
                for k in range(MATS - 1):
                    part = jnp.where(mats == float(k), inverse[k][:, :1], part)
                CE[p] = coef[...] * part

    set_coef(range(ZLO - 1, ZLO + PLANES + 1))
    eps_s = design((pltpu.roll(dens_s, 1, 1) + 2.0 * dens_s + pltpu.roll(dens_s, 127, 1)) / 16.0)[1]
    mats = strip(6)
    part = jnp.broadcast_to(inverse[MATS - 1], (EX, 128))
    for k in range(MATS - 1):
        part = jnp.where(mats == float(k), inverse[k], part)
    layer = (lane >= ZLO * ZL) & (lane < (ZLO + PLANES) * ZL)
    ce_s = ch_s * jnp.where(layer, 1.0 / eps_s, part)

    def yns(f):
        return pltpu.roll(f, 127, 1)

    def yps(f):
        return pltpu.roll(f, 1, 1)

    def zns(f):
        return jnp.where(lane < 128 - ZL, pltpu.roll(f, 128 - ZL, 1), 0.0)

    def zps(f):
        return jnp.where(lane >= ZL, pltpu.roll(f, ZL, 1), 0.0)

    def strip_h(ex, ey, ez, hx, hy, hz):
        cx = (yns(ez) - ez) - (zns(ey) - ey)
        cy = (zns(ex) - ex) - (xn(ez) - ez)
        cz = (xn(ey) - ey) - (yns(ex) - ex)
        return damp_s * hx - ch_s * cx, damp_s * hy - ch_s * cy, damp_s * hz - ch_s * cz

    def strip_e(ex, ey, ez, hx, hy, hz):
        cx = (hz - yps(hz)) - (hy - zps(hy))
        cy = (hx - zps(hx)) - (hz - xp(hz))
        cz = (hy - xp(hy)) - (hx - yps(hx))
        return damp_s * ex + ce_s * cx, damp_s * ey + ce_s * cy, damp_s * ez + ce_s * cz

    es = tuple(strip(c) for c in range(3))
    hs = tuple(strip(c) for c in range(3, 6))
    strips[0], strips[1] = es[0], es[2]
    hs = strip_h(*es, *hs)
    strips[2], strips[3] = hs[0], hs[2]
    es = strip_e(*es, *hs)
    strips[4], strips[5] = es[0], es[2]
    hs = strip_h(*es, *hs)
    strips[6], strips[7] = hs[0], hs[2]

    def half_h(p, n):
        ex, ey, ez = E[0, p], E[1, p], E[2, p]
        d, c = damp[...], coef[...]
        hx = d * H[0, p + 1] - c * ((yn(ez, strips[4 * n + 1], p) - ez) - (E[1, p + 1] - ey))
        hy = d * H[1, p + 1] - c * ((E[0, p + 1] - ex) - (xn(ez) - ez))
        hz = d * H[2, p + 1] - c * ((xn(ey) - ey) - (yn(ex, strips[4 * n], p) - ex))
        for i, value in enumerate((hx, hy, hz)):
            H[i, p + 1] = value
            if n:
                h_out[i, p] = value[:CX]

    def half_e(p, n):
        hx, hy, hz = H[0, p + 1], H[1, p + 1], H[2, p + 1]
        d, c = damp[...], CE[p]
        ex = d * E[0, p] + c * ((hz - yp(hz, strips[4 * n + 3], p)) - (hy - H[1, p]))
        ey = d * E[1, p] + c * ((hx - H[0, p]) - (hz - xp(hz)))
        ez = d * E[2, p] + c * ((hy - xp(hy)) - (hx - yp(hx, strips[4 * n + 2], p)))
        acc = inter[...]
        for i, value in enumerate((ex, ey, ez)):
            if n:
                e_out[i, p] = value[:CX]
            else:
                E[i, p] = value
            if ZLO <= p < ZLO + PLANES:
                acc = acc + gain[PLANES * i + (p - ZLO), n] * value[:CX]
        if ZLO <= p < ZLO + PLANES:
            inter[...] = acc

    before, behind_layer = ZLO - 2, ZLO + PLANES
    for p in range(before, behind_layer + 1):
        half_h(p, 0)
        if p > before:
            half_e(p, 0)
        if p > before + 1:
            half_h(p - 1, 1)
        if p > before + 2:
            half_e(p - 1, 1)
    local[...] = grad_scale * (eps_high - eps_low) * slope[...] * inter[...]

    plan = (
        (local.at[bottom, high], corner.at[0], (1, 1)),
        (local.at[bottom, low], corner.at[1], (1, -1)),
        (local.at[top, high], corner.at[2], (-1, 1)),
        (local.at[top, low], corner.at[3], (-1, -1)),
        (local.at[bottom], rim_prev, (1, 0)),
        (local.at[top], rim_next, (-1, 0)),
        (local.at[:, high], rim_left, (0, 1)),
        (local.at[:, low], rim_right, (0, -1)),
    )
    rims = [remote(src, dst, rim_send.at[i], rim_recv.at[i], near[to]) for i, (src, dst, to) in enumerate(plan)]
    for copy in rims:
        copy.start()

    for copy in halos[10:]:
        copy.wait_recv()
    take_halo(ORDER[EARLY:])
    set_coef([p for p in range(NZ) if not ZLO - 1 <= p <= ZLO + PLANES])
    for p in range(behind_layer + 1, NZ + 1):
        if p < NZ:
            half_h(p, 0)
            half_e(p, 0)
        half_h(p - 1, 1)
        half_e(p - 1, 1)

    hear_word(1)
    pass_word(2)

    def smooth_rows(main, left, right):
        count = main.shape[0]
        lanes = iota((count, 128), 1)

        def along_x(f):
            return pltpu.roll(f, 1, 0) + 2.0 * f + pltpu.roll(f, count - 1, 0)

        a, b = along_x(main[:, :128]), along_x(main[:, 128:])
        left = pltpu.roll(along_x(jnp.where(has_left, left, 0.0)), 1, 1)
        right = pltpu.roll(along_x(jnp.where(has_right, right, 0.0)), 127, 1)
        start, end = lanes == 0, lanes == 127
        ra, rb = pltpu.roll(a, 1, 1), pltpu.roll(b, 1, 1)
        la, lb = pltpu.roll(a, 127, 1), pltpu.roll(b, 127, 1)
        a = (jnp.where(start, left, ra) + 2.0 * a + jnp.where(end, lb, la)) / 16.0
        b = (jnp.where(start, ra, rb) + 2.0 * b + jnp.where(end, right, lb)) / 16.0
        return a, b

    def put(at, h, row):
        slim = iota((8, 128), 1) < TILE
        for j in range(4):
            even = cells[j // 2, pl.ds(at, 8, stride=2), :]
            odd = cells[j // 2, pl.ds(at + 1, 8, stride=2), :]
            if j % 2:
                tile = jnp.where(slim, pltpu.roll(even, TILE, 1), odd)
            else:
                tile = jnp.where(slim, even, pltpu.roll(odd, TILE, 1))
            message[h, pl.ds(4 * row + j, 8, stride=4), :] = tile

    first_stop = []

    def rows_of(turn, h):
        if isinstance(h, int):
            return pl.ds(32 * ((turn + 1 - h) % 2), 32)
        return pl.ds(pl.multiple_of(32 * lax.rem(turn + 1 - h, 2), 32), 32)

    def send_turn(turn):
        for i, (h, slot, to) in enumerate(targets):
            where = rows_of(turn, h if isinstance(h, int) else 1 - core)
            copy = remote(
                message.at[h, where], gathered.at[slot, where], a_send.at[turn, i], a_recv.at[turn, slot], to
            )
            copy.start()
            first_stop.append(copy)

    for copy in rims[6:]:
        copy.wait_recv()
    inner = pl.ds(8, 48)
    a, b = smooth_rows(local[inner], rim_left[inner], rim_right[inner])
    cells[0, inner] = a
    cells[1, inner] = b
    put(16, 0, 8)
    put(32, 1, 0)
    send_turn(0)
    for p in range(before):
        half_h(p, 0)
    for copy in rims[:6]:
        copy.wait_recv()
    tail, head = pl.ds(40, 24), pl.ds(0, 24)
    rows = jnp.where((wide < 4) & has_next, rim_next[...], jnp.where((wide >= 4) & has_prev, rim_prev[...], 0.0))
    side = lambda ahead, back: jnp.where(
        (narrow8 < 4) & has_next, corner[ahead], jnp.where((narrow8 >= 4) & has_prev, corner[back], 0.0)
    )
    a, b = smooth_rows(
        jnp.concatenate([local[tail], rows, local[head]], axis=0),
        jnp.concatenate([rim_left[tail], side(2, 0), rim_left[head]], axis=0),
        jnp.concatenate([rim_right[tail], side(3, 1), rim_right[head]], axis=0),
    )
    for i, value in enumerate((a, b)):
        cells[i, pl.ds(48, 16)] = value[8:24]
        cells[i, pl.ds(0, 16)] = value[32:48]
    put(0, 0, 0)
    put(48, 1, 8)
    send_turn(1)
    gathered[core] = message[core]

    for p in range(before + 1):
        half_e(p, 0)
    for p in range(before + 1):
        half_h(p, 1)
    for p in range(before + 2):
        half_e(p, 1)

    mine = (1 - core) * y + core * x

    def ring(k):
        there = wrapped(mine, k, G)
        return there, dev((1 - core) * x + core * there, (1 - core) * there + core * y, z, core)

    ahead, to_ahead = ring(1)
    behind, to_behind = ring(-1)
    across, _ = ring(2)
    second_stop = {}
    for turn in range(2):
        where = rows_of(turn, core)
        each_slot(
            lambda slot: remote(
                message.at[0, where], gathered.at[slot, where], a_send.at[turn, 0], a_recv.at[turn, slot], other
            ).wait_recv()
        )
        offset = 32 * lax.rem(turn + 1 - core, 2)
        for way in range(2):
            for m in range(2 * way, 2 * way + 2):
                eight = pl.ds(pl.multiple_of(offset + 8 * m, 8), 8)
                data = jnp.concatenate([gathered[slot, eight] for slot in range(slots)], axis=0)
                hi = data.astype(BF16)
                rest = data - hi.astype(F32)
                mid = rest.astype(BF16)
                lo = (rest - mid.astype(F32)).astype(BF16)
                picked = jnp.dot(chosen, jnp.concatenate([hi, mid, lo, hi], axis=0), preferred_element_type=F32)
                for parity in range(2):
                    for place_q in range(G):
                        start = parity * P_rows + place_q * per
                        sums[turn, way, place_q, 2 * (m - 2 * way) + parity] = picked[start : start + per]
            far, near_by = (to_ahead, to_behind) if way == 0 else (to_behind, to_ahead)
            straight = behind if way == 0 else ahead
            for kind, src, dst, to in ((0, across, passing, far), (1, straight, direct, near_by)):
                copy = remote(
                    sums.at[turn, way, src], dst.at[turn, way], b_send.at[turn, way, kind], b_recv.at[turn, way, kind], to
                )
                copy.start()
                second_stop[turn, way, kind] = copy
    for turn in range(2):
        for way in range(2):
            far = to_ahead if way == 0 else to_behind
            onward = ahead if way == 0 else behind
            second_stop[turn, way, 0].wait_recv()
            passing[turn, way] = passing[turn, way] + sums[turn, way, onward]
            copy = remote(
                passing.at[turn, way], combined.at[turn, way], b_send.at[turn, way, 2], b_recv.at[turn, way, 2], far
            )
            copy.start()
            second_stop[turn, way, 2] = copy
    hear_word(2)

    third_stop = []
    order = sorted(range(Zn), key=lambda k: -min(k, Zn - k))
    for turn in range(2):
        for way in range(2):
            second_stop[turn, way, 1].wait_recv()
            second_stop[turn, way, 2].wait_recv()
            for b in range(4):
                value = sums[turn, way, mine, b] + direct[turn, way, b] + combined[turn, way, b]
                ready[pl.ds(8 * turn + 4 * way + b, per, stride=16), :] = value
    for k in order:
        there = wrapped(z, k, Zn)
        for c in range(2):
            if k == 0 and c == 0:
                continue
            target = c if k else 1 - core
            start = pl.multiple_of((there * 2 + target) * 16, 16)
            copy = remote(
                ready.at[pl.ds(start, 16)], landed.at[2 * k + core], c_send.at[2 * k + c], c_recv.at[2 * k + core],
                dev(x, y, there, target),
            )
            copy.start()
            third_stop.append(copy)
    landed[core] = ready[pl.ds(pl.multiple_of((z * 2 + core) * 16, 16), 16)]

    def landing(slot):
        remote(ready.at[pl.ds(0, 16)], landed.at[slot], c_send.at[0], c_recv.at[slot], other).wait_recv()

    landing(1 - core)
    for k in sorted(range(1, Zn), key=lambda k: min(k, Zn - k)):
        for c in range(2):
            landing(2 * k + c)
    for h in range(2):
        value = landed[h]
        for k in range(1, Zn):
            value = value + landed[2 * k + h]
        for turn in range(2):
            out[pl.ds(16 * h + 8 * ((turn + 1 - h) % 2), 8)] = value[8 * turn : 8 * turn + 8]
    for copy in halos + rims + name_copies + first_stop + list(second_stop.values()) + third_stop:
        copy.wait_send()


def solve(G, Zn, e, h, mat, den, fwd, adj, table, tile_map):
    per = Zn * 2
    dma = pltpu.SemaphoreType.DMA
    vmem = lambda *shape: pltpu.VMEM(shape, F32)
    return pl.pallas_call(
        functools.partial(solve_kernel, G, Zn),
        name="solve",
        out_shape=(pltpu.VMEM(e.shape, F32), pltpu.VMEM(h.shape, F32), pltpu.VMEM((32, 128), F32)),
        in_specs=[ANY] * 8,
        out_specs=(VMEM, VMEM, VMEM),
        scratch_shapes=[
            pltpu.SMEM(table.shape, F32),
            pltpu.SMEM(tile_map.shape, jnp.int32),
            vmem(3, NZ + 1, EX, CY),
            vmem(3, NZ + 1, EX, CY),
            vmem(NZ, EX, CY),
            pltpu.VMEM(mat.shape, jnp.int32),
            vmem(CX, CY),
            pltpu.VMEM(fwd.shape, BF16),
            pltpu.VMEM(adj.shape, F32),
            vmem(3 * PLANES, STEPS, CX, CY),
            vmem(CX, CY),
            vmem(CX, CY),
            vmem(EX, CY),
            vmem(EX, CY),
            vmem(2, CX, 128),
            vmem(2, CX, 128),
            vmem(4, 8, 128),
            vmem(4, 8, 128),
            vmem(DOWN_GROUPS, 8, CY),
            vmem(UP_GROUPS, 8, CY),
            vmem(DOWN_GROUPS, 8, CY),
            vmem(UP_GROUPS, 8, CY),
            vmem(8, EX, 128),
            vmem(CX, CY),
            vmem(CX, 128),
            vmem(CX, 128),
            vmem(8, CY),
            vmem(8, CY),
            vmem(4, 8, 128),
            vmem(2, CX, 128),
            vmem(2, CX, 128),
            vmem(8, 128),
            vmem(2 * G, 8, 128),
            vmem(2 * G, CX, 128),
            vmem(2, 2, G, 4, per, 128),
            vmem(2, 2, 4, per, 128),
            vmem(2, 2, 4, per, 128),
            vmem(2, 2, 4, per, 128),
            vmem(per * 16, 128),
            vmem(2 * Zn, 16, 128),
            dma((3 * NZ + 5,)),
            dma((12,)),
            dma((12,)),
            dma((8,)),
            dma((8,)),
            dma((2 * G,)),
            dma((2 * G,)),
            dma((2, 2 * G)),
            dma((2, 2 * G)),
            dma((2, 2, 3)),
            dma((2, 2, 3)),
            dma((2 * Zn,)),
            dma((2 * Zn,)),
            pltpu.SemaphoreType.REGULAR((3,)),
        ],
        compiler_params=pltpu.CompilerParams(collective_id=0, has_side_effects=True),
    )(e, h, mat, den, fwd, adj, table, tile_map)


def write_kernel(e, h, params, e_out, h_out, params_out, sems):
    copies = []
    for src, dst in ((e, e_out), (h, h_out)):
        for c in range(3):
            for half in range(2):
                part = pl.ds(half * (NZ // 2), NZ // 2)
                copies.append(pltpu.make_async_copy(src.at[c, part], dst.at[c, part], sems.at[len(copies)]))
    copies.append(pltpu.make_async_copy(params, params_out, sems.at[len(copies)]))
    for copy in copies:
        copy.start()
    for copy in copies:
        copy.wait()


def write(e, h, params):
    shape = jax.ShapeDtypeStruct
    return pl.pallas_call(
        write_kernel,
        name="write",
        out_shape=tuple(shape(array.shape, F32) for array in (e, h, params)),
        in_specs=[VMEM] * 3,
        out_specs=(ANY,) * 3,
        scratch_shapes=[pltpu.SemaphoreType.DMA((13,))],
    )(*(pltpu.with_memory_space_constraint(array, pltpu.VMEM) for array in (e, h, params)))


def on_device(nx, ny, e_adj, h_adj, density, material, eps_table, dft_adj, dft_fwd, tile_map):
    G = ny // 2
    flat = lambda array: array.reshape(FREQ, 2, 3 * PLANES, CX, CY)
    e_out, h_out, params = solve(
        G, nx // G, e_adj, h_adj, material, density, flat(dft_fwd), flat(dft_adj), eps_table, tile_map
    )
    e_out, h_out, params = write(e_out, h_out, params)
    return e_out, h_out, params.reshape(1, TILE * TILE)


def solution(mesh):
    in_specs = (
        P(None, None, "gx", "gy"),
        P(None, None, "gx", "gy"),
        P("gx", "gy"),
        P(None, "gx", "gy"),
        P(),
        P(None, None, None, None, "gx", "gy"),
        P(None, None, None, None, "gx", "gy"),
        P("gx", "gy"),
    )
    out_specs = (P(None, None, "gx", "gy"), P(None, None, "gx", "gy"), P(("gx", "gy"), None))
    return jax.shard_map(
        functools.partial(on_device, mesh.shape["gx"], mesh.shape["gy"]),
        mesh=mesh,
        in_specs=in_specs,
        out_specs=out_specs,
        check_vma=False,
    )
```

```python
import functools
import math

import jax
import jax.numpy as jnp
from jax import lax
from jax.experimental import pallas as pl
from jax.experimental.pallas import tpu as pltpu
from jax.sharding import PartitionSpec as P

MESH = pl.DeviceIdType.MESH

PLANES = 2
ZLO = 3
STEPS = 2
FREQ = 4
PML = 12
MATS = 4
TILE = 64

courant = 0.5
sigma_peak = 0.8
dft_weight = 0.5
sharpness = 4.0
threshold = 0.5
eps_low = 2.1
eps_high = 12.1
grad_scale = 0.01

F32 = jnp.float32
BF16 = jnp.bfloat16
VMEM = pl.BlockSpec(memory_space=pltpu.VMEM)
ANY = pl.BlockSpec(memory_space=pl.ANY)

CX, CY, NZ = 64, 256, 8
EX = CX + 8
KINDS = 8
EDGE = 2
ZL = KINDS * EDGE


def iota(shape, dim):
    return lax.broadcasted_iota(jnp.int32, shape, dim)


def wrapped(index, shift, count):
    return lax.rem(index + (shift + count), count)


def around(gx, gy, nx, ny):
    places = {}
    for dx in (-1, 0, 1):
        for dy in (-1, 0, 1):
            if dx or dy:
                places[dx, dy] = (wrapped(gx, dx, nx), wrapped(gy, dy, ny))
    return places


def remote(src, dst, send, recv, device):
    return pltpu.make_async_remote_copy(
        src_ref=src, dst_ref=dst, send_sem=send, recv_sem=recv, device_id=device, device_id_type=MESH
    )


def profile(places, total):
    depth = jnp.maximum(jnp.maximum(PML - places, places - (total - 1 - PML)), 0.0) / PML
    return depth * depth * depth


ORDER = (1, 2, 3, 4, 5, 6, 0, 7)
EARLY = 6
DOWN_EARLY, DOWN_GROUPS = 11, 15
UP_EARLY, UP_GROUPS = 9, 12


def row_slot(down, kind, z):
    at = ORDER.index(z)
    early = DOWN_EARLY if down else UP_EARLY
    start, at, count = (0, at, EARLY) if at < EARLY else (early, at - EARLY, NZ - EARLY)
    if kind < 3:
        return start + at, 2 * kind, 2
    if kind == 6:
        return start + at, 6, 1
    each = 2 if down else 1
    row = (3 * at + kind - 3) * each
    return start + count + row // 8, row % 8, each


def solve_kernel(
    G, Zn,
    e_hbm, h_hbm, mat_hbm, den_hbm, fwd_hbm, adj_hbm, table_hbm, map_hbm,
    e_out, h_out, out,
    table_ref, tile_map, E, H, CE, mat, den, fwd, adj, gain, inter, slope, damp, coef, own, got, halo_prev, halo_next, xdown, xup, xprev, xnext, strips,
    local, rim_left, rim_right, rim_prev, rim_next, corner, cells, message, name_out, name_in, gathered, sums, passing, direct,
    combined, ready, landed,
    load_sem, halo_send, halo_recv,
    rim_send, rim_recv, name_send, name_recv, a_send, a_recv, b_send, b_recv, c_send, c_recv, heard,
):
    gx, gy = lax.axis_index("gx"), lax.axis_index("gy")
    nx, ny = Zn * G, 2 * G
    x, core = gy // 2, lax.rem(gy, 2)
    z, y = gx // G, lax.rem(gx, G)
    has_prev, has_next = gx > 0, gx < nx - 1
    has_left, has_right = gy > 0, gy < ny - 1
    total_x, total_y = nx * CX, ny * CY

    def dev(x, y, z, core):
        return (z * G + y, x * 2 + core)

    def signal(semaphore, device):
        pl.semaphore_signal(semaphore, inc=1, device_id=device, device_id_type=MESH)

    near = around(gx, gy, nx, ny)
    partners = list(near.values())
    for k in range(1, G):
        for c in range(2):
            partners.append(dev(wrapped(x, k, G), y, z, c))
            partners.append(dev(x, wrapped(y, k, G), z, c))
    partners.append(dev(x, y, z, 1 - core))
    above, below = wrapped(z, 1, Zn), wrapped(z, -1, Zn)
    for c in range(2):
        partners.append(dev(x, y, above, c))
        partners.append(dev(x, y, below, c))
    block = pl.ds(0, CX)
    loads = []

    def load(src, dst):
        copy = pltpu.make_async_copy(src, dst, load_sem.at[len(loads)])
        copy.start()
        loads.append(copy)
        return copy

    load_den = load(den_hbm, den)
    load_small = [load(map_hbm, tile_map), load(table_hbm, table_ref)]
    load_planes = {
        p: (
            load(e_hbm.at[:, p], E.at[:, p, block]),
            load(h_hbm.at[:, p], H.at[:, p + 1, block]),
            load(mat_hbm.at[p], mat.at[p]),
        )
        for p in ORDER
    }

    barrier = pltpu.get_barrier_semaphore()
    for device in partners:
        signal(barrier, device)

    lane64 = iota((CX, 128), 1)
    lane8 = iota((8, 128), 1)
    low, high, top, bottom = pl.ds(0, 128), pl.ds(128, 128), pl.ds(0, 8), pl.ds(CX - 8, 8)

    def plane(kind, p, rows, columns):
        if kind < 3:
            return E[kind, p, rows, columns]
        if kind < 6:
            return H[kind - 3, p + 1, rows, columns]
        if kind == 6:
            return mat[p, rows, columns].astype(F32)
        return den[rows, columns]

    load_den.wait()
    first = jnp.zeros((CX, 128), F32)
    last = jnp.zeros((CX, 128), F32)
    empty = jnp.zeros((8, CY), F32)
    for g in range(DOWN_GROUPS):
        xdown[g] = empty
    for g in range(UP_GROUPS):
        xup[g] = empty
    for p in ORDER:
        for copy in load_planes[p]:
            copy.wait()
        kinds = list(range(7)) + ([7] if ZLO <= p < ZLO + PLANES else [])
        for kind in kinds:
            at = p * ZL + EDGE * kind
            mine = (lane64 >= at) & (lane64 < at + EDGE)
            a = plane(kind, p, block, low)
            b = plane(kind, p, block, high)
            first = jnp.where(mine, pltpu.roll(a, at, 1) if at else a, first)
            last = jnp.where(mine, pltpu.roll(b, at + EDGE, 1) if at + EDGE < 128 else b, last)
        for kind in range(7):
            g, row, n = row_slot(True, kind, p)
            xdown[g, pl.ds(row, n)] = plane(kind, p, pl.ds(CX - n, n), pl.ds(0, CY))
            g, row, n = row_slot(False, kind, p)
            xup[g, pl.ds(row, n)] = plane(kind, p, pl.ds(0, n), pl.ds(0, CY))
        if p in ORDER[:2]:
            g = ORDER.index(p)
            xdown[g, pl.ds(7, 1)] = den[pl.ds(CX - 2 + g, 1), :]
            xup[g, pl.ds(7, 1)] = den[pl.ds(g, 1), :]
    own[0] = first
    own[1] = last

    for copy in load_small:
        copy.wait()
    names = jnp.zeros((8, 128), F32)
    for j in range(4):
        names = jnp.where(((lane8 == j) | (lane8 == 4 + j)), tile_map[0, j].astype(F32), names)
    name_out[...] = names
    pl.semaphore_wait(barrier, len(partners))

    rounds = Zn // 2 - 1

    def pass_word(i):
        if i < rounds:
            signal(heard.at[i], dev(x, y, above, core))
            signal(heard.at[i], dev(x, y, below, core))

    def hear_word(i):
        if i < rounds:
            pl.semaphore_wait(heard.at[i], 2)

    plan = (
        (own.at[1, bottom], halo_prev.at[0], (1, 1)),
        (own.at[0, bottom], halo_prev.at[3], (1, -1)),
        (own.at[1, top], halo_next.at[0], (-1, 1)),
        (own.at[0, top], halo_next.at[3], (-1, -1)),
        (own.at[:, bottom], halo_prev.at[pl.ds(1, 2)], (1, 0)),
        (own.at[:, top], halo_next.at[pl.ds(1, 2)], (-1, 0)),
        (xdown.at[pl.ds(0, DOWN_EARLY)], xprev.at[pl.ds(0, DOWN_EARLY)], (1, 0)),
        (xup.at[pl.ds(0, UP_EARLY)], xnext.at[pl.ds(0, UP_EARLY)], (-1, 0)),
        (own.at[1], got.at[0], (0, 1)),
        (own.at[0], got.at[1], (0, -1)),
        (xdown.at[pl.ds(DOWN_EARLY, DOWN_GROUPS - DOWN_EARLY)], xprev.at[pl.ds(DOWN_EARLY, DOWN_GROUPS - DOWN_EARLY)], (1, 0)),
        (xup.at[pl.ds(UP_EARLY, UP_GROUPS - UP_EARLY)], xnext.at[pl.ds(UP_EARLY, UP_GROUPS - UP_EARLY)], (-1, 0)),
    )
    halos = [remote(src, dst, halo_send.at[i], halo_recv.at[i], near[to]) for i, (src, dst, to) in enumerate(plan)]
    for copy in halos:
        copy.start()
    pass_word(0)

    targets = []
    for k in (2, 1, 3) if G == 4 else range(1, G):
        targets.append((0, 2 * k + core, dev(wrapped(x, k, G), y, z, 0)))
        targets.append((1, 2 * k + core, dev(x, wrapped(y, k, G), z, 1)))
    targets.append((1 - core, core, dev(x, y, z, 1 - core)))
    other = dev(x, y, z, 1 - core)
    slots = 2 * G
    name_copies = [
        remote(name_out, name_in.at[slot], name_send.at[i], name_recv.at[slot], to)
        for i, (_, slot, to) in enumerate(targets)
    ]
    for copy in name_copies:
        copy.start()
    name_in[core] = name_out[...]

    def each_slot(wait):
        wait(1 - core)
        for k in range(1, G):
            for c in range(2):
                wait(2 * k + c)

    load_dft = [load(fwd_hbm, fwd), load(adj_hbm, adj)]

    for copy in load_dft:
        copy.wait()
    cosines = [[dft_weight * math.cos((0.21 + 0.06 * f) * (n + 1)) for f in range(FREQ)] for n in range(STEPS)]
    sines = [[dft_weight * math.sin((0.21 + 0.06 * f) * (n + 1)) for f in range(FREQ)] for n in range(STEPS)]

    def chunk(r, _):
        rows = pl.ds(pl.multiple_of(r * 16, 16), 16)

        def entry(k, acc):
            one = jnp.zeros((16, CY), F32)
            two = jnp.zeros((16, CY), F32)
            for f in range(FREQ):
                re = fwd[f, 0, k, rows].astype(F32)
                im = fwd[f, 1, k, rows].astype(F32)
                acc = acc + (re * adj[f, 0, k, rows] - im * adj[f, 1, k, rows])
                one = one + (cosines[0][f] * re + sines[0][f] * im)
                two = two + (cosines[1][f] * re + sines[1][f] * im)
            gain[k, 0, rows] = one
            gain[k, 1, rows] = two
            return acc

        inter[rows] = lax.fori_loop(0, 3 * PLANES, entry, jnp.zeros((16, CY), F32))
        return 0

    lax.fori_loop(0, CX // 16, chunk, 0)

    lane = iota((EX, 128), 1)
    slot_of = lax.rem(lane, ZL)
    half_sum_scale = math.tanh(sharpness * threshold) + math.tanh(sharpness * (1.0 - threshold))

    def places(columns, width):
        rows = iota((EX, width), 0)
        rows = gx * CX + jnp.where(rows < CX + 4, rows, rows - EX)
        inside = (rows >= 0) & (rows < total_x) & (columns >= 0) & (columns < total_y)
        sigma = sigma_peak * (profile(rows.astype(F32), total_x) + profile(columns.astype(F32), total_y))
        part = jnp.where(inside, 1.0 / (1.0 + 0.5 * sigma), 0.0)
        return (1.0 - 0.5 * sigma) * part, courant * part

    damping, coef_h = places(gy * CY + iota((EX, CY), 1), CY)
    damp[...] = damping
    coef[...] = coef_h
    columns = gy * CY + jnp.where(slot_of < 4, slot_of - EDGE, slot_of + (CY - EDGE - 4))
    damp_s, ch_s = places(columns, 128)
    damp_s = jnp.where(slot_of < 8, damp_s, 0.0)
    ch_s = jnp.where(slot_of < 8, ch_s, 0.0)
    inverse = [1.0 / jnp.full((1, 128), table_ref[k], F32) for k in range(MATS)]

    each_slot(lambda slot: remote(name_out, name_in.at[slot], name_send.at[0], name_recv.at[slot], other).wait_recv())
    K = slots * 8
    P_rows = G * Zn * 2
    per = Zn * 2
    found = jnp.zeros((8, 128), F32)
    for slot in range(slots):
        part = name_in[slot]
        part = pltpu.roll(part, 8 * slot, 1) if slot else part
        found = jnp.where((lane8 >= 8 * slot) & (lane8 < 8 * slot + 8), part, found)
    shift = K
    while shift < 128:
        found = jnp.where(lane8 < shift, found, pltpu.roll(found, shift, 1))
        shift *= 2
    found = jnp.broadcast_to(found[0:1], (P_rows, 128))
    row = iota((P_rows, 128), 0)
    column = iota((P_rows, 128), 1)
    q = row // per
    place = lax.rem(row, per)
    fixed = (1 - core) * (x * 2) + core * (y * (2 * G))
    param = (place // 2) * (2 * G * G) + lax.rem(place, 2) + q * ((1 - core) * (2 * G) + core * 2) + fixed
    match = found == param.astype(F32)
    even_cells = lax.rem(column, 8) < 4
    both = jnp.concatenate(
        [jnp.where(match & even_cells, 1.0, 0.0), jnp.where(match & (~even_cells), 1.0, 0.0)], axis=0
    )
    if K == 64:
        third = jnp.where(iota((2 * P_rows, 128), 1) < 3 * K - 128, both, 0.0)
        chosen = jnp.concatenate([both, third], axis=1).astype(BF16)
    else:
        chosen = jnp.where(iota((2 * P_rows, 128), 1) < 3 * K, both, 0.0).astype(BF16)
    hear_word(0)
    pass_word(1)

    for copy in halos[:10]:
        copy.wait_recv()

    def xn(f):
        return pltpu.roll(f, EX - 1, 0)

    def xp(f):
        return pltpu.roll(f, 1, 0)

    def yn(f, strip, p):
        a, b = pltpu.roll(f[:, :128], 127, 1), pltpu.roll(f[:, 128:], 127, 1)
        edge = pltpu.roll(strip, (127 - 6 - p * ZL) % 128, 1)
        end = lane == 127
        return jnp.concatenate([jnp.where(end, b, a), jnp.where(end, edge, b)], axis=1)

    def yp(f, strip, p):
        a, b = pltpu.roll(f[:, :128], 1, 1), pltpu.roll(f[:, 128:], 1, 1)
        edge = pltpu.roll(strip, (127 - p * ZL) % 128, 1)
        start = lane == 0
        return jnp.concatenate([jnp.where(start, edge, a), jnp.where(start, a, b)], axis=1)

    wide = iota((8, CY), 0)
    narrow8 = iota((8, 128), 0)
    from_next, from_prev = (wide < 2) & has_next, (wide >= 6) & has_prev

    def x_halo(kind, p):
        if kind == 7:
            ahead = jnp.where(wide == 0, pltpu.roll(xnext[0], 1, 0), pltpu.roll(xnext[1], 2, 0))
            behind = jnp.where(wide == 6, pltpu.roll(xprev[0], 7, 0), xprev[1])
        else:
            g, at, _ = row_slot(False, kind, p)
            ahead = pltpu.roll(xnext[g], (8 - at) % 8, 0) if at else xnext[g]
            g, at, n = row_slot(True, kind, p)
            shift = (8 - n - at) % 8
            behind = pltpu.roll(xprev[g], shift, 0) if shift else xprev[g]
        return jnp.where(from_next, ahead, jnp.where(from_prev, behind, 0.0))

    halo_rows = pl.ds(CX, 8)
    for c in range(3):
        E[c, NZ] = jnp.zeros((EX, CY), F32)
        H[c, 0] = jnp.zeros((EX, CY), F32)

    def take_halo(planes):
        for p in planes:
            for c in range(3):
                E[c, p, halo_rows] = x_halo(c, p)
                H[c, p + 1, halo_rows] = x_halo(3 + c, p)

    take_halo(ORDER[:EARLY])

    pieces = []
    for i, body in enumerate((got[0], own[0], own[1], got[1])):
        rim = jnp.where((narrow8 < 4) & has_next, halo_next[i], jnp.where((narrow8 >= 4) & has_prev, halo_prev[i], 0.0))
        piece = jnp.concatenate([body, rim], axis=0)
        if i == 0:
            piece = jnp.where(has_left, piece, 0.0)
        if i == 3:
            piece = jnp.where(has_right, piece, 0.0)
        pieces.append(piece)

    def strip(kind):
        value = jnp.zeros((EX, 128), F32)
        for i, piece in enumerate(pieces):
            shift = (EDGE * i - EDGE * kind) % 128
            moved = pltpu.roll(piece, shift, 1) if shift else piece
            value = jnp.where((slot_of >= EDGE * i) & (slot_of < EDGE * (i + 1)), moved, value)
        return value

    def design(filtered):
        bend = jnp.tanh(sharpness * (filtered - threshold))
        projected = (math.tanh(sharpness * threshold) + bend) / half_sum_scale
        return bend, eps_low + (eps_high - eps_low) * projected

    dens = jnp.concatenate([den[...], x_halo(7, 0)], axis=0)
    dens_s = strip(7)
    dens = xp(dens) + 2.0 * dens + xn(dens)
    dens_s = xp(dens_s) + 2.0 * dens_s + xn(dens_s)
    bend, eps = design((yp(dens, dens_s, ZLO) + 2.0 * dens + yn(dens, dens_s, ZLO)) / 16.0)
    slope[...] = (sharpness * (1.0 - bend * bend) / half_sum_scale)[:CX]
    design_coef = coef[...] / eps

    def set_coef(planes):
        for p in planes:
            if ZLO <= p < ZLO + PLANES:
                CE[p] = design_coef
            else:
                mats = jnp.concatenate([mat[p].astype(F32), x_halo(6, p)], axis=0)
                part = jnp.broadcast_to(inverse[MATS - 1][:, :1], (EX, CY))
                for k in range(MATS - 1):
                    part = jnp.where(mats == float(k), inverse[k][:, :1], part)
                CE[p] = coef[...] * part

    set_coef(range(ZLO - 1, ZLO + PLANES + 1))
    eps_s = design((pltpu.roll(dens_s, 1, 1) + 2.0 * dens_s + pltpu.roll(dens_s, 127, 1)) / 16.0)[1]
    mats = strip(6)
    part = jnp.broadcast_to(inverse[MATS - 1], (EX, 128))
    for k in range(MATS - 1):
        part = jnp.where(mats == float(k), inverse[k], part)
    layer = (lane >= ZLO * ZL) & (lane < (ZLO + PLANES) * ZL)
    ce_s = ch_s * jnp.where(layer, 1.0 / eps_s, part)

    def yns(f):
        return pltpu.roll(f, 127, 1)

    def yps(f):
        return pltpu.roll(f, 1, 1)

    def zns(f):
        return jnp.where(lane < 128 - ZL, pltpu.roll(f, 128 - ZL, 1), 0.0)

    def zps(f):
        return jnp.where(lane >= ZL, pltpu.roll(f, ZL, 1), 0.0)

    def strip_h(ex, ey, ez, hx, hy, hz):
        cx = (yns(ez) - ez) - (zns(ey) - ey)
        cy = (zns(ex) - ex) - (xn(ez) - ez)
        cz = (xn(ey) - ey) - (yns(ex) - ex)
        return damp_s * hx - ch_s * cx, damp_s * hy - ch_s * cy, damp_s * hz - ch_s * cz

    def strip_e(ex, ey, ez, hx, hy, hz):
        cx = (hz - yps(hz)) - (hy - zps(hy))
        cy = (hx - zps(hx)) - (hz - xp(hz))
        cz = (hy - xp(hy)) - (hx - yps(hx))
        return damp_s * ex + ce_s * cx, damp_s * ey + ce_s * cy, damp_s * ez + ce_s * cz

    es = tuple(strip(c) for c in range(3))
    hs = tuple(strip(c) for c in range(3, 6))
    strips[0], strips[1] = es[0], es[2]
    hs = strip_h(*es, *hs)
    strips[2], strips[3] = hs[0], hs[2]
    es = strip_e(*es, *hs)
    strips[4], strips[5] = es[0], es[2]
    hs = strip_h(*es, *hs)
    strips[6], strips[7] = hs[0], hs[2]

    def half_h(p, n):
        ex, ey, ez = E[0, p], E[1, p], E[2, p]
        d, c = damp[...], coef[...]
        hx = d * H[0, p + 1] - c * ((yn(ez, strips[4 * n + 1], p) - ez) - (E[1, p + 1] - ey))
        hy = d * H[1, p + 1] - c * ((E[0, p + 1] - ex) - (xn(ez) - ez))
        hz = d * H[2, p + 1] - c * ((xn(ey) - ey) - (yn(ex, strips[4 * n], p) - ex))
        for i, value in enumerate((hx, hy, hz)):
            H[i, p + 1] = value
            if n:
                h_out[i, p] = value[:CX]

    def half_e(p, n):
        hx, hy, hz = H[0, p + 1], H[1, p + 1], H[2, p + 1]
        d, c = damp[...], CE[p]
        ex = d * E[0, p] + c * ((hz - yp(hz, strips[4 * n + 3], p)) - (hy - H[1, p]))
        ey = d * E[1, p] + c * ((hx - H[0, p]) - (hz - xp(hz)))
        ez = d * E[2, p] + c * ((hy - xp(hy)) - (hx - yp(hx, strips[4 * n + 2], p)))
        acc = inter[...]
        for i, value in enumerate((ex, ey, ez)):
            if n:
                e_out[i, p] = value[:CX]
            else:
                E[i, p] = value
            if ZLO <= p < ZLO + PLANES:
                acc = acc + gain[PLANES * i + (p - ZLO), n] * value[:CX]
        if ZLO <= p < ZLO + PLANES:
            inter[...] = acc

    before, behind_layer = ZLO - 2, ZLO + PLANES
    for p in range(before, behind_layer + 1):
        half_h(p, 0)
        if p > before:
            half_e(p, 0)
        if p > before + 1:
            half_h(p - 1, 1)
        if p > before + 2:
            half_e(p - 1, 1)
    local[...] = grad_scale * (eps_high - eps_low) * slope[...] * inter[...]

    plan = (
        (local.at[bottom, high], corner.at[0], (1, 1)),
        (local.at[bottom, low], corner.at[1], (1, -1)),
        (local.at[top, high], corner.at[2], (-1, 1)),
        (local.at[top, low], corner.at[3], (-1, -1)),
        (local.at[bottom], rim_prev, (1, 0)),
        (local.at[top], rim_next, (-1, 0)),
        (local.at[:, high], rim_left, (0, 1)),
        (local.at[:, low], rim_right, (0, -1)),
    )
    rims = [remote(src, dst, rim_send.at[i], rim_recv.at[i], near[to]) for i, (src, dst, to) in enumerate(plan)]
    for copy in rims:
        copy.start()

    for copy in halos[10:]:
        copy.wait_recv()
    take_halo(ORDER[EARLY:])
    set_coef([p for p in range(NZ) if not ZLO - 1 <= p <= ZLO + PLANES])
    for p in range(behind_layer + 1, NZ + 1):
        if p < NZ:
            half_h(p, 0)
            half_e(p, 0)
        half_h(p - 1, 1)
        half_e(p - 1, 1)

    hear_word(1)
    pass_word(2)

    def smooth_rows(main, left, right):
        count = main.shape[0]
        lanes = iota((count, 128), 1)

        def along_x(f):
            return pltpu.roll(f, 1, 0) + 2.0 * f + pltpu.roll(f, count - 1, 0)

        a, b = along_x(main[:, :128]), along_x(main[:, 128:])
        left = pltpu.roll(along_x(jnp.where(has_left, left, 0.0)), 1, 1)
        right = pltpu.roll(along_x(jnp.where(has_right, right, 0.0)), 127, 1)
        start, end = lanes == 0, lanes == 127
        ra, rb = pltpu.roll(a, 1, 1), pltpu.roll(b, 1, 1)
        la, lb = pltpu.roll(a, 127, 1), pltpu.roll(b, 127, 1)
        a = (jnp.where(start, left, ra) + 2.0 * a + jnp.where(end, lb, la)) / 16.0
        b = (jnp.where(start, ra, rb) + 2.0 * b + jnp.where(end, right, lb)) / 16.0
        return a, b

    def put(at, h, row):
        slim = iota((8, 128), 1) < TILE
        for j in range(4):
            even = cells[j // 2, pl.ds(at, 8, stride=2), :]
            odd = cells[j // 2, pl.ds(at + 1, 8, stride=2), :]
            if j % 2:
                tile = jnp.where(slim, pltpu.roll(even, TILE, 1), odd)
            else:
                tile = jnp.where(slim, even, pltpu.roll(odd, TILE, 1))
            message[h, pl.ds(4 * row + j, 8, stride=4), :] = tile

    first_stop = []

    def rows_of(turn, h):
        if isinstance(h, int):
            return pl.ds(32 * ((turn + 1 - h) % 2), 32)
        return pl.ds(pl.multiple_of(32 * lax.rem(turn + 1 - h, 2), 32), 32)

    def send_turn(turn):
        for i, (h, slot, to) in enumerate(targets):
            where = rows_of(turn, h if isinstance(h, int) else 1 - core)
            copy = remote(
                message.at[h, where], gathered.at[slot, where], a_send.at[turn, i], a_recv.at[turn, slot], to
            )
            copy.start()
            first_stop.append(copy)

    for copy in rims[6:]:
        copy.wait_recv()
    inner = pl.ds(8, 48)
    a, b = smooth_rows(local[inner], rim_left[inner], rim_right[inner])
    cells[0, inner] = a
    cells[1, inner] = b
    put(16, 0, 8)
    put(32, 1, 0)
    send_turn(0)
    for p in range(before):
        half_h(p, 0)
    for copy in rims[:6]:
        copy.wait_recv()
    tail, head = pl.ds(40, 24), pl.ds(0, 24)
    rows = jnp.where((wide < 4) & has_next, rim_next[...], jnp.where((wide >= 4) & has_prev, rim_prev[...], 0.0))
    side = lambda ahead, back: jnp.where(
        (narrow8 < 4) & has_next, corner[ahead], jnp.where((narrow8 >= 4) & has_prev, corner[back], 0.0)
    )
    a, b = smooth_rows(
        jnp.concatenate([local[tail], rows, local[head]], axis=0),
        jnp.concatenate([rim_left[tail], side(2, 0), rim_left[head]], axis=0),
        jnp.concatenate([rim_right[tail], side(3, 1), rim_right[head]], axis=0),
    )
    for i, value in enumerate((a, b)):
        cells[i, pl.ds(48, 16)] = value[8:24]
        cells[i, pl.ds(0, 16)] = value[32:48]
    put(0, 0, 0)
    put(48, 1, 8)
    send_turn(1)
    gathered[core] = message[core]

    for p in range(before + 1):
        half_e(p, 0)
    for p in range(before + 1):
        half_h(p, 1)
    for p in range(before + 2):
        half_e(p, 1)

    mine = (1 - core) * y + core * x

    def ring(k):
        there = wrapped(mine, k, G)
        return there, dev((1 - core) * x + core * there, (1 - core) * there + core * y, z, core)

    ahead, to_ahead = ring(1)
    behind, to_behind = ring(-1)
    across, _ = ring(2)
    second_stop = {}
    for turn in range(2):
        where = rows_of(turn, core)
        each_slot(
            lambda slot: remote(
                message.at[0, where], gathered.at[slot, where], a_send.at[turn, 0], a_recv.at[turn, slot], other
            ).wait_recv()
        )
        offset = 32 * lax.rem(turn + 1 - core, 2)
        for way in range(2):
            for m in range(2 * way, 2 * way + 2):
                eight = pl.ds(pl.multiple_of(offset + 8 * m, 8), 8)
                data = jnp.concatenate([gathered[slot, eight] for slot in range(slots)], axis=0)
                hi = data.astype(BF16)
                rest = data - hi.astype(F32)
                mid = rest.astype(BF16)
                lo = (rest - mid.astype(F32)).astype(BF16)
                picked = jnp.dot(chosen, jnp.concatenate([hi, mid, lo, hi], axis=0), preferred_element_type=F32)
                for parity in range(2):
                    for place_q in range(G):
                        start = parity * P_rows + place_q * per
                        sums[turn, way, place_q, 2 * (m - 2 * way) + parity] = picked[start : start + per]
            far, near_by = (to_ahead, to_behind) if way == 0 else (to_behind, to_ahead)
            straight = behind if way == 0 else ahead
            for kind, src, dst, to in ((0, across, passing, far), (1, straight, direct, near_by)):
                copy = remote(
                    sums.at[turn, way, src], dst.at[turn, way], b_send.at[turn, way, kind], b_recv.at[turn, way, kind], to
                )
                copy.start()
                second_stop[turn, way, kind] = copy
    for turn in range(2):
        for way in range(2):
            far = to_ahead if way == 0 else to_behind
            onward = ahead if way == 0 else behind
            second_stop[turn, way, 0].wait_recv()
            passing[turn, way] = passing[turn, way] + sums[turn, way, onward]
            copy = remote(
                passing.at[turn, way], combined.at[turn, way], b_send.at[turn, way, 2], b_recv.at[turn, way, 2], far
            )
            copy.start()
            second_stop[turn, way, 2] = copy
    hear_word(2)

    third_stop = []
    order = sorted(range(Zn), key=lambda k: -min(k, Zn - k))
    for turn in range(2):
        for way in range(2):
            second_stop[turn, way, 1].wait_recv()
            second_stop[turn, way, 2].wait_recv()
            for b in range(4):
                value = sums[turn, way, mine, b] + direct[turn, way, b] + combined[turn, way, b]
                ready[pl.ds(8 * turn + 4 * way + b, per, stride=16), :] = value
    for k in order:
        there = wrapped(z, k, Zn)
        for c in range(2):
            if k == 0 and c == 0:
                continue
            target = c if k else 1 - core
            start = pl.multiple_of((there * 2 + target) * 16, 16)
            copy = remote(
                ready.at[pl.ds(start, 16)], landed.at[2 * k + core], c_send.at[2 * k + c], c_recv.at[2 * k + core],
                dev(x, y, there, target),
            )
            copy.start()
            third_stop.append(copy)
    landed[core] = ready[pl.ds(pl.multiple_of((z * 2 + core) * 16, 16), 16)]

    def landing(slot):
        remote(ready.at[pl.ds(0, 16)], landed.at[slot], c_send.at[0], c_recv.at[slot], other).wait_recv()

    for copy in halos + rims + name_copies + first_stop + list(second_stop.values()):
        copy.wait_send()
    landing(1 - core)
    for k in sorted(range(1, Zn), key=lambda k: min(k, Zn - k)):
        for c in range(2):
            landing(2 * k + c)
    for h in range(2):
        value = landed[h]
        for k in range(1, Zn):
            value = value + landed[2 * k + h]
        for turn in range(2):
            out[pl.ds(16 * h + 8 * ((turn + 1 - h) % 2), 8)] = value[8 * turn : 8 * turn + 8]
    for copy in third_stop:
        copy.wait_send()


def solve(G, Zn, e, h, mat, den, fwd, adj, table, tile_map):
    per = Zn * 2
    dma = pltpu.SemaphoreType.DMA
    vmem = lambda *shape: pltpu.VMEM(shape, F32)
    return pl.pallas_call(
        functools.partial(solve_kernel, G, Zn),
        name="solve",
        out_shape=(pltpu.VMEM(e.shape, F32), pltpu.VMEM(h.shape, F32), pltpu.VMEM((32, 128), F32)),
        in_specs=[ANY] * 8,
        out_specs=(VMEM, VMEM, VMEM),
        scratch_shapes=[
            pltpu.SMEM(table.shape, F32),
            pltpu.SMEM(tile_map.shape, jnp.int32),
            vmem(3, NZ + 1, EX, CY),
            vmem(3, NZ + 1, EX, CY),
            vmem(NZ, EX, CY),
            pltpu.VMEM(mat.shape, jnp.int32),
            vmem(CX, CY),
            pltpu.VMEM(fwd.shape, BF16),
            pltpu.VMEM(adj.shape, F32),
            vmem(3 * PLANES, STEPS, CX, CY),
            vmem(CX, CY),
            vmem(CX, CY),
            vmem(EX, CY),
            vmem(EX, CY),
            vmem(2, CX, 128),
            vmem(2, CX, 128),
            vmem(4, 8, 128),
            vmem(4, 8, 128),
            vmem(DOWN_GROUPS, 8, CY),
            vmem(UP_GROUPS, 8, CY),
            vmem(DOWN_GROUPS, 8, CY),
            vmem(UP_GROUPS, 8, CY),
            vmem(8, EX, 128),
            vmem(CX, CY),
            vmem(CX, 128),
            vmem(CX, 128),
            vmem(8, CY),
            vmem(8, CY),
            vmem(4, 8, 128),
            vmem(2, CX, 128),
            vmem(2, CX, 128),
            vmem(8, 128),
            vmem(2 * G, 8, 128),
            vmem(2 * G, CX, 128),
            vmem(2, 2, G, 4, per, 128),
            vmem(2, 2, 4, per, 128),
            vmem(2, 2, 4, per, 128),
            vmem(2, 2, 4, per, 128),
            vmem(per * 16, 128),
            vmem(2 * Zn, 16, 128),
            dma((3 * NZ + 5,)),
            dma((12,)),
            dma((12,)),
            dma((8,)),
            dma((8,)),
            dma((2 * G,)),
            dma((2 * G,)),
            dma((2, 2 * G)),
            dma((2, 2 * G)),
            dma((2, 2, 3)),
            dma((2, 2, 3)),
            dma((2 * Zn,)),
            dma((2 * Zn,)),
            pltpu.SemaphoreType.REGULAR((3,)),
        ],
        compiler_params=pltpu.CompilerParams(collective_id=0, has_side_effects=True),
    )(e, h, mat, den, fwd, adj, table, tile_map)


def write_kernel(e, h, params, e_out, h_out, params_out, sems):
    copies = []
    for src, dst in ((e, e_out), (h, h_out)):
        for c in range(3):
            for half in range(2):
                part = pl.ds(half * (NZ // 2), NZ // 2)
                copies.append(pltpu.make_async_copy(src.at[c, part], dst.at[c, part], sems.at[len(copies)]))
    copies.append(pltpu.make_async_copy(params, params_out, sems.at[len(copies)]))
    for copy in copies:
        copy.start()
    for copy in copies:
        copy.wait()


def write(e, h, params):
    shape = jax.ShapeDtypeStruct
    return pl.pallas_call(
        write_kernel,
        name="write",
        out_shape=tuple(shape(array.shape, F32) for array in (e, h, params)),
        in_specs=[VMEM] * 3,
        out_specs=(ANY,) * 3,
        scratch_shapes=[pltpu.SemaphoreType.DMA((13,))],
    )(*(pltpu.with_memory_space_constraint(array, pltpu.VMEM) for array in (e, h, params)))


def on_device(nx, ny, e_adj, h_adj, density, material, eps_table, dft_adj, dft_fwd, tile_map):
    G = ny // 2
    flat = lambda array: array.reshape(FREQ, 2, 3 * PLANES, CX, CY)
    e_out, h_out, params = solve(
        G, nx // G, e_adj, h_adj, material, density, flat(dft_fwd), flat(dft_adj), eps_table, tile_map
    )
    e_out, h_out, params = write(e_out, h_out, params)
    return e_out, h_out, params.reshape(1, TILE * TILE)


def solution(mesh):
    in_specs = (
        P(None, None, "gx", "gy"),
        P(None, None, "gx", "gy"),
        P("gx", "gy"),
        P(None, "gx", "gy"),
        P(),
        P(None, None, None, None, "gx", "gy"),
        P(None, None, None, None, "gx", "gy"),
        P("gx", "gy"),
    )
    out_specs = (P(None, None, "gx", "gy"), P(None, None, "gx", "gy"), P(("gx", "gy"), None))
    return jax.shard_map(
        functools.partial(on_device, mesh.shape["gx"], mesh.shape["gy"]),
        mesh=mesh,
        in_specs=in_specs,
        out_specs=out_specs,
        check_vma=False,
    )
```
